32 devices in a mesh: group: 2 (over y), ctx: 4 (over x, core), tp: 4 (over z).
Axes of the slice: x: 2, y: 2, z: 4, core: 2. Of those that a mesh axis runs over, the one named last changes fastest.
Arguments:
- x_in: bfloat16 [4096, 16384], P(('group', 'ctx'), 'tp'), parts along dimension 0, may hold values from -6 to 6
- bc_in: bfloat16 [4096, 2, 2048], P(('group', 'ctx'), None, 'tp'), parts along dimension 0, may hold values from -6 to 6
- z_in: bfloat16 [4096, 16384], P(('group', 'ctx'), 'tp'), parts along dimension 0, may hold values from -6 to 6
- dt_raw: float32 [4096, 256], P(('group', 'ctx'), 'tp'), parts along dimension 0, may hold values from -3 to 3
- conv_x: bfloat16 [4, 16384], P(None, 'tp'), may hold values from -3 to 3
- conv_bc: bfloat16 [4, 2, 2048], P(None, None, 'tp'), may hold values from -3 to 3
- conv_bias_x: float32 [16384], P('tp'), may hold values from -0.9 to -0.1
- conv_bias_bc: float32 [2, 2048], P(None, 'tp'), may hold values from -0.9 to -0.1
- dt_bias: float32 [256], P('tp'), may hold values from -12 to 2
- a_log: float32 [256], P('tp'), may hold values from -12 to 4
- d_skip: float32 [256], P('tp'), may hold values from 0.5 to 2
- norm_gain: float32 [16384], P('tp'), may hold values from 0.5 to 1.5
Outputs:
- mixed: bfloat16 [4096, 16384], P(('group', 'ctx'), 'tp'), parts along dimension 0
- final_state: float32 [512, 64, 256], P(('group', 'tp'), None, 'ctx'), parts along dimension 0
The draws below stay inside these ranges and needn't reach their ends.
There are 2 independent parts, one for each index of `group`. The reference program is written for one: setup_inputs(seed, part) draws one part's arguments, and reference() takes and returns one part's arrays. A program takes and returns all parts, laid end to end along the dimension named above; an argument that names none is the same for every part. Nothing has to cross between parts.
All inputs are finite; a program needn't handle non-finite values.
Results may differ from the reference program's by a relative error of at most 0.0059.
Values may be sent and summed in bfloat16 or wider, within the bound.
A program may use at most 192 MiB of HBM per device.

```python
import jax
import jax.numpy as jnp
from jax import lax

HEADS = 256
HEAD_DIM = 64
STATE = 256
GROUPS = 8
KERNEL = 4
SPAN = 128
TOK_DEV = 512
TOKENS = 2048


def head_law(key):
    stream = jax.random.fold_in(key, 7)
    pick_key, slow_key, middle_key, fast_key = jax.random.split(stream, 4)
    slow_share = 0.5
    middle_share = 0.35
    picker = jax.random.uniform(pick_key, (HEADS,), jnp.float32)
    slow_mask = picker < slow_share
    middle_mask = picker < slow_share + middle_share
    slow_rate = jnp.exp(jax.random.uniform(slow_key, (HEADS,), jnp.float32, jnp.log(0.15), jnp.log(0.8))) / TOKENS
    middle_rate = jax.random.uniform(middle_key, (HEADS,), jnp.float32, 0.8, 1.5) / SPAN
    fast_rate = jax.random.uniform(fast_key, (HEADS,), jnp.float32, 8.0, 12.0) / SPAN
    fade_rate = jnp.where(slow_mask, slow_rate, jnp.where(middle_mask, middle_rate, fast_rate))
    window = 0.5 / fade_rate
    mean_step = 0.25 / (0.006 * window + 0.16 * jnp.sqrt(window) + 1.0)
    return (fade_rate, mean_step)


def draw_a_log(key, part):
    fade_rate, mean_step = head_law(key)
    return jnp.log(fade_rate / mean_step)


def draw_dt_bias(key, part):
    fade_rate, mean_step = head_law(key)
    return jnp.log(jnp.expm1(mean_step))


def draw_dt_raw(key, part):
    noise_key, offset_key = jax.random.split(jax.random.fold_in(key, 3))
    jitter = jnp.clip(0.7 * jax.random.normal(noise_key, (TOKENS, HEADS), jnp.float32), -2.1, 2.1)
    offsets = jax.random.uniform(offset_key, (TOKENS // TOK_DEV, HEADS), jnp.float32, -0.7, 0.7)
    return jnp.repeat(offsets, TOK_DEV, axis=0) + jitter


def block_scale(own_key, extent, cuts, low, top_value):
    def one(dim, parts):
        draws = jax.random.uniform(jax.random.fold_in(jax.random.fold_in(own_key, 6), dim), (parts,), jnp.float32, low / len(cuts), top_value / len(cuts))
        return jnp.repeat(jnp.exp(draws), extent[dim] // parts).reshape((-1,) + (1,) * (len(extent) - dim - 1))

    factor_of = one(*cuts[0])
    for cut in cuts[1:]:
        factor_of = factor_of * one(*cut)
    return factor_of


def bell_draw(key, extent, width, reach, cuts=(), kind=jnp.bfloat16):
    drawn = width * jax.random.normal(key, extent, jnp.float32)
    if cuts:
        drawn = drawn * block_scale(key, extent, cuts, -0.22, 0.18)
    return jnp.clip(drawn, -reach, reach).astype(kind)


def setup_inputs(seed: int = 0, part: int = 0) -> dict:
    key_list = jax.random.split(jax.random.key(seed), 13)
    part_keys = jax.random.split(jax.random.fold_in(key_list[12], part), 13)
    x_in = bell_draw(part_keys[0], (TOKENS, HEADS * HEAD_DIM), 1.0, 6.0, ((0, 4), (1, 4)))
    bc_in = bell_draw(part_keys[1], (TOKENS, 2, GROUPS * STATE), 1.0, 6.0, ((0, 4), (2, 4)))
    z_in = bell_draw(part_keys[2], (TOKENS, HEADS * HEAD_DIM), 1.0, 6.0, ((0, 4), (1, 4)))
    dt_raw = draw_dt_raw(jax.random.fold_in(jax.random.fold_in(key_list[12], part), 71), part)
    conv_x = bell_draw(key_list[4], (KERNEL, HEADS * HEAD_DIM), KERNEL ** -0.5, 3.0, ((1, 4),))
    conv_bc = bell_draw(key_list[5], (KERNEL, 2, GROUPS * STATE), KERNEL ** -0.5, 3.0, ((2, 4),))
    conv_bias_x = jnp.clip(-0.9 + 0.79999997 * jax.random.uniform(key_list[6], (HEADS * HEAD_DIM,), jnp.float32) ** block_scale(key_list[6], (HEADS * HEAD_DIM,), ((0, 4),), -0.2, 0.2), -0.9, -0.1)
    conv_bias_bc = jnp.clip(-0.9 + 0.79999997 * jax.random.uniform(key_list[7], (2, GROUPS * STATE), jnp.float32) ** block_scale(key_list[7], (2, GROUPS * STATE), ((1, 4),), -0.2, 0.2), -0.9, -0.1)
    dt_bias = draw_dt_bias(jax.random.fold_in(key_list[12], 71), part)
    a_log = draw_a_log(jax.random.fold_in(key_list[12], 71), part)
    d_skip = jnp.clip(0.5 + 1.5 * jax.random.uniform(key_list[10], (HEADS,), jnp.float32) ** block_scale(key_list[10], (HEADS,), ((0, 4),), -0.2, 0.2), 0.5, 2.0)
    norm_gain = jnp.clip(1.0 + 0.1 * jax.random.normal(key_list[11], (HEADS * HEAD_DIM,), jnp.float32), 0.5, 1.5)
    return {"x_in": x_in, "bc_in": bc_in, "z_in": z_in, "dt_raw": dt_raw, "conv_x": conv_x, "conv_bc": conv_bc, "conv_bias_x": conv_bias_x, "conv_bias_bc": conv_bias_bc, "dt_bias": dt_bias, "a_log": a_log, "d_skip": d_skip, "norm_gain": norm_gain}


eps = 1e-05

def conv_valid(padded, weight, offset_bias):
    lag_rows = weight.shape[0] - 1
    length = padded.shape[0] - lag_rows
    total = jnp.zeros((length,) + padded.shape[1:], jnp.float32) + offset_bias.astype(jnp.float32)
    for position in range(weight.shape[0]):
        total = total + padded[position:position + length].astype(jnp.float32) * weight[position].astype(jnp.float32)
    return jax.nn.silu(total).astype(jnp.bfloat16)

def span_parts(x_span, b_span, step_span, log_span):
    cumul = jnp.cumsum(log_span, axis=0)
    tail_fade = jnp.exp(cumul[-1][None] - cumul) * step_span
    scaled = tail_fade[..., None] * x_span
    contrib = jnp.einsum('sghp,sgn->ghpn', scaled, b_span, precision=lax.Precision.HIGHEST)
    return (contrib, jnp.exp(cumul[-1]))

def span_output(carried, x_span, b_span, c_span, step_span, log_span):
    cumul = jnp.cumsum(log_span, axis=0)
    length = cumul.shape[0]
    scores = jnp.einsum('tgn,sgn->tsg', c_span, b_span, precision=lax.Precision.HIGHEST)
    places = jnp.arange(length)
    causal = places[:, None] >= places[None, :]
    spacing = cumul[:, None] - cumul[None, :]
    decay_mat = jnp.exp(jnp.where(causal[:, :, None, None], spacing, -jnp.inf))
    weights = decay_mat * scores[..., None] * step_span[None]
    inside = jnp.einsum('tsgh,sghp->tghp', weights, x_span, precision=lax.Precision.HIGHEST)
    readout = jnp.einsum('tgn,ghpn->tghp', c_span, carried, precision=lax.Precision.HIGHEST)
    return inside + jnp.exp(cumul)[..., None] * readout

def reference(x_in, bc_in, z_in, dt_raw, conv_x, conv_bc, conv_bias_x, conv_bias_bc, dt_bias, a_log, d_skip, norm_gain):
    lag_rows = KERNEL - 1
    x_conv = conv_valid(jnp.concatenate([jnp.zeros((lag_rows, x_in.shape[1]), x_in.dtype), x_in], 0), conv_x, conv_bias_x)
    bc_conv = conv_valid(jnp.concatenate([jnp.zeros((lag_rows,) + bc_in.shape[1:], bc_in.dtype), bc_in], 0), conv_bc, conv_bias_bc)
    per_group = HEADS // GROUPS
    x_heads = x_conv.astype(jnp.float32).reshape(TOKENS, GROUPS, per_group, HEAD_DIM)
    b_all = bc_conv[:, 0].astype(jnp.float32).reshape(TOKENS, GROUPS, STATE)
    c_all = bc_conv[:, 1].astype(jnp.float32).reshape(TOKENS, GROUPS, STATE)
    step_size = jax.nn.softplus(dt_raw + dt_bias[None]).reshape(TOKENS, GROUPS, per_group)
    log_fade = (-jnp.exp(a_log)).reshape(GROUPS, per_group)[None] * step_size
    blocks = TOKENS // SPAN

    def by_block(values):
        return values.reshape((blocks, SPAN) + values.shape[1:])
    inputs = (by_block(x_heads), by_block(b_all), by_block(c_all), by_block(step_size), by_block(log_fade))

    def advance(carried, pieces):
        output = span_output(carried, pieces[0], pieces[1], pieces[2], pieces[3], pieces[4])
        contrib, fading = span_parts(pieces[0], pieces[1], pieces[3], pieces[4])
        return (fading[..., None, None] * carried + contrib, output)
    zero_state = jnp.zeros((GROUPS, per_group, HEAD_DIM, STATE), jnp.float32)
    last_state, outputs = lax.scan(advance, zero_state, inputs)
    ssm_out = outputs.reshape(TOKENS, GROUPS, per_group, HEAD_DIM)
    ssm_out = ssm_out + d_skip.reshape(GROUPS, per_group)[None, :, :, None] * x_heads
    gate_vals = jax.nn.silu(z_in.astype(jnp.float32)).reshape(TOKENS, GROUPS, per_group * HEAD_DIM)
    gated = ssm_out.reshape(TOKENS, GROUPS, per_group * HEAD_DIM) * gate_vals
    meansq = lax.optimization_barrier(jnp.mean(gated * gated, axis=-1, keepdims=True))
    normed = gated * lax.rsqrt(meansq + eps) * norm_gain.reshape(GROUPS, per_group * HEAD_DIM)[None]
    mixed = normed.astype(jnp.bfloat16).reshape(TOKENS, HEADS * HEAD_DIM)
    final_state = last_state.reshape(HEADS, HEAD_DIM, STATE)
    return (mixed, final_state)
```

```python
import functools
import math

import jax
import jax.numpy as jnp
from jax import lax
from jax.experimental import pallas as pl
from jax.experimental.pallas import tpu as pltpu
from jax.sharding import PartitionSpec as P

HEAD_DIM = 64
STATE = 256
SPAN = 128
CHUNK = 512
HEADS_CHUNK = CHUNK // HEAD_DIM
HALO = 8
LOG2E = math.log2(math.e)

eps = 1e-05
F32 = jnp.float32
BF16 = jnp.bfloat16


def silu(v):
    half = 0.5 * v
    return half * jnp.tanh(half) + half


def dot(a, b):
    return jnp.dot(a, b, preferred_element_type=F32)


def rescaled(gated, gain):
    gated = gated.astype(F32)
    meansq = jnp.mean(gated * gated, axis=-1, keepdims=True)
    return (gated * lax.rsqrt(meansq + eps) * gain).astype(BF16)


def finish_kernel(groups, gated_ref, gain_ref, final_ref, out_any, state_any, last, turned, sems):
    rows, channels = gated_ref.shape
    width = channels // groups
    done = channels - width
    blocks = rows // SPAN
    copies = []
    for g in range(groups - 1):
        lanes = pl.ds(g * width, width)
        copies.append(
            pltpu.make_async_copy(gated_ref.at[:, lanes], out_any.at[:, lanes], sems.at[g])
        )
        copies[-1].start()
    for b in range(blocks):
        at = slice(b * SPAN, (b + 1) * SPAN)
        last[at] = rescaled(gated_ref[at, done:], gain_ref[:, done:])
        copies.append(
            pltpu.make_async_copy(
                last.at[pl.ds(b * SPAN, SPAN)],
                out_any.at[pl.ds(b * SPAN, SPAN), pl.ds(done, width)],
                sems.at[groups - 1 + b],
            )
        )
        copies[-1].start()
    part = CHUNK // HEAD_DIM
    for c in range(channels // CHUNK):
        block = final_ref[:, c * CHUNK : (c + 1) * CHUNK].astype(F32).T
        turned[c * part : (c + 1) * part] = block.reshape(part, HEAD_DIM, block.shape[1])
    copies.append(pltpu.make_async_copy(turned, state_any, sems.at[groups - 1 + blocks]))
    copies[-1].start()
    for copy in copies:
        copy.wait()


def finish(gated, gain, final, groups):
    rows, channels = gated.shape
    share = final.shape[0]
    heads = channels // HEAD_DIM
    whole = pl.BlockSpec(memory_space=pltpu.VMEM)
    away = pl.BlockSpec(memory_space=pl.ANY)
    return pl.pallas_call(
        functools.partial(finish_kernel, groups),
        in_specs=[whole, whole, whole],
        out_specs=[away, away],
        out_shape=[
            jax.ShapeDtypeStruct((rows, channels), BF16),
            jax.ShapeDtypeStruct((heads, HEAD_DIM, share), F32),
        ],
        scratch_shapes=[
            pltpu.VMEM((rows, channels // groups), BF16),
            pltpu.VMEM((heads, HEAD_DIM, share), F32),
            pltpu.SemaphoreType.DMA((groups + rows // SPAN,)),
        ],
        compiler_params=pltpu.CompilerParams(vmem_limit_bytes=16 << 20),
        cost_estimate=pl.CostEstimate(
            flops=4 * rows * channels, bytes_accessed=4 * rows * channels, transcendentals=rows
        ),
    )(gated, gain, final)


EDGE = 16
EDGE_TOKENS = 4
BLOCK = 32
MESH = pl.DeviceIdType.MESH


def conv_rows(read, before, taps, bias, rows, write):
    step = 64
    lag = taps.shape[0] - 1
    for r in range(0, rows, step):
        here = read(r, step).astype(F32)
        window = jnp.concatenate([before, here], axis=0)
        before = here[step - HALO :]
        acc = bias + here * taps[lag][None]
        for k in range(lag):
            at = HALO - lag + k
            acc = acc + window[at : at + step] * taps[k][None]
        write(r, step, silu(acc))


def leading(n, chunks):
    return chunks + max(0, n - 4)


def exact_dot(a, b):
    return jnp.dot(a, b, preferred_element_type=F32, precision=lax.Precision.HIGHEST)


def split(v, parts):
    out = []
    for _ in range(parts):
        piece = v.astype(BF16)
        out.append(piece.astype(F32))
        v = v - out[-1]
    return jnp.concatenate(out, axis=1).astype(BF16)


def scan_kernel(
    n,
    x_ref,
    taps_ref,
    bias_ref,
    bc_ref,
    taps_bc_ref,
    bias_bc_ref,
    dt_ref,
    dt_bias_ref,
    a_log_ref,
    skip_ref,
    z_ref,
    gain_ref,
    x_any,
    bc_any,
    y_ref,
    final_out,
    xc,
    sent,
    came,
    piece,
    local,
    cumul_ref,
    row_ref,
    tail_ref,
    entry_ref,
    fade_ref,
    bt_ref,
    c_ref,
    acc_ref,
    edge_x,
    edge_bc,
    send_sem,
    recv_sem,
    piece_send,
    piece_recv,
    edge_send,
    edge_recv,
):
    s = pl.program_id(0)
    chunks = sent.shape[0]
    lead = leading(n, chunks)
    last_step = lead + chunks - 1
    me = lax.axis_index("ctx")
    rows = x_ref.shape[0]
    spans = rows // SPAN
    heads = dt_ref.shape[0]
    groups = bt_ref.shape[0]
    per = chunks // groups
    lines = bc_ref.shape[0] // rows
    tile = max(lines, 8)
    share = STATE // n
    right = jnp.minimum(me + 1, n - 1)

    def edge_copies():
        return [
            pltpu.make_async_remote_copy(
                src_ref=whole.at[pl.ds(whole.shape[0] - edge.shape[0], edge.shape[0])],
                dst_ref=edge,
                send_sem=edge_send.at[i],
                recv_sem=edge_recv.at[i],
                device_id={"ctx": right},
                device_id_type=MESH,
            )
            for i, (whole, edge) in enumerate(((bc_any, edge_bc), (x_any, edge_x)))
        ]

    def onward(c):
        return pltpu.make_async_remote_copy(
            src_ref=sent.at[c],
            dst_ref=came.at[c],
            send_sem=send_sem.at[c],
            recv_sem=recv_sem.at[c],
            device_id={"ctx": right},
            device_id_type=MESH,
        )

    def handed(q, c):
        return pltpu.make_async_remote_copy(
            src_ref=sent.at[c, pl.ds(pl.multiple_of(q * share, share), share)],
            dst_ref=piece.at[c],
            send_sem=piece_send.at[q, c],
            recv_sem=piece_recv.at[c],
            device_id={"ctx": q},
            device_id_type=MESH,
        )

    def spread_of(c, parts=1, kind=F32):
        shape = (parts * heads, CHUNK)
        return (
            lax.broadcasted_iota(jnp.int32, shape, 1) // HEAD_DIM + c * HEADS_CHUNK
            == lax.broadcasted_iota(jnp.int32, shape, 0) % heads
        ).astype(kind)

    def pick_of(c):
        shape = (3 * heads, 128)
        return (
            lax.broadcasted_iota(jnp.int32, shape, 1) + c * HEADS_CHUNK
            == lax.broadcasted_iota(jnp.int32, shape, 0) % heads
        ).astype(BF16)

    def bc_block(b):
        size = BLOCK * lines
        reach = EDGE_TOKENS * lines
        here = bc_ref[b * size : (b + 1) * size].astype(F32)
        before = edge_bc[...] if b == 0 else bc_ref[b * size - reach : b * size]
        window = jnp.concatenate([before.astype(F32), here], axis=0)
        taps_all = taps_bc_ref[...].astype(F32)
        lag = taps_all.shape[0] // lines - 1
        bias = bias_bc_ref[...]
        acc = jnp.concatenate([bias] * (tile // lines), axis=0)[None]
        for k in range(lag + 1):
            taps = taps_all[k * lines : (k + 1) * lines]
            taps = jnp.concatenate([taps] * (tile // lines), axis=0)
            first = (EDGE_TOKENS - lag + k) * lines
            acc = acc + window[first : first + size].reshape(size // tile, tile, 128) * taps[None]
        acc_ref[b * size : (b + 1) * size] = acc.reshape(size, 128)

    def project(side, g):
        for k in range(spans):
            at = slice(k * SPAN, (k + 1) * SPAN)
            for half in range(STATE // 128):
                line = 2 * (g * (STATE // 128) + half) + side
                own = slice(half * 128, (half + 1) * 128)
                v = silu(acc_ref[pl.ds(k * SPAN * lines + line, SPAN, stride=lines), :])
                if side == 0:
                    bt_ref[g, own, at] = v.astype(BF16).astype(F32).T.astype(BF16)
                else:
                    c_ref[g, at, own] = v.astype(BF16)

    @pl.when(s == 0)
    def _():
        barrier = pltpu.get_barrier_semaphore()
        for k in range(1, n):
            pl.semaphore_signal(
                barrier, inc=1, device_id={"ctx": lax.rem(me + k, n)}, device_id_type=MESH
            )
        rate = -LOG2E * jnp.exp(a_log_ref[...])
        lower = (
            lax.broadcasted_iota(jnp.int32, (SPAN, SPAN), 0)
            >= lax.broadcasted_iota(jnp.int32, (SPAN, SPAN), 1)
        ).astype(F32)
        so_far = jnp.zeros((1, heads), F32)
        for k in range(spans):
            at = slice(k * SPAN, (k + 1) * SPAN)
            v = dt_ref[:, at].T + dt_bias_ref[...]
            step = jnp.maximum(v, 0.0) + jnp.log1p(jnp.exp(-jnp.abs(v)))
            cumul = exact_dot(lower, step * rate)
            last = cumul[SPAN - 1 :]
            tail = jnp.exp2(last - cumul) * step
            entry = jnp.exp2(cumul)
            cumul_ref[at] = split(cumul, 3)
            tail_ref[at] = split(tail, 2)
            entry_ref[at] = split(entry, 2)
            rowed = cumul - jnp.log2(step)
            wide = jnp.concatenate([rowed] * (128 // heads), axis=1) if heads < 128 else rowed
            row_ref[:, at] = wide.T[:heads]
            fade_ref[k : k + 1] = jnp.exp2(last)
            fade_ref[spans + 2 + k : spans + 3 + k] = jnp.exp2(so_far)
            so_far = so_far + last
        fade_ref[spans : spans + 1] = jnp.exp2(so_far)
        fade_ref[spans + 1 : spans + 2] = skip_ref[...]
        if fade_ref.shape[0] > 2 * spans + 2:
            fade_ref[2 * spans + 2 :] = jnp.zeros((fade_ref.shape[0] - 2 * spans - 2, heads), F32)

        pl.semaphore_wait(barrier, n - 1)

        @pl.when(me < n - 1)
        def _():
            for copy in edge_copies():
                copy.start()

        for b in range(1, rows // BLOCK):
            bc_block(b)

        @pl.when(me == 0)
        def _():
            edge_x[...] = jnp.zeros_like(edge_x)
            edge_bc[...] = jnp.zeros_like(edge_bc)
            came[...] = jnp.zeros_like(came)

        @pl.when(me > 0)
        def _():
            for copy in edge_copies():
                copy.wait_recv()

        bc_block(0)
        project(0, 0)

    def join(c, carry):
        onward(c).wait_recv()
        got = came[c]
        fades = exact_dot(fade_ref[...], spread_of(c))
        mine = sent[c].astype(F32)
        sent[c] = (fades[spans : spans + 1] * got.astype(F32) + mine).astype(BF16)

        @pl.when(me < n - 1)
        def _():
            onward(c).start()

        @pl.when(me == n - 1)
        def _():
            lax.fori_loop(0, n - 1, lambda q, z: (handed(q, c).start(), z)[1], 0)

        return carry

    base = jnp.where(me == 1, 1, jnp.minimum(lead, chunks + me - 2))
    first = jnp.clip(s - base, 0, chunks)
    stop = jnp.where(s == last_step, chunks, jnp.clip(s - base + 1, 0, chunks))
    stop = jnp.where(me == 0, first, stop)
    lax.fori_loop(first, stop, join, 0)

    low = lax.broadcasted_iota(jnp.int32, (SPAN, 2 * HEAD_DIM), 1) < HEAD_DIM
    pairs = HEADS_CHUNK // 2

    def pair_lanes(pair):
        return slice(pair * 2 * HEAD_DIM, (pair + 1) * 2 * HEAD_DIM)

    @pl.when(s < chunks)
    def _():
        j = s
        bt = bt_ref.at[j // per]
        taps = taps_ref[...].astype(F32)
        before = edge_x[:, pl.ds(pl.multiple_of(j * CHUNK, CHUNK), CHUNK)].astype(F32)[EDGE - HALO :]
        fades = exact_dot(fade_ref[...], spread_of(j))
        spread = spread_of(j, 2, BF16)

        def write(r, size, value):
            xc[j, r : r + size] = value.astype(BF16)

        conv_rows(lambda r, size: x_ref[r : r + size], before, taps, bias_ref[...], rows, write)
        state = None
        for k in range(spans):
            at = slice(k * SPAN, (k + 1) * SPAN)
            scaled = (xc[j, at].astype(F32) * dot(tail_ref[at], spread)).astype(BF16)
            part = dot(bt[:, at], scaled)
            state = part if state is None else fades[k : k + 1] * state + part
            if k < spans - 1:
                local[j, k] = state.astype(BF16)
        sent[j] = state.astype(BF16)

        @pl.when(me == 0)
        def _():
            onward(j).start()

    @pl.when(s == 0)
    def _():
        project(1, 0)
        for g in range(1, groups):
            project(0, g)
            project(1, g)

    @pl.when(s >= lead)
    def _():
        j = s - lead
        fades = exact_dot(fade_ref[...], spread_of(j))
        spread = spread_of(j, 2, BF16)
        pick = pick_of(j)
        g = j // per
        causal = lax.broadcasted_iota(jnp.int32, (SPAN, SPAN), 0) >= lax.broadcasted_iota(
            jnp.int32, (SPAN, SPAN), 1
        )
        none = jnp.zeros((), BF16)
        head_rows = pl.ds(pl.multiple_of(j * HEADS_CHUNK, HEADS_CHUNK), HEADS_CHUNK)
        for k in range(spans):
            at = slice(k * SPAN, (k + 1) * SPAN)
            c_span = c_ref[g, at]
            scores = dot(c_span, bt_ref[g, :, at])
            row_span = row_ref[head_rows, at]
            if k == 0:
                state = came[j]
            else:
                faded = jnp.broadcast_to(fades[spans + 2 + k : spans + 3 + k], (STATE, CHUNK)).astype(BF16)
                state = local[j, k - 1] + faded * came[j]
            readout = dot(c_span, state) * dot(entry_ref[at], spread)
            col = dot(cumul_ref[at], pick)
            for pair in range(pairs):
                lanes = pair_lanes(pair)
                weights = []
                for h in (2 * pair, 2 * pair + 1):
                    spacing = col[:, h : h + 1] - row_span[h : h + 1]
                    decay = jnp.exp2(jnp.where(causal, spacing, -jnp.inf))
                    weights.append((decay * scores).astype(BF16))
                x_pair = xc[j, at, lanes]
                stacked = jnp.concatenate(
                    [jnp.where(low, x_pair, none), jnp.where(low, none, x_pair)], axis=0
                )
                within = dot(jnp.concatenate(weights, axis=1), stacked)
                out = (
                    within
                    + x_pair.astype(F32) * fades[spans + 1 : spans + 2, lanes]
                    + readout[:, lanes]
                )
                there = pl.ds(pl.multiple_of(j * CHUNK + pair * 2 * HEAD_DIM, 128), 2 * HEAD_DIM)
                y_ref[at, there] = (out * silu(z_ref[at, lanes].astype(F32))).astype(BF16)

    for g in range(groups - 1):

        @pl.when(s == lead + (g + 1) * per - 1)
        def _(g=g):
            own = slice(g * per * CHUNK, (g + 1) * per * CHUNK)
            for k in range(0, rows, BLOCK):
                y_ref[k : k + BLOCK, own] = rescaled(y_ref[k : k + BLOCK, own], gain_ref[:, own])

    @pl.when(s == last_step)
    def _():
        @pl.when(me < n - 1)
        def _():
            for copy in edge_copies():
                copy.wait_send()
            for c in range(chunks):
                onward(c).wait_send()
            for c in range(chunks):
                handed(0, c).wait_recv()
                final_out[:, c * CHUNK : (c + 1) * CHUNK] = piece[c]

        @pl.when(me == n - 1)
        def _():
            for c in range(chunks):
                lax.fori_loop(0, n - 1, lambda q, z: (handed(q, c).wait_send(), z)[1], 0)
                final_out[:, c * CHUNK : (c + 1) * CHUNK] = sent[c, (n - 1) * share :]


def scan(n, x, taps, bias, bc, taps_bc, bias_bc, dt, dt_bias, a_log, skip, z, gain, groups):
    rows, channels = x.shape
    chunks = channels // CHUNK
    heads = dt.shape[0]
    lead = leading(n, chunks)
    lines = bc.shape[0] // rows
    share = STATE // n
    spans = rows // SPAN
    turn = lambda s: (0, jnp.minimum(s, chunks - 1))
    later = lambda s: (0, jnp.maximum(s - lead, 0))
    still = lambda s: (0, 0)
    return pl.pallas_call(
        functools.partial(scan_kernel, n),
        grid=(lead + chunks,),
        in_specs=[
            pl.BlockSpec((rows, CHUNK), turn),
            pl.BlockSpec((taps.shape[0], CHUNK), turn),
            pl.BlockSpec((1, CHUNK), turn),
            pl.BlockSpec(bc.shape, still),
            pl.BlockSpec(taps_bc.shape, still),
            pl.BlockSpec(bias_bc.shape, still),
            pl.BlockSpec((heads, rows), still),
            pl.BlockSpec((1, heads), still),
            pl.BlockSpec((1, heads), still),
            pl.BlockSpec((1, heads), still),
            pl.BlockSpec((rows, CHUNK), later),
            pl.BlockSpec((1, channels), still),
            pl.BlockSpec(memory_space=pl.ANY),
            pl.BlockSpec(memory_space=pl.ANY),
        ],
        out_specs=[
            pl.BlockSpec(memory_space=pltpu.VMEM),
            pl.BlockSpec(memory_space=pltpu.VMEM),
        ],
        out_shape=[
            pltpu.VMEM((rows, channels), BF16),
            pltpu.VMEM((share, channels), BF16),
        ],
        scratch_shapes=[
            pltpu.VMEM((chunks, rows, CHUNK), BF16),
            pltpu.VMEM((chunks, STATE, CHUNK), BF16),
            pltpu.VMEM((chunks, STATE, CHUNK), BF16),
            pltpu.VMEM((chunks, share, CHUNK), BF16),
            pltpu.VMEM((chunks, spans - 1, STATE, CHUNK), BF16),
            pltpu.VMEM((rows, 3 * heads), BF16),
            pltpu.VMEM((heads, rows), F32),
            pltpu.VMEM((rows, 2 * heads), BF16),
            pltpu.VMEM((rows, 2 * heads), BF16),
            pltpu.VMEM((-(-(2 * spans + 2) // 8) * 8, heads), F32),
            pltpu.VMEM((groups, STATE, rows), BF16),
            pltpu.VMEM((groups, rows, STATE), BF16),
            pltpu.VMEM((rows * lines, 128), F32),
            pltpu.VMEM((EDGE, channels), BF16),
            pltpu.VMEM((EDGE_TOKENS * lines, 128), BF16),
            pltpu.SemaphoreType.DMA((chunks,)),
            pltpu.SemaphoreType.DMA((chunks,)),
            pltpu.SemaphoreType.DMA((n - 1, chunks)),
            pltpu.SemaphoreType.DMA((chunks,)),
            pltpu.SemaphoreType.DMA((2,)),
            pltpu.SemaphoreType.DMA((2,)),
        ],
        compiler_params=pltpu.CompilerParams(
            dimension_semantics=("arbitrary",),
            vmem_limit_bytes=56 << 20,
            collective_id=0,
            has_side_effects=True,
        ),
        cost_estimate=pl.CostEstimate(
            flops=20 * rows * channels * STATE, bytes_accessed=4 * rows * channels, transcendentals=4 * rows * channels
        ),
    )(x, taps, bias, bc, taps_bc, bias_bc, dt, dt_bias, a_log, skip, z, gain, x, bc)


def per_device(
    x_in,
    bc_in,
    z_in,
    dt_raw,
    conv_x,
    conv_bc,
    conv_bias_x,
    conv_bias_bc,
    dt_bias,
    a_log,
    d_skip,
    norm_gain,
):
    rows, channels = x_in.shape
    heads = dt_raw.shape[1]
    n = lax.axis_size("ctx")
    tiles = bc_in.shape[2] // 128
    groups = bc_in.shape[2] // STATE

    def lined(v):
        return v.reshape(-1, 2, tiles, 128).transpose(0, 2, 1, 3).reshape(-1, 128)

    gated, final = scan(
        n,
        x_in,
        conv_x,
        conv_bias_x[None],
        lined(bc_in),
        lined(conv_bc),
        lined(conv_bias_bc),
        dt_raw.T,
        dt_bias[None],
        a_log[None],
        d_skip[None],
        z_in,
        norm_gain[None],
        groups,
    )
    return tuple(finish(gated, norm_gain[None], final, groups))


def solution(mesh):
    in_specs = (
        P(("group", "ctx"), "tp"),
        P(("group", "ctx"), None, "tp"),
        P(("group", "ctx"), "tp"),
        P(("group", "ctx"), "tp"),
        P(None, "tp"),
        P(None, None, "tp"),
        P("tp"),
        P(None, "tp"),
        P("tp"),
        P("tp"),
        P("tp"),
        P("tp"),
    )
    out_specs = (P(("group", "ctx"), "tp"), P(("group", "tp"), None, "ctx"))
    return jax.shard_map(
        per_device, mesh=mesh, in_specs=in_specs, out_specs=out_specs, check_vma=False
    )
```

```python
import functools
import math

import jax
import jax.numpy as jnp
from jax import lax
from jax.experimental import pallas as pl
from jax.experimental.pallas import tpu as pltpu
from jax.sharding import PartitionSpec as P

HEAD_DIM = 64
STATE = 256
SPAN = 128
CHUNK = 512
HEADS_CHUNK = CHUNK // HEAD_DIM
HALO = 8
LOG2E = math.log2(math.e)

eps = 1e-05
F32 = jnp.float32
BF16 = jnp.bfloat16


def silu(v):
    half = 0.5 * v
    return half * jnp.tanh(half) + half


def dot(a, b):
    return jnp.dot(a, b, preferred_element_type=F32)


def rescaled(gated, gain):
    gated = gated.astype(F32)
    meansq = jnp.mean(gated * gated, axis=-1, keepdims=True)
    return (gated * lax.rsqrt(meansq + eps) * gain).astype(BF16)


def finish_kernel(groups, gated_ref, gain_ref, final_ref, out_any, state_any, last, turned, sems):
    rows, channels = gated_ref.shape
    width = channels // groups
    done = channels - width
    blocks = rows // SPAN
    copies = []
    for g in range(groups - 1):
        lanes = pl.ds(g * width, width)
        copies.append(
            pltpu.make_async_copy(gated_ref.at[:, lanes], out_any.at[:, lanes], sems.at[g])
        )
        copies[-1].start()
    for b in range(blocks):
        at = slice(b * SPAN, (b + 1) * SPAN)
        last[at] = rescaled(gated_ref[at, done:], gain_ref[:, done:])
        copies.append(
            pltpu.make_async_copy(
                last.at[pl.ds(b * SPAN, SPAN)],
                out_any.at[pl.ds(b * SPAN, SPAN), pl.ds(done, width)],
                sems.at[groups - 1 + b],
            )
        )
        copies[-1].start()
    part = CHUNK // HEAD_DIM
    for c in range(channels // CHUNK):
        block = final_ref[:, c * CHUNK : (c + 1) * CHUNK].astype(F32).T
        turned[c * part : (c + 1) * part] = block.reshape(part, HEAD_DIM, block.shape[1])
    copies.append(pltpu.make_async_copy(turned, state_any, sems.at[groups - 1 + blocks]))
    copies[-1].start()
    for copy in copies:
        copy.wait()


def finish(gated, gain, final, groups):
    rows, channels = gated.shape
    share = final.shape[0]
    heads = channels // HEAD_DIM
    whole = pl.BlockSpec(memory_space=pltpu.VMEM)
    away = pl.BlockSpec(memory_space=pl.ANY)
    return pl.pallas_call(
        functools.partial(finish_kernel, groups),
        in_specs=[whole, whole, whole],
        out_specs=[away, away],
        out_shape=[
            jax.ShapeDtypeStruct((rows, channels), BF16),
            jax.ShapeDtypeStruct((heads, HEAD_DIM, share), F32),
        ],
        scratch_shapes=[
            pltpu.VMEM((rows, channels // groups), BF16),
            pltpu.VMEM((heads, HEAD_DIM, share), F32),
            pltpu.SemaphoreType.DMA((groups + rows // SPAN,)),
        ],
        compiler_params=pltpu.CompilerParams(vmem_limit_bytes=16 << 20),
        cost_estimate=pl.CostEstimate(
            flops=4 * rows * channels, bytes_accessed=4 * rows * channels, transcendentals=rows
        ),
    )(gated, gain, final)


EDGE = 16
EDGE_TOKENS = 4
BLOCK = 32
MESH = pl.DeviceIdType.MESH


def leading(n, chunks):
    return chunks + max(0, n - 4)


def exact_dot(a, b):
    return jnp.dot(a, b, preferred_element_type=F32, precision=lax.Precision.HIGHEST)


def split(v, parts):
    out = []
    for _ in range(parts):
        piece = v.astype(BF16)
        out.append(piece.astype(F32))
        v = v - out[-1]
    return jnp.concatenate(out, axis=1).astype(BF16)


def scan_kernel(
    n,
    x_ref,
    taps_ref,
    bias_ref,
    bc_ref,
    taps_bc_ref,
    bias_bc_ref,
    dt_ref,
    dt_bias_ref,
    a_log_ref,
    skip_ref,
    z_ref,
    gain_ref,
    x_any,
    bc_any,
    y_ref,
    final_out,
    xc,
    sent,
    came,
    piece,
    local,
    cumul_ref,
    row_ref,
    tail_ref,
    entry_ref,
    fade_ref,
    bt_ref,
    c_ref,
    acc_ref,
    lift_ref,
    spread_ref,
    wide_ref,
    edge_x,
    edge_bc,
    send_sem,
    recv_sem,
    piece_send,
    piece_recv,
    edge_send,
    edge_recv,
):
    s = pl.program_id(0)
    chunks = sent.shape[0]
    lead = leading(n, chunks)
    last_step = lead + chunks - 1
    me = lax.axis_index("ctx")
    rows = x_ref.shape[0]
    spans = rows // SPAN
    heads = dt_ref.shape[0]
    groups = bt_ref.shape[0]
    per = chunks // groups
    lines = bc_ref.shape[0] // rows
    tile = max(lines, 8)
    share = STATE // n
    right = jnp.minimum(me + 1, n - 1)

    def edge_copies():
        return [
            pltpu.make_async_remote_copy(
                src_ref=whole.at[pl.ds(whole.shape[0] - edge.shape[0], edge.shape[0])],
                dst_ref=edge,
                send_sem=edge_send.at[i],
                recv_sem=edge_recv.at[i],
                device_id={"ctx": right},
                device_id_type=MESH,
            )
            for i, (whole, edge) in enumerate(((bc_any, edge_bc), (x_any, edge_x)))
        ]

    def onward(c):
        return pltpu.make_async_remote_copy(
            src_ref=sent.at[c],
            dst_ref=came.at[c],
            send_sem=send_sem.at[c],
            recv_sem=recv_sem.at[c],
            device_id={"ctx": right},
            device_id_type=MESH,
        )

    def handed(q, c):
        return pltpu.make_async_remote_copy(
            src_ref=sent.at[c, pl.ds(pl.multiple_of(q * share, share), share)],
            dst_ref=piece.at[c],
            send_sem=piece_send.at[q, c],
            recv_sem=piece_recv.at[c],
            device_id={"ctx": q},
            device_id_type=MESH,
        )

    def spread_of(c):
        shape = (3 * heads, CHUNK)
        return (
            lax.broadcasted_iota(jnp.int32, shape, 1) // HEAD_DIM + c * HEADS_CHUNK
            == lax.broadcasted_iota(jnp.int32, shape, 0) % heads
        ).astype(BF16)

    def pick_of(c):
        shape = (3 * heads, 128)
        return (
            lax.broadcasted_iota(jnp.int32, shape, 1) + c * HEADS_CHUNK
            == lax.broadcasted_iota(jnp.int32, shape, 0) % heads
        ).astype(BF16)

    def bc_block(b):
        size = BLOCK * lines
        reach = EDGE_TOKENS * lines
        here = bc_ref[b * size : (b + 1) * size].astype(F32)
        before = edge_bc[...] if b == 0 else bc_ref[b * size - reach : b * size]
        window = jnp.concatenate([before.astype(F32), here], axis=0)
        taps_all = taps_bc_ref[...].astype(F32)
        lag = taps_all.shape[0] // lines - 1
        bias = bias_bc_ref[...]
        acc = jnp.concatenate([bias] * (tile // lines), axis=0)[None]
        for k in range(lag + 1):
            taps = taps_all[k * lines : (k + 1) * lines]
            taps = jnp.concatenate([taps] * (tile // lines), axis=0)
            first = (EDGE_TOKENS - lag + k) * lines
            acc = acc + window[first : first + size].reshape(size // tile, tile, 128) * taps[None]
        acc_ref[b * size : (b + 1) * size] = acc.reshape(size, 128)

    def project(side, g):
        for k in range(spans):
            at = slice(k * SPAN, (k + 1) * SPAN)
            for half in range(STATE // 128):
                line = 2 * (g * (STATE // 128) + half) + side
                own = slice(half * 128, (half + 1) * 128)
                v = silu(acc_ref[pl.ds(k * SPAN * lines + line, SPAN, stride=lines), :])
                if side == 0:
                    bt_ref[g, own, at] = v.astype(BF16).astype(F32).T.astype(BF16)
                else:
                    c_ref[g, at, own] = v.astype(BF16)

    @pl.when(s == 0)
    def _():
        barrier = pltpu.get_barrier_semaphore()
        for k in range(1, n):
            pl.semaphore_signal(
                barrier, inc=1, device_id={"ctx": lax.rem(me + k, n)}, device_id_type=MESH
            )
        rate = -LOG2E * jnp.exp(a_log_ref[...])
        lower = (
            lax.broadcasted_iota(jnp.int32, (SPAN, SPAN), 0)
            >= lax.broadcasted_iota(jnp.int32, (SPAN, SPAN), 1)
        ).astype(F32)
        so_far = jnp.zeros((1, heads), F32)
        for k in range(spans):
            at = slice(k * SPAN, (k + 1) * SPAN)
            v = dt_ref[:, at].T + dt_bias_ref[...]
            step = jnp.maximum(v, 0.0) + jnp.log1p(jnp.exp(-jnp.abs(v)))
            cumul = exact_dot(lower, step * rate)
            last = cumul[SPAN - 1 :]
            tail = jnp.exp2(last - cumul) * step
            entry = jnp.exp2(cumul)
            cumul_ref[at] = split(cumul, 3)
            tail_ref[at] = split(tail, 2)
            entry_ref[at] = split(entry, 2)
            rowed = cumul - jnp.log2(step)
            wide = jnp.concatenate([rowed] * (128 // heads), axis=1) if heads < 128 else rowed
            row_ref[:, at] = wide.T[:heads]
            fade_ref[k : k + 1] = jnp.exp2(last)
            fade_ref[spans + 2 + k : spans + 3 + k] = jnp.exp2(so_far)
            so_far = so_far + last
        fade_ref[spans : spans + 1] = jnp.exp2(so_far)
        fade_ref[spans + 1 : spans + 2] = skip_ref[...]
        if fade_ref.shape[0] > 2 * spans + 2:
            fade_ref[2 * spans + 2 :] = jnp.zeros((fade_ref.shape[0] - 2 * spans - 2, heads), F32)

        pl.semaphore_wait(barrier, n - 1)

        @pl.when(me < n - 1)
        def _():
            for copy in edge_copies():
                copy.start()

        for b in range(1, rows // BLOCK):
            bc_block(b)

        @pl.when(me == 0)
        def _():
            edge_x[...] = jnp.zeros_like(edge_x)
            edge_bc[...] = jnp.zeros_like(edge_bc)
            came[...] = jnp.zeros_like(came)

        @pl.when(me > 0)
        def _():
            for copy in edge_copies():
                copy.wait_recv()

        bc_block(0)
        project(0, 0)

    def join(c, carry):
        onward(c).wait_recv()
        got = came[c]
        fades = wide_ref[c]
        mine = sent[c].astype(F32)
        sent[c] = (fades[spans : spans + 1] * got.astype(F32) + mine).astype(BF16)

        @pl.when(me < n - 1)
        def _():
            onward(c).start()

        @pl.when(me == n - 1)
        def _():
            lax.fori_loop(0, n - 1, lambda q, z: (handed(q, c).start(), z)[1], 0)

        return carry

    base = jnp.where(me == 1, 1, jnp.minimum(lead, chunks + me - 2))
    first = jnp.clip(s - base, 0, chunks)
    stop = jnp.where(s == last_step, chunks, jnp.clip(s - base + 1, 0, chunks))
    stop = jnp.where(me == 0, first, stop)
    lax.fori_loop(first, stop, join, 0)

    low = lax.broadcasted_iota(jnp.int32, (SPAN, 2 * HEAD_DIM), 1) < HEAD_DIM
    pairs = HEADS_CHUNK // 2

    def pair_lanes(pair):
        return slice(pair * 2 * HEAD_DIM, (pair + 1) * 2 * HEAD_DIM)

    @pl.when(s < chunks)
    def _():
        j = s
        bt = bt_ref.at[j // per]
        taps = 0.5 * taps_ref[...].astype(F32)
        bias = 0.5 * bias_ref[...]
        lag = taps.shape[0] - 1
        before = edge_x[:, pl.ds(pl.multiple_of(j * CHUNK, CHUNK), CHUNK)].astype(F32)[EDGE - HALO :]
        spread = spread_of(j)
        spread_ref[j] = spread
        fades = dot(split(fade_ref[...], 3), spread)
        wide_ref[j] = fades
        tiles = [slice(i * 128, (i + 1) * 128) for i in range(CHUNK // 128)]
        for i, lanes in enumerate(tiles):
            lift_ref[i, :HALO] = before[:, lanes]
            lift_ref[i, HALO:] = x_ref[:, lanes].astype(F32)
        state = None
        for k in range(spans):
            at = slice(k * SPAN, (k + 1) * SPAN)
            tail = dot(tail_ref[at], spread[: 2 * heads])
            parts = []
            for i, lanes in enumerate(tiles):
                column = []
                for r in range(0, SPAN, 64):
                    first = k * SPAN + r
                    half = bias[:, lanes]
                    for q in range(lag + 1):
                        begin = HALO - lag + q + first
                        half = half + lift_ref[i, begin : begin + 64] * taps[q : q + 1, lanes]
                    value = half * jnp.tanh(half) + half
                    xc[j, first : first + 64, lanes] = value.astype(BF16)
                    column.append((value * tail[r : r + 64, lanes]).astype(BF16))
                parts.append(jnp.concatenate(column, axis=0))
            scaled = jnp.concatenate(parts, axis=1)
            part = dot(bt[:, at], scaled)
            state = part if state is None else fades[k : k + 1] * state + part
            if k < spans - 1:
                local[j, k] = state.astype(BF16)
        sent[j] = state.astype(BF16)

        @pl.when(me == 0)
        def _():
            onward(j).start()

    @pl.when(s == 0)
    def _():
        project(1, 0)
        for g in range(1, groups):
            project(0, g)
            project(1, g)

    @pl.when(s >= lead)
    def _():
        j = s - lead
        fades = wide_ref[j]
        pick = pick_of(j)
        g = j // per
        causal = lax.broadcasted_iota(jnp.int32, (SPAN, SPAN), 0) >= lax.broadcasted_iota(
            jnp.int32, (SPAN, SPAN), 1
        )
        none = jnp.zeros((), BF16)
        head_rows = pl.ds(pl.multiple_of(j * HEADS_CHUNK, HEADS_CHUNK), HEADS_CHUNK)
        for k in range(spans):
            at = slice(k * SPAN, (k + 1) * SPAN)
            c_span = c_ref[g, at]
            scores = dot(c_span, bt_ref[g, :, at])
            row_span = row_ref[head_rows, at]
            if k == 0:
                state = came[j]
            else:
                faded = jnp.broadcast_to(fades[spans + 2 + k : spans + 3 + k], (STATE, CHUNK)).astype(BF16)
                state = local[j, k - 1] + faded * came[j]
            readout = dot(c_span, state) * dot(entry_ref[at], spread_ref[j, : 2 * heads])
            col = dot(cumul_ref[at], pick)
            for pair in range(pairs):
                lanes = pair_lanes(pair)
                weights = []
                for h in (2 * pair, 2 * pair + 1):
                    spacing = col[:, h : h + 1] - row_span[h : h + 1]
                    decay = jnp.exp2(jnp.where(causal, spacing, -jnp.inf))
                    weights.append((decay * scores).astype(BF16))
                x_pair = xc[j, at, lanes]
                stacked = jnp.concatenate(
                    [jnp.where(low, x_pair, none), jnp.where(low, none, x_pair)], axis=0
                )
                within = dot(jnp.concatenate(weights, axis=1), stacked)
                out = (
                    within
                    + x_pair.astype(F32) * fades[spans + 1 : spans + 2, lanes]
                    + readout[:, lanes]
                )
                there = pl.ds(pl.multiple_of(j * CHUNK + pair * 2 * HEAD_DIM, 128), 2 * HEAD_DIM)
                y_ref[at, there] = (out * silu(z_ref[at, lanes].astype(F32))).astype(BF16)

    for g in range(groups - 1):

        @pl.when(s == lead + (g + 1) * per - 1)
        def _(g=g):
            own = slice(g * per * CHUNK, (g + 1) * per * CHUNK)
            for k in range(0, rows, BLOCK):
                y_ref[k : k + BLOCK, own] = rescaled(y_ref[k : k + BLOCK, own], gain_ref[:, own])

    @pl.when(s == last_step)
    def _():
        @pl.when(me < n - 1)
        def _():
            for copy in edge_copies():
                copy.wait_send()
            for c in range(chunks):
                onward(c).wait_send()
            for c in range(chunks):
                handed(0, c).wait_recv()
                final_out[:, c * CHUNK : (c + 1) * CHUNK] = piece[c]

        @pl.when(me == n - 1)
        def _():
            for c in range(chunks):
                lax.fori_loop(0, n - 1, lambda q, z: (handed(q, c).wait_send(), z)[1], 0)
                final_out[:, c * CHUNK : (c + 1) * CHUNK] = sent[c, (n - 1) * share :]


def scan(n, x, taps, bias, bc, taps_bc, bias_bc, dt, dt_bias, a_log, skip, z, gain, groups):
    rows, channels = x.shape
    chunks = channels // CHUNK
    heads = dt.shape[0]
    lead = leading(n, chunks)
    lines = bc.shape[0] // rows
    share = STATE // n
    spans = rows // SPAN
    turn = lambda s: (0, jnp.minimum(s, chunks - 1))
    later = lambda s: (0, jnp.maximum(s - lead, 0))
    still = lambda s: (0, 0)
    return pl.pallas_call(
        functools.partial(scan_kernel, n),
        grid=(lead + chunks,),
        in_specs=[
            pl.BlockSpec((rows, CHUNK), turn),
            pl.BlockSpec((taps.shape[0], CHUNK), turn),
            pl.BlockSpec((1, CHUNK), turn),
            pl.BlockSpec(bc.shape, still),
            pl.BlockSpec(taps_bc.shape, still),
            pl.BlockSpec(bias_bc.shape, still),
            pl.BlockSpec((heads, rows), still),
            pl.BlockSpec((1, heads), still),
            pl.BlockSpec((1, heads), still),
            pl.BlockSpec((1, heads), still),
            pl.BlockSpec((rows, CHUNK), later),
            pl.BlockSpec((1, channels), still),
            pl.BlockSpec(memory_space=pl.ANY),
            pl.BlockSpec(memory_space=pl.ANY),
        ],
        out_specs=[
            pl.BlockSpec(memory_space=pltpu.VMEM),
            pl.BlockSpec(memory_space=pltpu.VMEM),
        ],
        out_shape=[
            pltpu.VMEM((rows, channels), BF16),
            pltpu.VMEM((share, channels), BF16),
        ],
        scratch_shapes=[
            pltpu.VMEM((chunks, rows, CHUNK), BF16),
            pltpu.VMEM((chunks, STATE, CHUNK), BF16),
            pltpu.VMEM((chunks, STATE, CHUNK), BF16),
            pltpu.VMEM((chunks, share, CHUNK), BF16),
            pltpu.VMEM((chunks, spans - 1, STATE, CHUNK), BF16),
            pltpu.VMEM((rows, 3 * heads), BF16),
            pltpu.VMEM((heads, rows), F32),
            pltpu.VMEM((rows, 2 * heads), BF16),
            pltpu.VMEM((rows, 2 * heads), BF16),
            pltpu.VMEM((16, heads), F32),
            pltpu.VMEM((groups, STATE, rows), BF16),
            pltpu.VMEM((groups, rows, STATE), BF16),
            pltpu.VMEM((rows * lines, 128), F32),
            pltpu.VMEM((CHUNK // 128, HALO + rows, 128), F32),
            pltpu.VMEM((chunks, 3 * heads, CHUNK), BF16),
            pltpu.VMEM((chunks, 16, CHUNK), F32),
            pltpu.VMEM((EDGE, channels), BF16),
            pltpu.VMEM((EDGE_TOKENS * lines, 128), BF16),
            pltpu.SemaphoreType.DMA((chunks,)),
            pltpu.SemaphoreType.DMA((chunks,)),
            pltpu.SemaphoreType.DMA((n - 1, chunks)),
            pltpu.SemaphoreType.DMA((chunks,)),
            pltpu.SemaphoreType.DMA((2,)),
            pltpu.SemaphoreType.DMA((2,)),
        ],
        compiler_params=pltpu.CompilerParams(
            dimension_semantics=("arbitrary",),
            vmem_limit_bytes=56 << 20,
            collective_id=0,
            has_side_effects=True,
        ),
        cost_estimate=pl.CostEstimate(
            flops=20 * rows * channels * STATE, bytes_accessed=4 * rows * channels, transcendentals=4 * rows * channels
        ),
    )(x, taps, bias, bc, taps_bc, bias_bc, dt, dt_bias, a_log, skip, z, gain, x, bc)


def per_device(
    x_in,
    bc_in,
    z_in,
    dt_raw,
    conv_x,
    conv_bc,
    conv_bias_x,
    conv_bias_bc,
    dt_bias,
    a_log,
    d_skip,
    norm_gain,
):
    rows, channels = x_in.shape
    heads = dt_raw.shape[1]
    n = lax.axis_size("ctx")
    tiles = bc_in.shape[2] // 128
    groups = bc_in.shape[2] // STATE

    def lined(v):
        return v.reshape(-1, 2, tiles, 128).transpose(0, 2, 1, 3).reshape(-1, 128)

    gated, final = scan(
        n,
        x_in,
        conv_x,
        conv_bias_x[None],
        lined(bc_in),
        lined(conv_bc),
        lined(conv_bias_bc),
        dt_raw.T,
        dt_bias[None],
        a_log[None],
        d_skip[None],
        z_in,
        norm_gain[None],
        groups,
    )
    return tuple(finish(gated, norm_gain[None], final, groups))


def solution(mesh):
    in_specs = (
        P(("group", "ctx"), "tp"),
        P(("group", "ctx"), None, "tp"),
        P(("group", "ctx"), "tp"),
        P(("group", "ctx"), "tp"),
        P(None, "tp"),
        P(None, None, "tp"),
        P("tp"),
        P(None, "tp"),
        P("tp"),
        P("tp"),
        P("tp"),
        P("tp"),
    )
    out_specs = (P(("group", "ctx"), "tp"), P(("group", "tp"), None, "ctx"))
    return jax.shard_map(
        per_device, mesh=mesh, in_specs=in_specs, out_specs=out_specs, check_vma=False
    )
```

```python
import functools
import math

import jax
import jax.numpy as jnp
from jax import lax
from jax.experimental import pallas as pl
from jax.experimental.pallas import tpu as pltpu
from jax.sharding import PartitionSpec as P

HEAD_DIM = 64
STATE = 256
SPAN = 128
CHUNK = 512
HEADS_CHUNK = CHUNK // HEAD_DIM
HALO = 8
LOG2E = math.log2(math.e)

eps = 1e-05
F32 = jnp.float32
BF16 = jnp.bfloat16


def silu(v):
    half = 0.5 * v
    return half * jnp.tanh(half) + half


def dot(a, b):
    return jnp.dot(a, b, preferred_element_type=F32)


def rescaled(gated, gain):
    gated = gated.astype(F32)
    meansq = jnp.mean(gated * gated, axis=-1, keepdims=True)
    return (gated * lax.rsqrt(meansq + eps) * gain).astype(BF16)


def finish_kernel(groups, gated_ref, gain_ref, final_ref, out_any, state_any, last, turned, sems):
    rows, channels = gated_ref.shape
    width = channels // groups
    done = channels - width
    blocks = rows // SPAN
    copies = []
    for g in range(groups - 1):
        lanes = pl.ds(g * width, width)
        copies.append(
            pltpu.make_async_copy(gated_ref.at[:, lanes], out_any.at[:, lanes], sems.at[g])
        )
        copies[-1].start()
    for b in range(blocks):
        at = slice(b * SPAN, (b + 1) * SPAN)
        last[at] = rescaled(gated_ref[at, done:], gain_ref[:, done:])
        copies.append(
            pltpu.make_async_copy(
                last.at[pl.ds(b * SPAN, SPAN)],
                out_any.at[pl.ds(b * SPAN, SPAN), pl.ds(done, width)],
                sems.at[groups - 1 + b],
            )
        )
        copies[-1].start()
    part = CHUNK // HEAD_DIM
    for c in range(channels // CHUNK):
        block = final_ref[:, c * CHUNK : (c + 1) * CHUNK].astype(F32).T
        turned[c * part : (c + 1) * part] = block.reshape(part, HEAD_DIM, block.shape[1])
    copies.append(pltpu.make_async_copy(turned, state_any, sems.at[groups - 1 + blocks]))
    copies[-1].start()
    for copy in copies:
        copy.wait()


def finish(gated, gain, final, groups):
    rows, channels = gated.shape
    share = final.shape[0]
    heads = channels // HEAD_DIM
    whole = pl.BlockSpec(memory_space=pltpu.VMEM)
    away = pl.BlockSpec(memory_space=pl.ANY)
    return pl.pallas_call(
        functools.partial(finish_kernel, groups),
        in_specs=[whole, whole, whole],
        out_specs=[away, away],
        out_shape=[
            jax.ShapeDtypeStruct((rows, channels), BF16),
            jax.ShapeDtypeStruct((heads, HEAD_DIM, share), F32),
        ],
        scratch_shapes=[
            pltpu.VMEM((rows, channels // groups), BF16),
            pltpu.VMEM((heads, HEAD_DIM, share), F32),
            pltpu.SemaphoreType.DMA((groups + rows // SPAN,)),
        ],
        compiler_params=pltpu.CompilerParams(vmem_limit_bytes=16 << 20),
        cost_estimate=pl.CostEstimate(
            flops=4 * rows * channels, bytes_accessed=4 * rows * channels, transcendentals=rows
        ),
    )(gated, gain, final)


EDGE = 16
EDGE_TOKENS = 4
BLOCK = 32
HALF = SPAN // 2
MESH = pl.DeviceIdType.MESH


def leading(n, chunks):
    return chunks + max(0, n - 4)


def exact_dot(a, b):
    return jnp.dot(a, b, preferred_element_type=F32, precision=lax.Precision.HIGHEST)


def split(v, parts):
    out = []
    for _ in range(parts):
        piece = v.astype(BF16)
        out.append(piece.astype(F32))
        v = v - out[-1]
    return jnp.concatenate(out, axis=1).astype(BF16)


def scan_kernel(
    n,
    x_ref,
    taps_ref,
    bias_ref,
    bc_ref,
    taps_bc_ref,
    bias_bc_ref,
    dt_ref,
    dt_bias_ref,
    a_log_ref,
    skip_ref,
    z_ref,
    gain_ref,
    x_any,
    bc_any,
    y_ref,
    final_out,
    xc,
    sent,
    came,
    piece,
    local,
    cumul_ref,
    row_ref,
    turn_ref,
    tail_ref,
    fade_ref,
    bt_ref,
    c_ref,
    near_ref,
    far_ref,
    kept,
    acc_ref,
    lift_ref,
    spread_ref,
    wide_ref,
    edge_x,
    edge_bc,
    send_sem,
    recv_sem,
    piece_send,
    piece_recv,
    edge_send,
    edge_recv,
):
    s = pl.program_id(0)
    chunks = sent.shape[0]
    lead = leading(n, chunks)
    last_step = lead + chunks - 1
    me = lax.axis_index("ctx")
    rows = x_ref.shape[0]
    spans = rows // SPAN
    heads = dt_ref.shape[0]
    groups = bt_ref.shape[0]
    per = chunks // groups
    lines = bc_ref.shape[0] // rows
    tile = max(lines, 8)
    share = STATE // n
    right = jnp.minimum(me + 1, n - 1)

    def edge_copies():
        return [
            pltpu.make_async_remote_copy(
                src_ref=whole.at[pl.ds(whole.shape[0] - edge.shape[0], edge.shape[0])],
                dst_ref=edge,
                send_sem=edge_send.at[i],
                recv_sem=edge_recv.at[i],
                device_id={"ctx": right},
                device_id_type=MESH,
            )
            for i, (whole, edge) in enumerate(((bc_any, edge_bc), (x_any, edge_x)))
        ]

    def onward(c):
        return pltpu.make_async_remote_copy(
            src_ref=sent.at[c],
            dst_ref=came.at[c],
            send_sem=send_sem.at[c],
            recv_sem=recv_sem.at[c],
            device_id={"ctx": right},
            device_id_type=MESH,
        )

    def handed(q, c):
        return pltpu.make_async_remote_copy(
            src_ref=sent.at[c, pl.ds(pl.multiple_of(q * share, share), share)],
            dst_ref=piece.at[c],
            send_sem=piece_send.at[q, c],
            recv_sem=piece_recv.at[c],
            device_id={"ctx": q},
            device_id_type=MESH,
        )

    def spread_of(c):
        shape = (3 * heads, CHUNK)
        return (
            lax.broadcasted_iota(jnp.int32, shape, 1) // HEAD_DIM + c * HEADS_CHUNK
            == lax.broadcasted_iota(jnp.int32, shape, 0) % heads
        ).astype(BF16)

    def bc_block(b):
        size = BLOCK * lines
        reach = EDGE_TOKENS * lines
        here = bc_ref[b * size : (b + 1) * size].astype(F32)
        before = edge_bc[...] if b == 0 else bc_ref[b * size - reach : b * size]
        window = jnp.concatenate([before.astype(F32), here], axis=0)
        taps_all = taps_bc_ref[...].astype(F32)
        lag = taps_all.shape[0] // lines - 1
        bias = bias_bc_ref[...]
        acc = jnp.concatenate([bias] * (tile // lines), axis=0)[None]
        for k in range(lag + 1):
            taps = taps_all[k * lines : (k + 1) * lines]
            taps = jnp.concatenate([taps] * (tile // lines), axis=0)
            first = (EDGE_TOKENS - lag + k) * lines
            acc = acc + window[first : first + size].reshape(size // tile, tile, 128) * taps[None]
        acc_ref[b * size : (b + 1) * size] = acc.reshape(size, 128)

    def project(side, g):
        for k in range(spans):
            at = slice(k * SPAN, (k + 1) * SPAN)
            for half in range(STATE // 128):
                line = 2 * (g * (STATE // 128) + half) + side
                own = slice(half * 128, (half + 1) * 128)
                v = silu(acc_ref[pl.ds(k * SPAN * lines + line, SPAN, stride=lines), :])
                if side == 0:
                    bt_ref[g, own, at] = v.astype(BF16).astype(F32).T.astype(BF16)
                else:
                    c_ref[g, at, own] = v.astype(BF16)

    @pl.when(s == 0)
    def _():
        barrier = pltpu.get_barrier_semaphore()
        for k in range(1, n):
            pl.semaphore_signal(
                barrier, inc=1, device_id={"ctx": lax.rem(me + k, n)}, device_id_type=MESH
            )
        rate = -LOG2E * jnp.exp(a_log_ref[...])
        above = lax.broadcasted_iota(jnp.int32, (SPAN, SPAN), 0)
        left = lax.broadcasted_iota(jnp.int32, (SPAN, SPAN), 1)
        lower = ((above >= left) & (above // HALF == left // HALF)).astype(F32)
        so_far = jnp.zeros((1, heads), F32)
        fade_ref[...] = jnp.zeros_like(fade_ref)
        for k in range(spans):
            at = slice(k * SPAN, (k + 1) * SPAN)
            v = dt_ref[:, at].T + dt_bias_ref[...]
            step = jnp.maximum(v, 0.0) + jnp.log1p(jnp.exp(-jnp.abs(v)))
            cumul = exact_dot(lower, step * rate)
            ends = cumul[HALF - 1 : HALF], cumul[SPAN - 1 :]
            tail = jnp.concatenate(
                [end - cumul[i * HALF : (i + 1) * HALF] for i, end in enumerate(ends)], axis=0
            )
            cumul_ref[at] = split(cumul, 3)
            tail_ref[at] = split(jnp.exp2(tail) * step, 2)
            rowed = cumul - jnp.log2(step)
            wide = jnp.concatenate([rowed] * (128 // heads), axis=1) if heads < 128 else rowed
            turn_ref[...] = wide.T[:heads]
            even = turn_ref[pl.ds(0, heads // 2, stride=2), :]
            odd = turn_ref[pl.ds(1, heads // 2, stride=2), :]
            for i in range(2):
                own = slice(i * HALF, (i + 1) * HALF)
                pairs_row = jnp.concatenate([even[:, own], odd[:, own]], axis=1)
                for c in range(chunks):
                    row_ref[c, :, (2 * k + i) * SPAN : (2 * k + i + 1) * SPAN] = pairs_row[
                        c * (HEADS_CHUNK // 2) : (c + 1) * (HEADS_CHUNK // 2)
                    ]
                fade_ref[2 * k + i : 2 * k + i + 1] = jnp.exp2(ends[i])
            fade_ref[2 * spans + 2 + k : 2 * spans + 3 + k] = jnp.exp2(so_far)
            so_far = so_far + ends[0] + ends[1]
        fade_ref[2 * spans : 2 * spans + 1] = jnp.exp2(so_far)
        fade_ref[2 * spans + 1 : 2 * spans + 2] = skip_ref[...]

        pl.semaphore_wait(barrier, n - 1)

        @pl.when(me < n - 1)
        def _():
            for copy in edge_copies():
                copy.start()

        for b in range(1, rows // BLOCK):
            bc_block(b)

        @pl.when(me == 0)
        def _():
            edge_x[...] = jnp.zeros_like(edge_x)
            edge_bc[...] = jnp.zeros_like(edge_bc)
            came[...] = jnp.zeros_like(came)

        @pl.when(me > 0)
        def _():
            for copy in edge_copies():
                copy.wait_recv()

        bc_block(0)
        project(0, 0)

    def join(c, carry):
        onward(c).wait_recv()
        got = came[c]
        fades = wide_ref[c]
        mine = sent[c].astype(F32)
        sent[c] = (fades[2 * spans : 2 * spans + 1] * got.astype(F32) + mine).astype(BF16)

        @pl.when(me < n - 1)
        def _():
            onward(c).start()

        @pl.when(me == n - 1)
        def _():
            lax.fori_loop(0, n - 1, lambda q, z: (handed(q, c).start(), z)[1], 0)

        return carry

    base = jnp.where(me == 1, 1, jnp.minimum(lead, chunks + me - 2))
    first = jnp.clip(s - base, 0, chunks)
    stop = jnp.where(s == last_step, chunks, jnp.clip(s - base + 1, 0, chunks))
    stop = jnp.where(me == 0, first, stop)
    lax.fori_loop(first, stop, join, 0)

    pairs = HEADS_CHUNK // 2

    def pair_lanes(pair):
        return slice(pair * 2 * HEAD_DIM, (pair + 1) * 2 * HEAD_DIM)

    @pl.when(s < chunks)
    def _():
        j = s
        bt = bt_ref.at[j // per]
        taps = 0.5 * taps_ref[...].astype(F32)
        bias = 0.5 * bias_ref[...]
        lag = taps.shape[0] - 1
        before = edge_x[:, pl.ds(pl.multiple_of(j * CHUNK, CHUNK), CHUNK)].astype(F32)[EDGE - HALO :]
        spread = spread_of(j)
        spread_ref[j] = spread
        fades = dot(split(fade_ref[...], 3), spread)
        wide_ref[j] = fades
        tiles = [slice(i * 128, (i + 1) * 128) for i in range(CHUNK // 128)]
        for i, lanes in enumerate(tiles):
            lift_ref[i, :HALO] = before[:, lanes]
            lift_ref[i, HALO:] = x_ref[:, lanes].astype(F32)
        state = None
        for k in range(spans):
            at = slice(k * SPAN, (k + 1) * SPAN)
            tail = dot(tail_ref[at], spread[: 2 * heads])
            parts = []
            for i, lanes in enumerate(tiles):
                column = []
                for r in range(0, SPAN, HALF):
                    first = k * SPAN + r
                    half = bias[:, lanes]
                    for q in range(lag + 1):
                        begin = HALO - lag + q + first
                        half = half + lift_ref[i, begin : begin + HALF] * taps[q : q + 1, lanes]
                    value = half * jnp.tanh(half) + half
                    xc[j, first : first + HALF, lanes] = value.astype(BF16)
                    column.append(value * tail[r : r + HALF, lanes])
                parts.append(column)
            scaled = jnp.concatenate([column[1] for column in parts], axis=1).astype(BF16)
            first = jnp.concatenate([column[0] for column in parts], axis=1)
            kept[j, k] = first.astype(BF16)
            first = (first * fades[2 * k + 1 : 2 * k + 2]).astype(BF16)
            scaled = jnp.concatenate([first, scaled], axis=0)
            part = dot(bt[:, at], scaled)
            state = part if state is None else fades[2 * k : 2 * k + 1] * fades[2 * k + 1 : 2 * k + 2] * state + part
            if k < spans - 1:
                local[j, k] = state.astype(BF16)
        sent[j] = state.astype(BF16)

        @pl.when(me == 0)
        def _():
            onward(j).start()

    @pl.when(s == 0)
    def _():
        causal = lax.broadcasted_iota(jnp.int32, (HALF, SPAN), 0) >= (
            lax.broadcasted_iota(jnp.int32, (HALF, SPAN), 1) % HALF
        )
        for g in range(groups):
            if g > 0:
                project(0, g)
            project(1, g)
            for k in range(spans):
                at = slice(k * SPAN, (k + 1) * SPAN)
                scores = dot(c_ref[g, at], bt_ref[g, :, at])
                for i in range(2):
                    own = slice(i * HALF, (i + 1) * HALF)
                    near = jnp.concatenate([scores[own, own]] * 2, axis=1)
                    near_ref[g, k * SPAN + i * HALF : k * SPAN + (i + 1) * HALF] = jnp.where(
                        causal, near, 0.0
                    )
                far_ref[g, k * HALF : (k + 1) * HALF] = scores[HALF:, :HALF].astype(BF16)

    @pl.when(s >= lead)
    def _():
        j = s - lead
        fades = wide_ref[j]
        spread = spread_ref[j]
        g = j // per
        none = jnp.zeros((), BF16)
        low = lax.broadcasted_iota(jnp.int32, (HALF, 2 * HEAD_DIM), 1) < HEAD_DIM

        def row_of(i):
            return jnp.broadcast_to(fades[i : i + 1], (16, CHUNK)).astype(BF16)[None]

        def by_row(block, i):
            return (block.reshape(STATE // 16, 16, CHUNK) * row_of(i)).reshape(STATE, CHUNK)

        for k in range(spans):
            at = slice(k * SPAN, (k + 1) * SPAN)
            cumul = dot(cumul_ref[at], spread)
            state = came[j]
            if k > 0:
                state = local[j, k - 1] + by_row(state, 2 * spans + 2 + k)
            for i in range(2):
                mine = slice(i * HALF, (i + 1) * HALF)
                there = slice(k * SPAN + i * HALF, k * SPAN + (i + 1) * HALF)
                c_half = c_ref[g, there]
                if i == 0:
                    readout = dot(c_half, state)
                else:
                    readout = dot(c_half, by_row(state, 2 * k)) + dot(
                        far_ref[g, k * HALF : (k + 1) * HALF], kept[j, k]
                    )
                near = near_ref[g, there]
                for pair in range(pairs):
                    lanes = pair_lanes(pair)
                    away = cumul[mine, lanes]
                    spacing = away - row_ref[
                        j, pair : pair + 1, (2 * k + i) * SPAN : (2 * k + i + 1) * SPAN
                    ]
                    weights = (jnp.exp2(jnp.minimum(spacing, 64.0)) * near).astype(BF16)
                    x_pair = xc[j, there, lanes]
                    stacked = jnp.concatenate(
                        [jnp.where(low, x_pair, none), jnp.where(low, none, x_pair)], axis=0
                    )
                    out = (
                        dot(weights, stacked)
                        + x_pair.astype(F32) * fades[2 * spans + 1 : 2 * spans + 2, lanes]
                        + jnp.exp2(away) * readout[:, lanes]
                    )
                    half = (0.5 * z_ref[there, lanes]).astype(F32)
                    gate = half * jnp.tanh(half) + half
                    own = pl.ds(pl.multiple_of(j * CHUNK + pair * 2 * HEAD_DIM, 128), 2 * HEAD_DIM)
                    y_ref[there, own] = (out * gate).astype(BF16)

    for g in range(groups - 1):

        @pl.when(s == lead + (g + 1) * per - 1)
        def _(g=g):
            own = slice(g * per * CHUNK, (g + 1) * per * CHUNK)
            for k in range(0, rows, BLOCK):
                y_ref[k : k + BLOCK, own] = rescaled(y_ref[k : k + BLOCK, own], gain_ref[:, own])

    @pl.when(s == last_step)
    def _():
        @pl.when(me < n - 1)
        def _():
            for copy in edge_copies():
                copy.wait_send()
            for c in range(chunks):
                onward(c).wait_send()
            for c in range(chunks):
                handed(0, c).wait_recv()
                final_out[:, c * CHUNK : (c + 1) * CHUNK] = piece[c]

        @pl.when(me == n - 1)
        def _():
            for c in range(chunks):
                lax.fori_loop(0, n - 1, lambda q, z: (handed(q, c).wait_send(), z)[1], 0)
                final_out[:, c * CHUNK : (c + 1) * CHUNK] = sent[c, (n - 1) * share :]


def scan(n, x, taps, bias, bc, taps_bc, bias_bc, dt, dt_bias, a_log, skip, z, gain, groups):
    rows, channels = x.shape
    chunks = channels // CHUNK
    heads = dt.shape[0]
    lead = leading(n, chunks)
    lines = bc.shape[0] // rows
    fade_rows = -(-(3 * (rows // SPAN) + 2) // 8) * 8
    share = STATE // n
    spans = rows // SPAN
    turn = lambda s: (0, jnp.minimum(s, chunks - 1))
    later = lambda s: (0, jnp.maximum(s - lead, 0))
    still = lambda s: (0, 0)
    return pl.pallas_call(
        functools.partial(scan_kernel, n),
        grid=(lead + chunks,),
        in_specs=[
            pl.BlockSpec((rows, CHUNK), turn),
            pl.BlockSpec((taps.shape[0], CHUNK), turn),
            pl.BlockSpec((1, CHUNK), turn),
            pl.BlockSpec(bc.shape, still),
            pl.BlockSpec(taps_bc.shape, still),
            pl.BlockSpec(bias_bc.shape, still),
            pl.BlockSpec((heads, rows), still),
            pl.BlockSpec((1, heads), still),
            pl.BlockSpec((1, heads), still),
            pl.BlockSpec((1, heads), still),
            pl.BlockSpec((rows, CHUNK), later),
            pl.BlockSpec((1, channels), still),
            pl.BlockSpec(memory_space=pl.ANY),
            pl.BlockSpec(memory_space=pl.ANY),
        ],
        out_specs=[
            pl.BlockSpec(memory_space=pltpu.VMEM),
            pl.BlockSpec(memory_space=pltpu.VMEM),
        ],
        out_shape=[
            pltpu.VMEM((rows, channels), BF16),
            pltpu.VMEM((share, channels), BF16),
        ],
        scratch_shapes=[
            pltpu.VMEM((chunks, rows, CHUNK), BF16),
            pltpu.VMEM((chunks, STATE, CHUNK), BF16),
            pltpu.VMEM((chunks, STATE, CHUNK), BF16),
            pltpu.VMEM((chunks, share, CHUNK), BF16),
            pltpu.VMEM((chunks, spans - 1, STATE, CHUNK), BF16),
            pltpu.VMEM((rows, 3 * heads), BF16),
            pltpu.VMEM((chunks, HEADS_CHUNK // 2, 2 * rows), F32),
            pltpu.VMEM((heads, SPAN), F32),
            pltpu.VMEM((rows, 2 * heads), BF16),
            pltpu.VMEM((fade_rows, heads), F32),
            pltpu.VMEM((groups, STATE, rows), BF16),
            pltpu.VMEM((groups, rows, STATE), BF16),
            pltpu.VMEM((groups, rows, SPAN), F32),
            pltpu.VMEM((groups, rows // 2, HALF), BF16),
            pltpu.VMEM((chunks, spans, HALF, CHUNK), BF16),
            pltpu.VMEM((rows * lines, 128), F32),
            pltpu.VMEM((CHUNK // 128, HALO + rows, 128), F32),
            pltpu.VMEM((chunks, 3 * heads, CHUNK), BF16),
            pltpu.VMEM((chunks, fade_rows, CHUNK), F32),
            pltpu.VMEM((EDGE, channels), BF16),
            pltpu.VMEM((EDGE_TOKENS * lines, 128), BF16),
            pltpu.SemaphoreType.DMA((chunks,)),
            pltpu.SemaphoreType.DMA((chunks,)),
            pltpu.SemaphoreType.DMA((n - 1, chunks)),
            pltpu.SemaphoreType.DMA((chunks,)),
            pltpu.SemaphoreType.DMA((2,)),
            pltpu.SemaphoreType.DMA((2,)),
        ],
        compiler_params=pltpu.CompilerParams(
            dimension_semantics=("arbitrary",),
            vmem_limit_bytes=56 << 20,
            collective_id=0,
            has_side_effects=True,
        ),
        cost_estimate=pl.CostEstimate(
            flops=20 * rows * channels * STATE, bytes_accessed=4 * rows * channels, transcendentals=4 * rows * channels
        ),
    )(x, taps, bias, bc, taps_bc, bias_bc, dt, dt_bias, a_log, skip, z, gain, x, bc)


def per_device(
    x_in,
    bc_in,
    z_in,
    dt_raw,
    conv_x,
    conv_bc,
    conv_bias_x,
    conv_bias_bc,
    dt_bias,
    a_log,
    d_skip,
    norm_gain,
):
    rows, channels = x_in.shape
    heads = dt_raw.shape[1]
    n = lax.axis_size("ctx")
    tiles = bc_in.shape[2] // 128
    groups = bc_in.shape[2] // STATE

    def lined(v):
        return v.reshape(-1, 2, tiles, 128).transpose(0, 2, 1, 3).reshape(-1, 128)

    gated, final = scan(
        n,
        x_in,
        conv_x,
        conv_bias_x[None],
        lined(bc_in),
        lined(conv_bc),
        lined(conv_bias_bc),
        dt_raw.T,
        dt_bias[None],
        a_log[None],
        d_skip[None],
        z_in,
        norm_gain[None],
        groups,
    )
    return tuple(finish(gated, norm_gain[None], final, groups))


def solution(mesh):
    in_specs = (
        P(("group", "ctx"), "tp"),
        P(("group", "ctx"), None, "tp"),
        P(("group", "ctx"), "tp"),
        P(("group", "ctx"), "tp"),
        P(None, "tp"),
        P(None, None, "tp"),
        P("tp"),
        P(None, "tp"),
        P("tp"),
        P("tp"),
        P("tp"),
        P("tp"),
    )
    out_specs = (P(("group", "ctx"), "tp"), P(("group", "tp"), None, "ctx"))
    return jax.shard_map(
        per_device, mesh=mesh, in_specs=in_specs, out_specs=out_specs, check_vma=False
    )
```

```python
import functools
import math

import jax
import jax.numpy as jnp
from jax import lax
from jax.experimental import pallas as pl
from jax.experimental.pallas import tpu as pltpu
from jax.sharding import PartitionSpec as P

HEAD_DIM = 64
STATE = 256
SPAN = 128
CHUNK = 512
HEADS_CHUNK = CHUNK // HEAD_DIM
HALO = 8
LOG2E = math.log2(math.e)

eps = 1e-05
F32 = jnp.float32
BF16 = jnp.bfloat16


def dot(a, b):
    return jnp.dot(a, b, preferred_element_type=F32)


def rescaled(gated, gain):
    gated = gated.astype(F32)
    meansq = jnp.mean(gated * gated, axis=-1, keepdims=True)
    return (gated * lax.rsqrt(meansq + eps) * gain).astype(BF16)


def finish_kernel(groups, gated_ref, gain_ref, final_ref, out_any, state_any, mixed, turned, sems):
    rows, channels = gated_ref.shape
    width = channels // groups
    blocks = rows // SPAN
    part = CHUNK // HEAD_DIM
    for c in range(channels // CHUNK):
        block = final_ref[:, c * CHUNK : (c + 1) * CHUNK].astype(F32).T
        turned[c * part : (c + 1) * part] = block.reshape(part, HEAD_DIM, block.shape[1])
    copies = [pltpu.make_async_copy(turned, state_any, sems.at[blocks])]
    copies[-1].start()
    for b in range(blocks):
        at = slice(b * SPAN, (b + 1) * SPAN)
        for g in range(groups):
            own = slice(g * width, (g + 1) * width)
            mixed[at, own] = rescaled(gated_ref[at, own], gain_ref[:, own])
        there = pl.ds(b * SPAN, SPAN)
        copies.append(pltpu.make_async_copy(mixed.at[there], out_any.at[there], sems.at[b]))
        copies[-1].start()
    for copy in copies:
        copy.wait()


def finish(gated, gain, final, groups):
    rows, channels = gated.shape
    share = final.shape[0]
    heads = channels // HEAD_DIM
    whole = pl.BlockSpec(memory_space=pltpu.VMEM)
    away = pl.BlockSpec(memory_space=pl.ANY)
    return pl.pallas_call(
        functools.partial(finish_kernel, groups),
        in_specs=[whole, whole, whole],
        out_specs=[away, away],
        out_shape=[
            jax.ShapeDtypeStruct((rows, channels), BF16),
            jax.ShapeDtypeStruct((heads, HEAD_DIM, share), F32),
        ],
        scratch_shapes=[
            pltpu.VMEM((rows, channels), BF16),
            pltpu.VMEM((heads, HEAD_DIM, share), F32),
            pltpu.SemaphoreType.DMA((1 + rows // SPAN,)),
        ],
        compiler_params=pltpu.CompilerParams(vmem_limit_bytes=16 << 20),
        cost_estimate=pl.CostEstimate(
            flops=4 * rows * channels, bytes_accessed=4 * rows * channels, transcendentals=rows
        ),
    )(gated, gain, final)


EDGE = 16
EDGE_TOKENS = 4
BLOCK = 32
HALF = SPAN // 2
MESH = pl.DeviceIdType.MESH


def leading(n, chunks):
    return chunks + max(0, n - 4)


def exact_dot(a, b):
    return jnp.dot(a, b, preferred_element_type=F32, precision=lax.Precision.HIGHEST)


def split(v, parts):
    out = []
    for _ in range(parts):
        piece = v.astype(BF16)
        out.append(piece.astype(F32))
        v = v - out[-1]
    return jnp.concatenate(out, axis=1).astype(BF16)


def scan_kernel(
    n,
    x_ref,
    taps_ref,
    bias_ref,
    bc_ref,
    taps_bc_ref,
    bias_bc_ref,
    dt_ref,
    dt_bias_ref,
    a_log_ref,
    skip_ref,
    z_ref,
    x_any,
    bc_any,
    y_ref,
    final_out,
    xc,
    sent,
    merged,
    came,
    later_out,
    later_in,
    fade_out,
    fade_in,
    local,
    exact_ref,
    rowed_ref,
    cumul_ref,
    row_ref,
    turn_ref,
    tail_ref,
    fade_ref,
    bt_ref,
    c_ref,
    near_ref,
    far_ref,
    kept,
    even,
    mid_ref,
    inside,
    outside,
    raw_ref,
    lift_ref,
    spread_ref,
    wide_ref,
    edge_x,
    edge_bc,
    send_sem,
    recv_sem,
    later_send,
    later_recv,
    fade_send,
    fade_recv,
    edge_send,
    edge_recv,
):
    s = pl.program_id(0)
    chunks = sent.shape[0]
    lead = leading(n, chunks)
    last_step = lead + chunks - 1
    me = lax.axis_index("ctx")
    rows = x_ref.shape[0]
    spans = rows // SPAN
    heads = dt_ref.shape[0]
    groups = bt_ref.shape[0]
    per = chunks // groups
    lines = bc_ref.shape[0] // rows
    reach = EDGE_TOKENS * lines
    share = STATE // n
    right = jnp.minimum(me + 1, n - 1)
    left = jnp.maximum(me - 1, 0)
    total = 2 * spans

    def edge_copies():
        return [
            pltpu.make_async_remote_copy(
                src_ref=whole.at[pl.ds(whole.shape[0] - edge.shape[0], edge.shape[0])],
                dst_ref=edge,
                send_sem=edge_send.at[i],
                recv_sem=edge_recv.at[i],
                device_id={"ctx": right},
                device_id_type=MESH,
            )
            for i, (whole, edge) in enumerate(((bc_any, edge_bc), (x_any, edge_x)))
        ]

    def onward(c):
        return pltpu.make_async_remote_copy(
            src_ref=merged.at[c],
            dst_ref=came.at[c],
            send_sem=send_sem.at[c],
            recv_sem=recv_sem.at[c],
            device_id={"ctx": right},
            device_id_type=MESH,
        )

    def rows_of(q):
        return pl.ds(pl.multiple_of(q * share, share), share)

    def behind(q, c):
        return pltpu.make_async_remote_copy(
            src_ref=later_out.at[c, rows_of(q)],
            dst_ref=later_in.at[c, rows_of(q)],
            send_sem=later_send.at[q, c],
            recv_sem=later_recv.at[q, c],
            device_id={"ctx": left},
            device_id_type=MESH,
        )

    def fading(c):
        return pltpu.make_async_remote_copy(
            src_ref=fade_out.at[c],
            dst_ref=fade_in.at[c],
            send_sem=fade_send.at[c],
            recv_sem=fade_recv.at[c],
            device_id={"ctx": left},
            device_id_type=MESH,
        )

    def spread_of(c):
        shape = (3 * heads, CHUNK)
        return (
            lax.broadcasted_iota(jnp.int32, shape, 1) // HEAD_DIM + c * HEADS_CHUNK
            == lax.broadcasted_iota(jnp.int32, shape, 0) % heads
        ).astype(BF16)

    def project(side, g):
        taps = 0.5 * taps_bc_ref[...].astype(F32)
        bias = 0.5 * bias_bc_ref[...]
        lag = taps.shape[0] // lines - 1
        for k in range(spans):
            at = slice(k * SPAN, (k + 1) * SPAN)
            for i in range(STATE // 128):
                line = 2 * (g * (STATE // 128) + i) + side
                own = slice(i * 128, (i + 1) * 128)
                half = bias[line : line + 1]
                for q in range(lag + 1):
                    begin = (k * SPAN + EDGE_TOKENS - lag + q) * lines + line
                    tap = taps[q * lines + line : q * lines + line + 1]
                    half = half + raw_ref[pl.ds(begin, SPAN, stride=lines), :] * tap
                v = half * jnp.tanh(half) + half
                if side == 0:
                    bt_ref[g, own, at] = v.astype(BF16).astype(F32).T.astype(BF16)
                else:
                    c_ref[g, at, own] = v.astype(BF16)

    @pl.when(s == 0)
    def _():
        barrier = pltpu.get_barrier_semaphore()
        for k in range(1, n):
            pl.semaphore_signal(
                barrier, inc=1, device_id={"ctx": lax.rem(me + k, n)}, device_id_type=MESH
            )
        rate = -LOG2E * jnp.exp(a_log_ref[...])
        above = lax.broadcasted_iota(jnp.int32, (SPAN, SPAN), 0)
        left = lax.broadcasted_iota(jnp.int32, (SPAN, SPAN), 1)
        lower = ((above >= left) & (above // HALF == left // HALF)).astype(F32)
        so_far = jnp.zeros((1, heads), F32)
        fade_ref[...] = jnp.zeros_like(fade_ref)
        for k in range(spans):
            at = slice(k * SPAN, (k + 1) * SPAN)
            v = dt_ref[:, at].T + dt_bias_ref[...]
            step = jnp.maximum(v, 0.0) + jnp.log1p(jnp.exp(-jnp.abs(v)))
            cumul = exact_dot(lower, step * rate)
            ends = cumul[HALF - 1 : HALF], cumul[SPAN - 1 :]
            tail = jnp.concatenate(
                [end - cumul[i * HALF : (i + 1) * HALF] for i, end in enumerate(ends)], axis=0
            )
            exact_ref[at] = cumul
            rowed_ref[at] = cumul - jnp.log2(step)
            tail_ref[at] = split(jnp.exp2(tail) * step, 2)
            for i in range(2):
                part = 2 * k + i
                fade_ref[part : part + 1] = jnp.exp2(ends[i])
                fade_ref[total + 2 + part : total + 3 + part] = jnp.exp2(so_far)
                so_far = so_far + ends[i]
        fade_ref[2 * spans : 2 * spans + 1] = jnp.exp2(so_far)
        fade_ref[2 * spans + 1 : 2 * spans + 2] = skip_ref[...]
        raw_ref[reach:] = bc_ref[...].astype(F32)

        pl.semaphore_wait(barrier, n - 1)

        @pl.when(me < n - 1)
        def _():
            for copy in edge_copies():
                copy.start()

        @pl.when(me == 0)
        def _():
            edge_x[...] = jnp.zeros_like(edge_x)
            edge_bc[...] = jnp.zeros_like(edge_bc)

        @pl.when(me > 0)
        def _():
            for copy in edge_copies():
                copy.wait_recv()

        raw_ref[:reach] = edge_bc[...].astype(F32)
        project(0, 0)

    def join(c, carry):
        onward(c).wait_recv()
        got = came[c].astype(F32)
        merged[c] = (wide_ref[c, total : total + 1] * got + sent[c].astype(F32)).astype(BF16)

        @pl.when(me < n - 1)
        def _():
            onward(c).start()

        return carry

    def turn_back(c, carry):
        lax.fori_loop(0, me + 1, lambda q, z: (behind(q, c).wait_recv(), z)[1], 0)
        fading(c).wait_recv()

        def add(q, z):
            mine = sent[c, rows_of(q)].astype(F32)
            after = later_in[c, rows_of(q)].astype(F32)
            later_out[c, rows_of(q)] = (fade_in[c, :1] * mine + after).astype(BF16)
            behind(q, c).start()
            return z

        lax.fori_loop(0, me, add, 0)

        @pl.when(me > 0)
        def _():
            fade_out[c] = fade_in[c] * wide_ref[c, total : total + 1]
            fading(c).start()

        return carry

    def close(c, carry):
        there = pl.ds(pl.multiple_of(c * CHUNK, CHUNK), CHUNK)

        @pl.when(me < n - 1)
        def _():
            mine = merged[c, rows_of(me)].astype(F32)
            after = later_in[c, rows_of(jnp.minimum(me, n - 2))].astype(F32)
            final_out[:, there] = (fade_in[c, :1] * mine + after).astype(BF16)

        @pl.when(me == n - 1)
        def _():
            final_out[:, there] = merged[c, STATE - share :]

        return carry

    def each(first, work):
        start = jnp.clip(s - first, 0, chunks)
        stop = jnp.where(s == last_step, chunks, jnp.clip(s - first + 1, 0, chunks))
        lax.fori_loop(start, stop, work, 0)

    join_at = jnp.where(me == 1, 0, jnp.minimum(lead, chunks + me - 2))
    back_at = 2 + 3 * jnp.maximum(n - 2 - me, 0)
    close_at = jnp.maximum(jnp.where(me == 0, 0, join_at), jnp.where(me < n - 1, back_at, 0))

    @pl.when(me < n - 1)
    def _():
        each(back_at, turn_back)

    pairs = HEADS_CHUNK // 2

    def pair_lanes(pair):
        return slice(pair * 2 * HEAD_DIM, (pair + 1) * 2 * HEAD_DIM)

    @pl.when(s < chunks)
    def _():
        j = s
        bt = bt_ref.at[j // per]
        taps = 0.5 * taps_ref[...].astype(F32)
        bias = 0.5 * bias_ref[...]
        lag = taps.shape[0] - 1
        before = edge_x[:, pl.ds(pl.multiple_of(j * CHUNK, CHUNK), CHUNK)].astype(F32)[EDGE - HALO :]
        spread = spread_of(j)
        spread_ref[j] = spread
        fades = dot(split(fade_ref[...], 3), spread)
        wide_ref[j] = fades
        tiles = [slice(i * 128, (i + 1) * 128) for i in range(CHUNK // 128)]
        for i, lanes in enumerate(tiles):
            lift_ref[i, :HALO] = before[:, lanes]
            lift_ref[i, HALO:] = x_ref[:, lanes].astype(F32)
        state = None
        for k in range(spans):
            at = slice(k * SPAN, (k + 1) * SPAN)
            tail = dot(tail_ref[at], spread[: 2 * heads])
            parts = []
            for i, lanes in enumerate(tiles):
                column = []
                for r in range(0, SPAN, HALF):
                    first = k * SPAN + r
                    half = bias[:, lanes]
                    for q in range(lag + 1):
                        begin = HALO - lag + q + first
                        half = half + lift_ref[i, begin : begin + HALF] * taps[q : q + 1, lanes]
                    value = half * jnp.tanh(half) + half
                    xc[j, first : first + HALF, lanes] = value.astype(BF16)
                    column.append(value * tail[r : r + HALF, lanes])
                parts.append(column)
            scaled = jnp.concatenate([column[1] for column in parts], axis=1).astype(BF16)
            first = jnp.concatenate([column[0] for column in parts], axis=1)
            kept[j, k] = first.astype(BF16)
            first = (first * fades[2 * k + 1 : 2 * k + 2]).astype(BF16)
            scaled = jnp.concatenate([first, scaled], axis=0)
            if k % 2 == 0:
                even[j, k // 2] = scaled
                row = jnp.broadcast_to(
                    fades[2 * k + 2 : 2 * k + 3] * fades[2 * k + 3 : 2 * k + 4], (16, CHUNK)
                ).astype(BF16)[None]
                held = (scaled.reshape(SPAN // 16, 16, CHUNK) * row).reshape(SPAN, CHUNK)
                continue
            scaled = jnp.concatenate([held, scaled], axis=0)
            at = slice((k - 1) * SPAN, (k + 1) * SPAN)
            part = dot(bt[:, at], scaled)
            if state is not None:
                local[j, k // 2 - 1] = state.astype(BF16)
                row = fades[2 * k - 2 : 2 * k - 1]
                for i in range(1, 4):
                    row = row * fades[2 * k - 2 + i : 2 * k - 1 + i]
                part = row * state + part
            state = part
        state = state.astype(BF16)
        sent[j] = state

        @pl.when(me == 0)
        def _():
            merged[j] = state
            onward(j).start()

        @pl.when(me == n - 1)
        def _():
            later_out[j] = state[: STATE - share]
            fade_out[j] = jnp.broadcast_to(fades[total : total + 1], (8, CHUNK))
            lax.fori_loop(0, n - 1, lambda q, z: (behind(q, j).start(), z)[1], 0)
            fading(j).start()

    @pl.when(s == 0)
    def _():
        causal = lax.broadcasted_iota(jnp.int32, (HALF, SPAN), 0) >= (
            lax.broadcasted_iota(jnp.int32, (HALF, SPAN), 1) % HALF
        )
        for g in range(groups):
            if g > 0:
                project(0, g)
            project(1, g)
            for k in range(spans):
                at = slice(k * SPAN, (k + 1) * SPAN)
                scores = dot(c_ref[g, at], bt_ref[g, :, at])
                if k % 2:
                    prior = bt_ref[g, :, (k - 1) * SPAN : k * SPAN]
                    mid_ref[g, (k // 2) * SPAN : (k // 2 + 1) * SPAN] = dot(
                        c_ref[g, at], prior
                    ).astype(BF16)
                for i in range(2):
                    own = slice(i * HALF, (i + 1) * HALF)
                    near = jnp.concatenate([scores[own, own]] * 2, axis=1)
                    near_ref[g, k * SPAN + i * HALF : k * SPAN + (i + 1) * HALF] = jnp.where(
                        causal, near, 0.0
                    )
                far_ref[g, k * HALF : (k + 1) * HALF] = scores[HALF:, :HALF].astype(BF16)
        for k in range(spans):
            at = slice(k * SPAN, (k + 1) * SPAN)
            cumul_ref[at] = split(exact_ref[at], 3)
            rowed = rowed_ref[at]
            wide = jnp.concatenate([rowed] * (128 // heads), axis=1) if heads < 128 else rowed
            turn_ref[...] = wide.T[:heads]
            first = turn_ref[pl.ds(0, heads // 2, stride=2), :]
            second = turn_ref[pl.ds(1, heads // 2, stride=2), :]
            for i in range(2):
                own = slice(i * HALF, (i + 1) * HALF)
                pairs_row = jnp.concatenate([first[:, own], second[:, own]], axis=1)
                for c in range(chunks):
                    row_ref[c, :, (2 * k + i) * SPAN : (2 * k + i + 1) * SPAN] = pairs_row[
                        c * (HEADS_CHUNK // 2) : (c + 1) * (HEADS_CHUNK // 2)
                    ]

        @pl.when(me == 0)
        def _():
            came[...] = jnp.zeros_like(came)

    @pl.when(s >= lead)
    def _():
        j = s - lead
        fades = wide_ref[j]
        spread = spread_ref[j]
        g = j // per
        none = jnp.zeros((), BF16)
        low = lax.broadcasted_iota(jnp.int32, (HALF, 2 * HEAD_DIM), 1) < HEAD_DIM

        for k in range(spans):
            at = slice(k * SPAN, (k + 1) * SPAN)
            cumul = dot(cumul_ref[at], spread)
            carried = None
            if k > 1:
                carried = dot(c_ref[g, at], local[j, k // 2 - 1])
            if k % 2:
                prior = dot(mid_ref[g, (k // 2) * SPAN : (k // 2 + 1) * SPAN], even[j, k // 2])
                if carried is not None:
                    prior = prior + carried * (
                        fades[2 * k - 2 : 2 * k - 1] * fades[2 * k - 1 : 2 * k]
                    )
                carried = prior
            beside = dot(far_ref[g, k * HALF : (k + 1) * HALF], kept[j, k])
            for i in range(2):
                mine = slice(i * HALF, (i + 1) * HALF)
                there = slice(k * SPAN + i * HALF, k * SPAN + (i + 1) * HALF)
                near = near_ref[g, there]
                before = None if carried is None else carried[mine]
                if i == 1:
                    before = beside if before is None else beside + before * fades[2 * k : 2 * k + 1]
                so_far = fades[total + 2 + 2 * k + i : total + 3 + 2 * k + i]
                for pair in range(pairs):
                    lanes = pair_lanes(pair)
                    away = cumul[mine, lanes]
                    spacing = away - row_ref[
                        j, pair : pair + 1, (2 * k + i) * SPAN : (2 * k + i + 1) * SPAN
                    ]
                    weights = (jnp.exp2(jnp.minimum(spacing, 64.0)) * near).astype(BF16)
                    x_pair = xc[j, there, lanes]
                    stacked = jnp.concatenate(
                        [jnp.where(low, x_pair, none), jnp.where(low, none, x_pair)], axis=0
                    )
                    within = dot(weights, stacked) + x_pair.astype(F32) * fades[
                        total + 1 : total + 2, lanes
                    ]
                    half = (0.5 * z_ref[there, lanes]).astype(F32)
                    gate = half * jnp.tanh(half) + half
                    entry = jnp.exp2(away)
                    if before is not None:
                        within = within + entry * before[:, lanes]
                    inside[there, lanes] = within * gate
                    outside[there, lanes] = entry * gate * so_far[:, lanes]

    @pl.when(me > 0)
    def _():
        each(join_at, join)

    each(close_at, close)

    @pl.when(s >= lead)
    def _():
        j = s - lead
        g = j // per
        own = pl.ds(pl.multiple_of(j * CHUNK, CHUNK), CHUNK)
        for k in range(spans):
            at = slice(k * SPAN, (k + 1) * SPAN)
            readout = dot(c_ref[g, at], came[j])
            y_ref[at, own] = (inside[at] + outside[at] * readout).astype(BF16)

    @pl.when(s == last_step)
    def _():
        @pl.when(me < n - 1)
        def _():
            for copy in edge_copies():
                copy.wait_send()
            for c in range(chunks):
                onward(c).wait_send()

        @pl.when(me > 0)
        def _():
            for c in range(chunks):
                lax.fori_loop(0, me, lambda q, z: (behind(q, c).wait_send(), z)[1], 0)
                fading(c).wait_send()


def scan(n, x, taps, bias, bc, taps_bc, bias_bc, dt, dt_bias, a_log, skip, z, groups):
    rows, channels = x.shape
    chunks = channels // CHUNK
    heads = dt.shape[0]
    lead = leading(n, chunks)
    lines = bc.shape[0] // rows
    fade_rows = -(-(4 * (rows // SPAN) + 2) // 8) * 8
    share = STATE // n
    spans = rows // SPAN
    turn = lambda s: (0, jnp.minimum(s, chunks - 1))
    later = lambda s: (0, jnp.maximum(s - lead, 0))
    still = lambda s: (0, 0)
    return pl.pallas_call(
        functools.partial(scan_kernel, n),
        grid=(lead + chunks,),
        in_specs=[
            pl.BlockSpec((rows, CHUNK), turn),
            pl.BlockSpec((taps.shape[0], CHUNK), turn),
            pl.BlockSpec((1, CHUNK), turn),
            pl.BlockSpec(bc.shape, still),
            pl.BlockSpec(taps_bc.shape, still),
            pl.BlockSpec(bias_bc.shape, still),
            pl.BlockSpec((heads, rows), still),
            pl.BlockSpec((1, heads), still),
            pl.BlockSpec((1, heads), still),
            pl.BlockSpec((1, heads), still),
            pl.BlockSpec((rows, CHUNK), later),
            pl.BlockSpec(memory_space=pl.ANY),
            pl.BlockSpec(memory_space=pl.ANY),
        ],
        out_specs=[
            pl.BlockSpec(memory_space=pltpu.VMEM),
            pl.BlockSpec(memory_space=pltpu.VMEM),
        ],
        out_shape=[
            pltpu.VMEM((rows, channels), BF16),
            pltpu.VMEM((share, channels), BF16),
        ],
        scratch_shapes=[
            pltpu.VMEM((chunks, rows, CHUNK), BF16),
            pltpu.VMEM((chunks, STATE, CHUNK), BF16),
            pltpu.VMEM((chunks, STATE, CHUNK), BF16),
            pltpu.VMEM((chunks, STATE, CHUNK), BF16),
            pltpu.VMEM((chunks, STATE - share, CHUNK), BF16),
            pltpu.VMEM((chunks, STATE - share, CHUNK), BF16),
            pltpu.VMEM((chunks, 8, CHUNK), F32),
            pltpu.VMEM((chunks, 8, CHUNK), F32),
            pltpu.VMEM((chunks, max(spans // 2 - 1, 1), STATE, CHUNK), BF16),
            pltpu.VMEM((rows, heads), F32),
            pltpu.VMEM((rows, heads), F32),
            pltpu.VMEM((rows, 3 * heads), BF16),
            pltpu.VMEM((chunks, HEADS_CHUNK // 2, 2 * rows), F32),
            pltpu.VMEM((heads, SPAN), F32),
            pltpu.VMEM((rows, 2 * heads), BF16),
            pltpu.VMEM((fade_rows, heads), F32),
            pltpu.VMEM((groups, STATE, rows), BF16),
            pltpu.VMEM((groups, rows, STATE), BF16),
            pltpu.VMEM((groups, rows, SPAN), F32),
            pltpu.VMEM((groups, rows // 2, HALF), BF16),
            pltpu.VMEM((chunks, spans, HALF, CHUNK), BF16),
            pltpu.VMEM((chunks, spans // 2, SPAN, CHUNK), BF16),
            pltpu.VMEM((groups, rows // 2, SPAN), BF16),
            pltpu.VMEM((rows, CHUNK), F32),
            pltpu.VMEM((rows, CHUNK), F32),
            pltpu.VMEM(((EDGE_TOKENS + rows) * lines, 128), F32),
            pltpu.VMEM((CHUNK // 128, HALO + rows, 128), F32),
            pltpu.VMEM((chunks, 3 * heads, CHUNK), BF16),
            pltpu.VMEM((chunks, fade_rows, CHUNK), F32),
            pltpu.VMEM((EDGE, channels), BF16),
            pltpu.VMEM((EDGE_TOKENS * lines, 128), BF16),
            pltpu.SemaphoreType.DMA((chunks,)),
            pltpu.SemaphoreType.DMA((chunks,)),
            pltpu.SemaphoreType.DMA((n - 1, chunks)),
            pltpu.SemaphoreType.DMA((n - 1, chunks)),
            pltpu.SemaphoreType.DMA((chunks,)),
            pltpu.SemaphoreType.DMA((chunks,)),
            pltpu.SemaphoreType.DMA((2,)),
            pltpu.SemaphoreType.DMA((2,)),
        ],
        compiler_params=pltpu.CompilerParams(
            dimension_semantics=("arbitrary",),
            vmem_limit_bytes=56 << 20,
            collective_id=0,
            has_side_effects=True,
        ),
        cost_estimate=pl.CostEstimate(
            flops=20 * rows * channels * STATE, bytes_accessed=4 * rows * channels, transcendentals=4 * rows * channels
        ),
    )(x, taps, bias, bc, taps_bc, bias_bc, dt, dt_bias, a_log, skip, z, x, bc)


def per_device(
    x_in,
    bc_in,
    z_in,
    dt_raw,
    conv_x,
    conv_bc,
    conv_bias_x,
    conv_bias_bc,
    dt_bias,
    a_log,
    d_skip,
    norm_gain,
):
    rows, channels = x_in.shape
    heads = dt_raw.shape[1]
    n = lax.axis_size("ctx")
    tiles = bc_in.shape[2] // 128
    groups = bc_in.shape[2] // STATE

    def lined(v):
        return v.reshape(-1, 2, tiles, 128).transpose(0, 2, 1, 3).reshape(-1, 128)

    gated, final = scan(
        n,
        x_in,
        conv_x,
        conv_bias_x[None],
        lined(bc_in),
        lined(conv_bc),
        lined(conv_bias_bc),
        dt_raw.T,
        dt_bias[None],
        a_log[None],
        d_skip[None],
        z_in,
        groups,
    )
    return tuple(finish(gated, norm_gain[None], final, groups))


def solution(mesh):
    in_specs = (
        P(("group", "ctx"), "tp"),
        P(("group", "ctx"), None, "tp"),
        P(("group", "ctx"), "tp"),
        P(("group", "ctx"), "tp"),
        P(None, "tp"),
        P(None, None, "tp"),
        P("tp"),
        P(None, "tp"),
        P("tp"),
        P("tp"),
        P("tp"),
        P("tp"),
    )
    out_specs = (P(("group", "ctx"), "tp"), P(("group", "tp"), None, "ctx"))
    return jax.shard_map(
        per_device, mesh=mesh, in_specs=in_specs, out_specs=out_specs, check_vma=False
    )
```

```python
import functools
import math

import jax
import jax.numpy as jnp
from jax import lax
from jax.experimental import pallas as pl
from jax.experimental.pallas import tpu as pltpu
from jax.sharding import PartitionSpec as P

HEAD_DIM = 64
STATE = 256
SPAN = 128
CHUNK = 512
HEADS_CHUNK = CHUNK // HEAD_DIM
HALO = 8
LOG2E = math.log2(math.e)

eps = 1e-05
F32 = jnp.float32
BF16 = jnp.bfloat16


def dot(a, b):
    return jnp.dot(a, b, preferred_element_type=F32)


def rescaled(gated, gain):
    gated = gated.astype(F32)
    meansq = jnp.mean(gated * gated, axis=-1, keepdims=True)
    return (gated * lax.rsqrt(meansq + eps) * gain).astype(BF16)


def finish_kernel(groups, gated_ref, gain_ref, final_ref, out_any, state_any, mixed, turned, sems):
    rows, channels = gated_ref.shape
    width = channels // groups
    blocks = rows // SPAN
    part = CHUNK // HEAD_DIM
    for c in range(channels // CHUNK):
        block = final_ref[:, c * CHUNK : (c + 1) * CHUNK].astype(F32).T
        turned[c * part : (c + 1) * part] = block.reshape(part, HEAD_DIM, block.shape[1])
    copies = [pltpu.make_async_copy(turned, state_any, sems.at[blocks])]
    copies[-1].start()
    for b in range(blocks):
        at = slice(b * SPAN, (b + 1) * SPAN)
        for g in range(groups):
            own = slice(g * width, (g + 1) * width)
            mixed[at, own] = rescaled(gated_ref[at, own], gain_ref[:, own])
        there = pl.ds(b * SPAN, SPAN)
        copies.append(pltpu.make_async_copy(mixed.at[there], out_any.at[there], sems.at[b]))
        copies[-1].start()
    for copy in copies:
        copy.wait()


def finish(gated, gain, final, groups):
    rows, channels = gated.shape
    share = final.shape[0]
    heads = channels // HEAD_DIM
    whole = pl.BlockSpec(memory_space=pltpu.VMEM)
    away = pl.BlockSpec(memory_space=pl.ANY)
    return pl.pallas_call(
        functools.partial(finish_kernel, groups),
        in_specs=[whole, whole, whole],
        out_specs=[away, away],
        out_shape=[
            jax.ShapeDtypeStruct((rows, channels), BF16),
            jax.ShapeDtypeStruct((heads, HEAD_DIM, share), F32),
        ],
        scratch_shapes=[
            pltpu.VMEM((rows, channels), BF16),
            pltpu.VMEM((heads, HEAD_DIM, share), F32),
            pltpu.SemaphoreType.DMA((1 + rows // SPAN,)),
        ],
        compiler_params=pltpu.CompilerParams(vmem_limit_bytes=16 << 20),
        cost_estimate=pl.CostEstimate(
            flops=4 * rows * channels, bytes_accessed=4 * rows * channels, transcendentals=rows
        ),
    )(gated, gain, final)


EDGE = 16
EDGE_TOKENS = 4
HALF = SPAN // 2
MESH = pl.DeviceIdType.MESH


def leading(n, chunks):
    return chunks + max(0, n - 4)


def pieces(v, parts):
    out = []
    for _ in range(parts):
        out.append(v.astype(BF16))
        v = v - out[-1].astype(F32)
    return out


def split(v, parts):
    return jnp.concatenate([piece.astype(F32) for piece in pieces(v, parts)], axis=1).astype(BF16)


def scan_kernel(
    n,
    x_ref,
    taps_ref,
    bias_ref,
    bc_ref,
    taps_bc_ref,
    bias_bc_ref,
    dt_ref,
    dt_bias_ref,
    a_log_ref,
    skip_ref,
    z_any,
    x_any,
    bc_any,
    y_ref,
    final_out,
    xc,
    sent,
    merged,
    came,
    later_out,
    later_in,
    fade_out,
    fade_in,
    local,
    exact_ref,
    step_ref,
    cumul_ref,
    row_ref,
    turn_ref,
    tail_ref,
    fade_ref,
    bt_ref,
    c_ref,
    near_ref,
    far_ref,
    kept,
    even,
    mid_ref,
    inside,
    outside,
    raw_ref,
    lift_ref,
    spread_ref,
    wide_ref,
    z_buf,
    edge_x,
    edge_bc,
    z_sem,
    send_sem,
    recv_sem,
    later_send,
    later_recv,
    fade_send,
    fade_recv,
    edge_send,
    edge_recv,
):
    s = pl.program_id(0)
    chunks = sent.shape[0]
    lead = leading(n, chunks)
    last_step = lead + chunks - 1
    me = lax.axis_index("ctx")
    rows = x_ref.shape[0]
    spans = rows // SPAN
    heads = dt_ref.shape[0]
    groups = bt_ref.shape[0]
    per = chunks // groups
    lines = bc_ref.shape[0] // rows
    reach = EDGE_TOKENS * lines
    share = STATE // n
    right = jnp.minimum(me + 1, n - 1)
    left = jnp.maximum(me - 1, 0)
    total = 2 * spans

    def edge_copies():
        return [
            pltpu.make_async_remote_copy(
                src_ref=whole.at[pl.ds(whole.shape[0] - edge.shape[0], edge.shape[0])],
                dst_ref=edge,
                send_sem=edge_send.at[i],
                recv_sem=edge_recv.at[i],
                device_id={"ctx": right},
                device_id_type=MESH,
            )
            for i, (whole, edge) in enumerate(((bc_any, edge_bc), (x_any, edge_x)))
        ]

    def onward(c):
        return pltpu.make_async_remote_copy(
            src_ref=merged.at[c],
            dst_ref=came.at[c],
            send_sem=send_sem.at[c],
            recv_sem=recv_sem.at[c],
            device_id={"ctx": right},
            device_id_type=MESH,
        )

    def fetch(c):
        return pltpu.make_async_copy(
            z_any.at[:, pl.ds(pl.multiple_of(c * CHUNK, CHUNK), CHUNK)],
            z_buf.at[lax.rem(c, 2)],
            z_sem.at[lax.rem(c, 2)],
        )

    def rows_of(q):
        return pl.ds(pl.multiple_of(q * share, share), share)

    def behind(q, c):
        return pltpu.make_async_remote_copy(
            src_ref=later_out.at[c, rows_of(q)],
            dst_ref=later_in.at[c, rows_of(q)],
            send_sem=later_send.at[q, c],
            recv_sem=later_recv.at[q, c],
            device_id={"ctx": left},
            device_id_type=MESH,
        )

    def fading(c):
        return pltpu.make_async_remote_copy(
            src_ref=fade_out.at[c],
            dst_ref=fade_in.at[c],
            send_sem=fade_send.at[c],
            recv_sem=fade_recv.at[c],
            device_id={"ctx": left},
            device_id_type=MESH,
        )

    def spread_of(c):
        shape = (3 * heads, CHUNK)
        return (
            lax.broadcasted_iota(jnp.int32, shape, 1) // HEAD_DIM + c * HEADS_CHUNK
            == lax.broadcasted_iota(jnp.int32, shape, 0) % heads
        ).astype(BF16)

    def project(side, g, over):
        taps = 0.5 * taps_bc_ref[...].astype(F32)
        bias = 0.5 * bias_bc_ref[...]
        lag = taps.shape[0] // lines - 1
        for k in over:
            at = slice(k * SPAN, (k + 1) * SPAN)
            for i in range(STATE // 128):
                line = 2 * (g * (STATE // 128) + i) + side
                own = slice(i * 128, (i + 1) * 128)
                half = bias[line : line + 1]
                for q in range(lag + 1):
                    begin = (k * SPAN + EDGE_TOKENS - lag + q) * lines + line
                    tap = taps[q * lines + line : q * lines + line + 1]
                    half = half + raw_ref[pl.ds(begin, SPAN, stride=lines), :] * tap
                v = half * jnp.tanh(half) + half
                if side == 0:
                    bt_ref[g, own, at] = v.astype(BF16).astype(F32).T.astype(BF16)
                else:
                    c_ref[g, at, own] = v.astype(BF16)

    @pl.when(s == 0)
    def _():
        barrier = pltpu.get_barrier_semaphore()
        for k in range(1, n):
            pl.semaphore_signal(
                barrier, inc=1, device_id={"ctx": lax.rem(me + k, n)}, device_id_type=MESH
            )
        rate = -LOG2E * jnp.exp(a_log_ref[...])
        above = lax.broadcasted_iota(jnp.int32, (SPAN, SPAN), 0)
        left = lax.broadcasted_iota(jnp.int32, (SPAN, SPAN), 1)
        lower = ((above >= left) & (above // HALF == left // HALF)).astype(BF16)
        lower = jnp.concatenate([lower] * 3, axis=1)
        so_far = jnp.zeros((1, heads), F32)
        fade_ref[...] = jnp.zeros_like(fade_ref)
        ats = [slice(k * SPAN, (k + 1) * SPAN) for k in range(spans)]
        raws = [dt_ref[:, at].T + dt_bias_ref[...] for at in ats]
        steps = [jnp.maximum(v, 0.0) + jnp.log1p(jnp.exp(-jnp.abs(v))) for v in raws]
        cumuls = [dot(lower, jnp.concatenate(pieces(step * rate, 3), axis=0)) for step in steps]
        for k, at in enumerate(ats):
            cumul = cumuls[k]
            step = steps[k]
            ends = cumul[HALF - 1 : HALF], cumul[SPAN - 1 :]
            tail = jnp.concatenate(
                [end - cumul[i * HALF : (i + 1) * HALF] for i, end in enumerate(ends)], axis=0
            )
            exact_ref[at] = cumul
            step_ref[at] = step
            tail_ref[at] = split(jnp.exp2(tail) * step, 2)
            for i in range(2):
                part = 2 * k + i
                fade_ref[part : part + 1] = jnp.exp2(ends[i])
                fade_ref[total + 2 + part : total + 3 + part] = jnp.exp2(so_far)
                so_far = so_far + ends[i]
        fade_ref[2 * spans : 2 * spans + 1] = jnp.exp2(so_far)
        fade_ref[2 * spans + 1 : 2 * spans + 2] = skip_ref[...]
        pl.semaphore_wait(barrier, n - 1)

        @pl.when(me < n - 1)
        def _():
            for copy in edge_copies():
                copy.start()

        raw_ref[reach:] = bc_ref[...].astype(F32)
        project(0, 0, range(1, spans))

        @pl.when(me == 0)
        def _():
            edge_x[...] = jnp.zeros_like(edge_x)
            edge_bc[...] = jnp.zeros_like(edge_bc)

        @pl.when(me > 0)
        def _():
            for copy in edge_copies():
                copy.wait_recv()

        raw_ref[:reach] = edge_bc[...].astype(F32)
        project(0, 0, range(1))

    def join(c, carry):
        onward(c).wait_recv()
        got = came[c].astype(F32)
        merged[c] = (wide_ref[c, total : total + 1] * got + sent[c].astype(F32)).astype(BF16)

        @pl.when(me < n - 1)
        def _():
            onward(c).start()

        return carry

    def turn_back(c, carry):
        lax.fori_loop(0, me + 1, lambda q, z: (behind(q, c).wait_recv(), z)[1], 0)
        fading(c).wait_recv()

        def add(q, z):
            mine = sent[c, rows_of(q)].astype(F32)
            after = later_in[c, rows_of(q)].astype(F32)
            later_out[c, rows_of(q)] = (fade_in[c, :1] * mine + after).astype(BF16)
            behind(q, c).start()
            return z

        lax.fori_loop(0, me, add, 0)

        @pl.when(me > 0)
        def _():
            fade_out[c] = fade_in[c] * wide_ref[c, total : total + 1]
            fading(c).start()

        return carry

    def close(c, carry):
        there = pl.ds(pl.multiple_of(c * CHUNK, CHUNK), CHUNK)

        @pl.when(me < n - 1)
        def _():
            mine = merged[c, rows_of(me)].astype(F32)
            after = later_in[c, rows_of(jnp.minimum(me, n - 2))].astype(F32)
            final_out[:, there] = (fade_in[c, :1] * mine + after).astype(BF16)

        @pl.when(me == n - 1)
        def _():
            final_out[:, there] = merged[c, STATE - share :]

        return carry

    def each(first, work):
        start = jnp.clip(s - first, 0, chunks)
        stop = jnp.where(s == last_step, chunks, jnp.clip(s - first + 1, 0, chunks))
        lax.fori_loop(start, stop, work, 0)

    join_at = jnp.where(me == 1, 0, jnp.minimum(lead, chunks + me - 2))
    back_at = 2 + 3 * jnp.maximum(n - 2 - me, 0)
    close_at = jnp.maximum(jnp.where(me == 0, 0, join_at), jnp.where(me < n - 1, back_at, 0))

    @pl.when(me < n - 1)
    def _():
        each(back_at, turn_back)

    pairs = HEADS_CHUNK // 2

    def pair_lanes(pair):
        return slice(pair * 2 * HEAD_DIM, (pair + 1) * 2 * HEAD_DIM)

    @pl.when(s < chunks)
    def _():
        j = s
        bt = bt_ref.at[j // per]
        taps = 0.5 * taps_ref[...].astype(F32)
        bias = 0.5 * bias_ref[...]
        lag = taps.shape[0] - 1
        before = edge_x[:, pl.ds(pl.multiple_of(j * CHUNK, CHUNK), CHUNK)].astype(F32)[EDGE - HALO :]
        spread = spread_of(j)
        spread_ref[j] = spread
        fades = dot(split(fade_ref[...], 3), spread)
        wide_ref[j] = fades
        tiles = [slice(i * 128, (i + 1) * 128) for i in range(CHUNK // 128)]
        for i, lanes in enumerate(tiles):
            lift_ref[i, :HALO] = before[:, lanes]
            lift_ref[i, HALO:] = x_ref[:, lanes].astype(F32)
        inside[...] = dot(tail_ref[...], spread[: 2 * heads])
        state = None
        for k in range(spans):
            at = slice(k * SPAN, (k + 1) * SPAN)
            parts = []
            for i, lanes in enumerate(tiles):
                column = []
                for r in range(0, SPAN, HALF):
                    first = k * SPAN + r
                    half = bias[:, lanes]
                    for q in range(lag + 1):
                        begin = HALO - lag + q + first
                        half = half + lift_ref[i, begin : begin + HALF] * taps[q : q + 1, lanes]
                    value = half * jnp.tanh(half) + half
                    xc[j, first : first + HALF, lanes] = value.astype(BF16)
                    column.append(value * inside[first : first + HALF, lanes])
                parts.append(column)
            scaled = jnp.concatenate([column[1] for column in parts], axis=1).astype(BF16)
            first = jnp.concatenate([column[0] for column in parts], axis=1)
            kept[j, k] = first.astype(BF16)
            first = (first * fades[2 * k + 1 : 2 * k + 2]).astype(BF16)
            scaled = jnp.concatenate([first, scaled], axis=0)
            if k % 2 == 0:
                even[j, k // 2] = scaled
                row = jnp.broadcast_to(
                    fades[2 * k + 2 : 2 * k + 3] * fades[2 * k + 3 : 2 * k + 4], (16, CHUNK)
                ).astype(BF16)[None]
                held = (scaled.reshape(SPAN // 16, 16, CHUNK) * row).reshape(SPAN, CHUNK)
                continue
            scaled = jnp.concatenate([held, scaled], axis=0)
            at = slice((k - 1) * SPAN, (k + 1) * SPAN)
            part = dot(bt[:, at], scaled)
            if state is not None:
                local[j, k // 2 - 1] = state.astype(BF16)
                row = fades[2 * k - 2 : 2 * k - 1]
                for i in range(1, 4):
                    row = row * fades[2 * k - 2 + i : 2 * k - 1 + i]
                part = row * state + part
            state = part
        state = state.astype(BF16)
        sent[j] = state

        @pl.when(me == 0)
        def _():
            merged[j] = state
            onward(j).start()

        @pl.when(me == n - 1)
        def _():
            later_out[j] = state[: STATE - share]
            fade_out[j] = jnp.broadcast_to(fades[total : total + 1], (8, CHUNK))
            lax.fori_loop(0, n - 1, lambda q, z: (behind(q, j).start(), z)[1], 0)
            fading(j).start()

    @pl.when(s == 0)
    def _():
        for g in range(1, groups):
            project(0, g, range(spans))
        project(1, 0, range(spans))

    @pl.when(s == 1)
    def _():
        fetch(0).start()
        for g in range(1, groups):
            project(1, g, range(spans))
        causal = lax.broadcasted_iota(jnp.int32, (HALF, SPAN), 0) >= (
            lax.broadcasted_iota(jnp.int32, (HALF, SPAN), 1) % HALF
        )
        for g in range(groups):
            for k in range(spans):
                at = slice(k * SPAN, (k + 1) * SPAN)
                scores = dot(c_ref[g, at], bt_ref[g, :, at])
                if k % 2:
                    prior = bt_ref[g, :, (k - 1) * SPAN : k * SPAN]
                    mid_ref[g, (k // 2) * SPAN : (k // 2 + 1) * SPAN] = dot(
                        c_ref[g, at], prior
                    ).astype(BF16)
                for i in range(2):
                    own = slice(i * HALF, (i + 1) * HALF)
                    near = jnp.concatenate([scores[own, own]] * 2, axis=1)
                    near_ref[g, k * SPAN + i * HALF : k * SPAN + (i + 1) * HALF] = jnp.where(
                        causal, near, 0.0
                    )
                far_ref[g, k * HALF : (k + 1) * HALF] = scores[HALF:, :HALF].astype(BF16)
        for k in range(spans):
            at = slice(k * SPAN, (k + 1) * SPAN)
            cumul_ref[at] = split(exact_ref[at], 3)
            rowed = exact_ref[at] - jnp.log2(step_ref[at])
            wide = jnp.concatenate([rowed] * (128 // heads), axis=1) if heads < 128 else rowed
            turn_ref[...] = wide.T[:heads]
            first = turn_ref[pl.ds(0, heads // 2, stride=2), :]
            second = turn_ref[pl.ds(1, heads // 2, stride=2), :]
            for i in range(2):
                own = slice(i * HALF, (i + 1) * HALF)
                pairs_row = jnp.concatenate([first[:, own], second[:, own]], axis=1)
                for c in range(chunks):
                    row_ref[c, :, (2 * k + i) * SPAN : (2 * k + i + 1) * SPAN] = pairs_row[
                        c * (HEADS_CHUNK // 2) : (c + 1) * (HEADS_CHUNK // 2)
                    ]

        @pl.when(me == 0)
        def _():
            came[...] = jnp.zeros_like(came)

    @pl.when(s >= lead)
    def _():
        j = s - lead
        fetch(j).wait()

        @pl.when(s < last_step)
        def _():
            fetch(j + 1).start()

        slot = lax.rem(j, 2)
        fades = wide_ref[j]
        spread = spread_ref[j]
        g = j // per
        none = jnp.zeros((), BF16)
        low = lax.broadcasted_iota(jnp.int32, (HALF, 2 * HEAD_DIM), 1) < HEAD_DIM

        outside[...] = dot(cumul_ref[...], spread)
        for k in range(spans):
            at = slice(k * SPAN, (k + 1) * SPAN)
            carried = None
            if k > 1:
                if k % 2 == 0:
                    both = slice(k * SPAN, (k + 2) * SPAN)
                    inside[both] = dot(c_ref[g, both], local[j, k // 2 - 1])
                carried = inside[at]
            if k % 2:
                prior = dot(mid_ref[g, (k // 2) * SPAN : (k // 2 + 1) * SPAN], even[j, k // 2])
                if carried is not None:
                    prior = prior + carried * (
                        fades[2 * k - 2 : 2 * k - 1] * fades[2 * k - 1 : 2 * k]
                    )
                carried = prior
            beside = dot(far_ref[g, k * HALF : (k + 1) * HALF], kept[j, k])
            for i in range(2):
                mine = slice(i * HALF, (i + 1) * HALF)
                there = slice(k * SPAN + i * HALF, k * SPAN + (i + 1) * HALF)
                near = near_ref[g, there]
                before = None if carried is None else carried[mine]
                if i == 1:
                    before = beside if before is None else beside + before * fades[2 * k : 2 * k + 1]
                so_far = fades[total + 2 + 2 * k + i : total + 3 + 2 * k + i]
                for pair in range(pairs):
                    lanes = pair_lanes(pair)
                    away = outside[there, lanes]
                    spacing = away - row_ref[
                        j, pair : pair + 1, (2 * k + i) * SPAN : (2 * k + i + 1) * SPAN
                    ]
                    weights = (jnp.exp2(jnp.minimum(spacing, 64.0)) * near).astype(BF16)
                    x_pair = xc[j, there, lanes]
                    stacked = jnp.concatenate(
                        [jnp.where(low, x_pair, none), jnp.where(low, none, x_pair)], axis=0
                    )
                    within = dot(weights, stacked) + x_pair.astype(F32) * fades[
                        total + 1 : total + 2, lanes
                    ]
                    half = (0.5 * z_buf[slot, there, lanes]).astype(F32)
                    gate = half * jnp.tanh(half) + half
                    entry = jnp.exp2(away)
                    if before is not None:
                        within = within + entry * before[:, lanes]
                    inside[there, lanes] = within * gate
                    outside[there, lanes] = entry * gate * so_far[:, lanes]

    @pl.when(me > 0)
    def _():
        each(join_at, join)

    each(close_at, close)

    @pl.when(s >= lead)
    def _():
        j = s - lead
        g = j // per
        own = pl.ds(pl.multiple_of(j * CHUNK, CHUNK), CHUNK)
        readout = dot(c_ref[g], came[j])
        y_ref[:, own] = (inside[...] + outside[...] * readout).astype(BF16)

    @pl.when(s == last_step)
    def _():
        @pl.when(me < n - 1)
        def _():
            for copy in edge_copies():
                copy.wait_send()
            for c in range(chunks):
                onward(c).wait_send()

        @pl.when(me > 0)
        def _():
            for c in range(chunks):
                lax.fori_loop(0, me, lambda q, z: (behind(q, c).wait_send(), z)[1], 0)
                fading(c).wait_send()


def scan(n, x, taps, bias, bc, taps_bc, bias_bc, dt, dt_bias, a_log, skip, z, groups):
    rows, channels = x.shape
    chunks = channels // CHUNK
    heads = dt.shape[0]
    lead = leading(n, chunks)
    lines = bc.shape[0] // rows
    fade_rows = -(-(4 * (rows // SPAN) + 2) // 8) * 8
    share = STATE // n
    spans = rows // SPAN
    turn = lambda s: (0, jnp.minimum(s, chunks - 1))
    still = lambda s: (0, 0)
    return pl.pallas_call(
        functools.partial(scan_kernel, n),
        grid=(lead + chunks,),
        in_specs=[
            pl.BlockSpec((rows, CHUNK), turn),
            pl.BlockSpec((taps.shape[0], CHUNK), turn),
            pl.BlockSpec((1, CHUNK), turn),
            pl.BlockSpec(bc.shape, still),
            pl.BlockSpec(taps_bc.shape, still),
            pl.BlockSpec(bias_bc.shape, still),
            pl.BlockSpec((heads, rows), still),
            pl.BlockSpec((1, heads), still),
            pl.BlockSpec((1, heads), still),
            pl.BlockSpec((1, heads), still),
            pl.BlockSpec(memory_space=pl.ANY),
            pl.BlockSpec(memory_space=pl.ANY),
            pl.BlockSpec(memory_space=pl.ANY),
        ],
        out_specs=[
            pl.BlockSpec(memory_space=pltpu.VMEM),
            pl.BlockSpec(memory_space=pltpu.VMEM),
        ],
        out_shape=[
            pltpu.VMEM((rows, channels), BF16),
            pltpu.VMEM((share, channels), BF16),
        ],
        scratch_shapes=[
            pltpu.VMEM((chunks, rows, CHUNK), BF16),
            pltpu.VMEM((chunks, STATE, CHUNK), BF16),
            pltpu.VMEM((chunks, STATE, CHUNK), BF16),
            pltpu.VMEM((chunks, STATE, CHUNK), BF16),
            pltpu.VMEM((chunks, STATE - share, CHUNK), BF16),
            pltpu.VMEM((chunks, STATE - share, CHUNK), BF16),
            pltpu.VMEM((chunks, 8, CHUNK), F32),
            pltpu.VMEM((chunks, 8, CHUNK), F32),
            pltpu.VMEM((chunks, max(spans // 2 - 1, 1), STATE, CHUNK), BF16),
            pltpu.VMEM((rows, heads), F32),
            pltpu.VMEM((rows, heads), F32),
            pltpu.VMEM((rows, 3 * heads), BF16),
            pltpu.VMEM((chunks, HEADS_CHUNK // 2, 2 * rows), F32),
            pltpu.VMEM((heads, SPAN), F32),
            pltpu.VMEM((rows, 2 * heads), BF16),
            pltpu.VMEM((fade_rows, heads), F32),
            pltpu.VMEM((groups, STATE, rows), BF16),
            pltpu.VMEM((groups, rows, STATE), BF16),
            pltpu.VMEM((groups, rows, SPAN), F32),
            pltpu.VMEM((groups, rows // 2, HALF), BF16),
            pltpu.VMEM((chunks, spans, HALF, CHUNK), BF16),
            pltpu.VMEM((chunks, spans // 2, SPAN, CHUNK), BF16),
            pltpu.VMEM((groups, rows // 2, SPAN), BF16),
            pltpu.VMEM((rows, CHUNK), F32),
            pltpu.VMEM((rows, CHUNK), F32),
            pltpu.VMEM(((EDGE_TOKENS + rows) * lines, 128), F32),
            pltpu.VMEM((CHUNK // 128, HALO + rows, 128), F32),
            pltpu.VMEM((chunks, 3 * heads, CHUNK), BF16),
            pltpu.VMEM((chunks, fade_rows, CHUNK), F32),
            pltpu.VMEM((2, rows, CHUNK), BF16),
            pltpu.VMEM((EDGE, channels), BF16),
            pltpu.VMEM((EDGE_TOKENS * lines, 128), BF16),
            pltpu.SemaphoreType.DMA((2,)),
            pltpu.SemaphoreType.DMA((chunks,)),
            pltpu.SemaphoreType.DMA((chunks,)),
            pltpu.SemaphoreType.DMA((n - 1, chunks)),
            pltpu.SemaphoreType.DMA((n - 1, chunks)),
            pltpu.SemaphoreType.DMA((chunks,)),
            pltpu.SemaphoreType.DMA((chunks,)),
            pltpu.SemaphoreType.DMA((2,)),
            pltpu.SemaphoreType.DMA((2,)),
        ],
        compiler_params=pltpu.CompilerParams(
            dimension_semantics=("arbitrary",),
            vmem_limit_bytes=56 << 20,
            collective_id=0,
            has_side_effects=True,
        ),
        cost_estimate=pl.CostEstimate(
            flops=20 * rows * channels * STATE, bytes_accessed=4 * rows * channels, transcendentals=4 * rows * channels
        ),
    )(x, taps, bias, bc, taps_bc, bias_bc, dt, dt_bias, a_log, skip, z, x, bc)


def per_device(
    x_in,
    bc_in,
    z_in,
    dt_raw,
    conv_x,
    conv_bc,
    conv_bias_x,
    conv_bias_bc,
    dt_bias,
    a_log,
    d_skip,
    norm_gain,
):
    rows, channels = x_in.shape
    heads = dt_raw.shape[1]
    n = lax.axis_size("ctx")
    tiles = bc_in.shape[2] // 128
    groups = bc_in.shape[2] // STATE

    def lined(v):
        return v.reshape(-1, 2, tiles, 128).transpose(0, 2, 1, 3).reshape(-1, 128)

    gated, final = scan(
        n,
        x_in,
        conv_x,
        conv_bias_x[None],
        lined(bc_in),
        lined(conv_bc),
        lined(conv_bias_bc),
        dt_raw.T,
        dt_bias[None],
        a_log[None],
        d_skip[None],
        z_in,
        groups,
    )
    return tuple(finish(gated, norm_gain[None], final, groups))


def solution(mesh):
    in_specs = (
        P(("group", "ctx"), "tp"),
        P(("group", "ctx"), None, "tp"),
        P(("group", "ctx"), "tp"),
        P(("group", "ctx"), "tp"),
        P(None, "tp"),
        P(None, None, "tp"),
        P("tp"),
        P(None, "tp"),
        P("tp"),
        P("tp"),
        P("tp"),
        P("tp"),
    )
    out_specs = (P(("group", "ctx"), "tp"), P(("group", "tp"), None, "ctx"))
    return jax.shard_map(
        per_device, mesh=mesh, in_specs=in_specs, out_specs=out_specs, check_vma=False
    )
```

```python
import functools
import math

import jax
import jax.numpy as jnp
from jax import lax
from jax.experimental import pallas as pl
from jax.experimental.pallas import tpu as pltpu
from jax.sharding import PartitionSpec as P

HEAD_DIM = 64
STATE = 256
SPAN = 128
CHUNK = 512
HEADS_CHUNK = CHUNK // HEAD_DIM
HALO = 8
LOG2E = math.log2(math.e)

eps = 1e-05
F32 = jnp.float32
BF16 = jnp.bfloat16


def dot(a, b):
    return jnp.dot(a, b, preferred_element_type=F32)


def rescaled(gated, gain):
    gated = gated.astype(F32)
    meansq = jnp.mean(gated * gated, axis=-1, keepdims=True)
    return (gated * lax.rsqrt(meansq + eps) * gain).astype(BF16)


def finish_kernel(groups, gated_ref, gain_ref, final_ref, out_any, state_any, mixed, turned, sems):
    rows, channels = gated_ref.shape
    width = channels // groups
    blocks = rows // SPAN
    part = CHUNK // HEAD_DIM
    for c in range(channels // CHUNK):
        block = final_ref[:, c * CHUNK : (c + 1) * CHUNK].astype(F32).T
        turned[c * part : (c + 1) * part] = block.reshape(part, HEAD_DIM, block.shape[1])
    copies = [pltpu.make_async_copy(turned, state_any, sems.at[blocks])]
    copies[-1].start()
    for b in range(blocks):
        at = slice(b * SPAN, (b + 1) * SPAN)
        for g in range(groups):
            own = slice(g * width, (g + 1) * width)
            mixed[at, own] = rescaled(gated_ref[at, own], gain_ref[:, own])
        there = pl.ds(b * SPAN, SPAN)
        copies.append(pltpu.make_async_copy(mixed.at[there], out_any.at[there], sems.at[b]))
        copies[-1].start()
    for copy in copies:
        copy.wait()


def finish(gated, gain, final, groups):
    rows, channels = gated.shape
    share = final.shape[0]
    heads = channels // HEAD_DIM
    whole = pl.BlockSpec(memory_space=pltpu.VMEM)
    away = pl.BlockSpec(memory_space=pl.ANY)
    return pl.pallas_call(
        functools.partial(finish_kernel, groups),
        in_specs=[whole, whole, whole],
        out_specs=[away, away],
        out_shape=[
            jax.ShapeDtypeStruct((rows, channels), BF16),
            jax.ShapeDtypeStruct((heads, HEAD_DIM, share), F32),
        ],
        scratch_shapes=[
            pltpu.VMEM((rows, channels), BF16),
            pltpu.VMEM((heads, HEAD_DIM, share), F32),
            pltpu.SemaphoreType.DMA((1 + rows // SPAN,)),
        ],
        compiler_params=pltpu.CompilerParams(vmem_limit_bytes=16 << 20),
        cost_estimate=pl.CostEstimate(
            flops=4 * rows * channels, bytes_accessed=4 * rows * channels, transcendentals=rows
        ),
    )(gated, gain, final)


EDGE = 16
EDGE_TOKENS = 4
HALF = SPAN // 2
MESH = pl.DeviceIdType.MESH


def leading(n, chunks):
    return chunks + max(0, n - 4)


def pieces(v, parts):
    out = []
    for _ in range(parts):
        out.append(v.astype(BF16))
        v = v - out[-1].astype(F32)
    return out


def split(v, parts):
    return jnp.concatenate([piece.astype(F32) for piece in pieces(v, parts)], axis=1).astype(BF16)


def scan_kernel(
    n,
    x_any,
    taps_any,
    bias_any,
    bc_any,
    taps_bc_any,
    bias_bc_any,
    dt_any,
    dt_bias_any,
    a_log_any,
    skip_any,
    z_any,
    y_ref,
    final_out,
    xc,
    sent,
    merged,
    came,
    later_out,
    later_in,
    fade_out,
    fade_in,
    local,
    exact_ref,
    step_ref,
    cumul_ref,
    row_ref,
    turn_ref,
    tail_ref,
    fade_ref,
    bt_ref,
    c_ref,
    near_ref,
    far_ref,
    kept,
    even,
    mid_ref,
    inside,
    outside,
    raw_ref,
    lift_ref,
    spread_ref,
    wide_ref,
    z_buf,
    x_buf,
    taps_ref,
    bias_ref,
    bc_ref,
    taps_bc_ref,
    bias_bc_ref,
    dt_ref,
    dt_bias_ref,
    a_log_ref,
    skip_ref,
    edge_x,
    edge_bc,
    z_sem,
    x_sem,
    in_sem,
    send_sem,
    recv_sem,
    later_send,
    later_recv,
    fade_send,
    fade_recv,
    edge_send,
    edge_recv,
):
    s = pl.program_id(0)
    chunks = sent.shape[0]
    lead = leading(n, chunks)
    last_step = lead + chunks - 1
    me = lax.axis_index("ctx")
    rows = x_any.shape[0]
    spans = rows // SPAN
    heads = dt_ref.shape[0]
    groups = bt_ref.shape[0]
    per = chunks // groups
    lines = bc_ref.shape[0] // rows
    reach = EDGE_TOKENS * lines
    share = STATE // n
    right = jnp.minimum(me + 1, n - 1)
    left = jnp.maximum(me - 1, 0)
    total = 2 * spans

    def edge_copies():
        ends = [(bc_any, edge_bc, 0, 128), (x_any, edge_x, 0, CHUNK)]
        if chunks > 1:
            ends.append((x_any, edge_x, CHUNK, (chunks - 1) * CHUNK))
        return [
            pltpu.make_async_remote_copy(
                src_ref=whole.at[
                    pl.ds(whole.shape[0] - edge.shape[0], edge.shape[0]), pl.ds(at, size)
                ],
                dst_ref=edge.at[:, pl.ds(at, size)],
                send_sem=edge_send.at[i],
                recv_sem=edge_recv.at[i],
                device_id={"ctx": right},
                device_id_type=MESH,
            )
            for i, (whole, edge, at, size) in enumerate(ends)
        ]

    def onward(c):
        return pltpu.make_async_remote_copy(
            src_ref=merged.at[c],
            dst_ref=came.at[c],
            send_sem=send_sem.at[c],
            recv_sem=recv_sem.at[c],
            device_id={"ctx": right},
            device_id_type=MESH,
        )

    def load(c):
        return pltpu.make_async_copy(
            x_any.at[:, pl.ds(pl.multiple_of(c * CHUNK, CHUNK), CHUNK)],
            x_buf.at[lax.rem(c, 2)],
            x_sem.at[lax.rem(c, 2)],
        )

    early = [
        pltpu.make_async_copy(src, dst, in_sem.at[i])
        for i, (src, dst) in enumerate(
            (
                (dt_any, dt_ref),
                (dt_bias_any, dt_bias_ref),
                (a_log_any, a_log_ref),
                (skip_any, skip_ref),
                (bc_any, bc_ref),
                (taps_bc_any, taps_bc_ref),
                (bias_bc_any, bias_bc_ref),
                (taps_any, taps_ref),
                (bias_any, bias_ref),
            )
        )
    ]

    def fetch(c):
        return pltpu.make_async_copy(
            z_any.at[:, pl.ds(pl.multiple_of(c * CHUNK, CHUNK), CHUNK)],
            z_buf.at[lax.rem(c, 2)],
            z_sem.at[lax.rem(c, 2)],
        )

    def rows_of(q):
        return pl.ds(pl.multiple_of(q * share, share), share)

    def behind(q, c):
        return pltpu.make_async_remote_copy(
            src_ref=later_out.at[c, rows_of(q)],
            dst_ref=later_in.at[c, rows_of(q)],
            send_sem=later_send.at[q, c],
            recv_sem=later_recv.at[q, c],
            device_id={"ctx": left},
            device_id_type=MESH,
        )

    def fading(c):
        return pltpu.make_async_remote_copy(
            src_ref=fade_out.at[c],
            dst_ref=fade_in.at[c],
            send_sem=fade_send.at[c],
            recv_sem=fade_recv.at[c],
            device_id={"ctx": left},
            device_id_type=MESH,
        )

    def spread_of(c):
        shape = (3 * heads, CHUNK)
        return (
            lax.broadcasted_iota(jnp.int32, shape, 1) // HEAD_DIM + c * HEADS_CHUNK
            == lax.broadcasted_iota(jnp.int32, shape, 0) % heads
        ).astype(BF16)

    def project(side, g, over):
        taps = 0.5 * taps_bc_ref[...].astype(F32)
        bias = 0.5 * bias_bc_ref[...]
        lag = taps.shape[0] // lines - 1
        for k in over:
            at = slice(k * SPAN, (k + 1) * SPAN)
            for i in range(STATE // 128):
                line = 2 * (g * (STATE // 128) + i) + side
                own = slice(i * 128, (i + 1) * 128)
                half = bias[line : line + 1]
                for q in range(lag + 1):
                    begin = (k * SPAN + EDGE_TOKENS - lag + q) * lines + line
                    tap = taps[q * lines + line : q * lines + line + 1]
                    half = half + raw_ref[pl.ds(begin, SPAN, stride=lines), :] * tap
                v = half * jnp.tanh(half) + half
                if side == 0:
                    bt_ref[g, own, at] = v.astype(BF16).astype(F32).T.astype(BF16)
                else:
                    c_ref[g, at, own] = v.astype(BF16)

    @pl.when(s == 0)
    def _():
        barrier = pltpu.get_barrier_semaphore()
        for k in range(1, n):
            pl.semaphore_signal(
                barrier, inc=1, device_id={"ctx": lax.rem(me + k, n)}, device_id_type=MESH
            )
        for copy in early:
            copy.start()
        load(0).start()
        for copy in early[:4]:
            copy.wait()
        rate = -LOG2E * jnp.exp(a_log_ref[...])
        above = lax.broadcasted_iota(jnp.int32, (SPAN, SPAN), 0)
        left = lax.broadcasted_iota(jnp.int32, (SPAN, SPAN), 1)
        lower = ((above >= left) & (above // HALF == left // HALF)).astype(BF16)
        lower = jnp.concatenate([lower] * 3, axis=1)
        so_far = jnp.zeros((1, heads), F32)
        fade_ref[...] = jnp.zeros_like(fade_ref)
        ats = [slice(k * SPAN, (k + 1) * SPAN) for k in range(spans)]
        raws = [dt_ref[:, at].T + dt_bias_ref[...] for at in ats]
        steps = [jnp.maximum(v, 0.0) + jnp.log1p(jnp.exp(-jnp.abs(v))) for v in raws]
        cumuls = [dot(lower, jnp.concatenate(pieces(step * rate, 3), axis=0)) for step in steps]
        for k, at in enumerate(ats):
            cumul = cumuls[k]
            step = steps[k]
            ends = cumul[HALF - 1 : HALF], cumul[SPAN - 1 :]
            tail = jnp.concatenate(
                [end - cumul[i * HALF : (i + 1) * HALF] for i, end in enumerate(ends)], axis=0
            )
            exact_ref[at] = cumul
            step_ref[at] = step
            tail_ref[at] = split(jnp.exp2(tail) * step, 2)
            for i in range(2):
                part = 2 * k + i
                fade_ref[part : part + 1] = jnp.exp2(ends[i])
                fade_ref[total + 2 + part : total + 3 + part] = jnp.exp2(so_far)
                so_far = so_far + ends[i]
        fade_ref[2 * spans : 2 * spans + 1] = jnp.exp2(so_far)
        fade_ref[2 * spans + 1 : 2 * spans + 2] = skip_ref[...]
        pl.semaphore_wait(barrier, n - 1)

        @pl.when(me < n - 1)
        def _():
            for copy in edge_copies():
                copy.start()

        for copy in early[4:]:
            copy.wait()
        raw_ref[reach:] = bc_ref[...].astype(F32)
        project(0, 0, range(1, spans))

        @pl.when(me == 0)
        def _():
            edge_x[...] = jnp.zeros_like(edge_x)
            edge_bc[...] = jnp.zeros_like(edge_bc)

        @pl.when(me > 0)
        def _():
            for copy in edge_copies()[:2]:
                copy.wait_recv()

        raw_ref[:reach] = edge_bc[...].astype(F32)
        project(0, 0, range(1))

    def join(c, carry):
        onward(c).wait_recv()
        got = came[c].astype(F32)
        merged[c] = (wide_ref[c, total : total + 1] * got + sent[c].astype(F32)).astype(BF16)

        @pl.when(me < n - 1)
        def _():
            onward(c).start()

        return carry

    def turn_back(c, carry):
        lax.fori_loop(0, me + 1, lambda q, z: (behind(q, c).wait_recv(), z)[1], 0)
        fading(c).wait_recv()

        def add(q, z):
            mine = sent[c, rows_of(q)].astype(F32)
            after = later_in[c, rows_of(q)].astype(F32)
            later_out[c, rows_of(q)] = (fade_in[c, :1] * mine + after).astype(BF16)
            behind(q, c).start()
            return z

        lax.fori_loop(0, me, add, 0)

        @pl.when(me > 0)
        def _():
            fade_out[c] = fade_in[c] * wide_ref[c, total : total + 1]
            fading(c).start()

        return carry

    def close(c, carry):
        there = pl.ds(pl.multiple_of(c * CHUNK, CHUNK), CHUNK)

        @pl.when(me < n - 1)
        def _():
            mine = merged[c, rows_of(me)].astype(F32)
            after = later_in[c, rows_of(jnp.minimum(me, n - 2))].astype(F32)
            final_out[:, there] = (fade_in[c, :1] * mine + after).astype(BF16)

        @pl.when(me == n - 1)
        def _():
            final_out[:, there] = merged[c, STATE - share :]

        return carry

    def each(first, work):
        start = jnp.clip(s - first, 0, chunks)
        stop = jnp.where(s == last_step, chunks, jnp.clip(s - first + 1, 0, chunks))
        lax.fori_loop(start, stop, work, 0)

    join_at = jnp.where(me == 1, 0, jnp.minimum(lead, chunks + me - 2))
    back_at = 2 + 3 * jnp.maximum(n - 2 - me, 0)
    close_at = jnp.maximum(jnp.where(me == 0, 0, join_at), jnp.where(me < n - 1, back_at, 0))

    @pl.when(me < n - 1)
    def _():
        each(back_at, turn_back)

    pairs = HEADS_CHUNK // 2

    def pair_lanes(pair):
        return slice(pair * 2 * HEAD_DIM, (pair + 1) * 2 * HEAD_DIM)

    if chunks > 1:

        @pl.when((s == 1) & (me > 0))
        def _():
            edge_copies()[2].wait_recv()

    @pl.when(s < chunks)
    def _():
        j = s
        bt = bt_ref.at[j // per]
        load(j).wait()

        @pl.when(s < chunks - 1)
        def _():
            load(j + 1).start()

        count = taps_ref.shape[0] // (chunks * CHUNK // 128)
        block = count * CHUNK // 128
        taps = 0.5 * taps_ref[pl.ds(pl.multiple_of(j * block, block), block)].astype(F32)
        bias = 0.5 * bias_ref[:, pl.ds(pl.multiple_of(j * CHUNK, CHUNK), CHUNK)]
        lag = count - 1
        turn = lax.rem(j, 2)
        before = edge_x[:, pl.ds(pl.multiple_of(j * CHUNK, CHUNK), CHUNK)].astype(F32)[EDGE - HALO :]
        spread = spread_of(j)
        spread_ref[j] = spread
        fades = dot(split(fade_ref[...], 3), spread)
        wide_ref[j] = fades
        tiles = [slice(i * 128, (i + 1) * 128) for i in range(CHUNK // 128)]
        for i, lanes in enumerate(tiles):
            lift_ref[i, :HALO] = before[:, lanes]
            lift_ref[i, HALO:] = x_buf[turn, :, lanes].astype(F32)
        inside[...] = dot(tail_ref[...], spread[: 2 * heads])
        state = None
        for k in range(spans):
            at = slice(k * SPAN, (k + 1) * SPAN)
            parts = []
            for i, lanes in enumerate(tiles):
                column = []
                for r in range(0, SPAN, HALF):
                    first = k * SPAN + r
                    half = bias[:, lanes]
                    for q in range(lag + 1):
                        begin = HALO - lag + q + first
                        half = half + lift_ref[i, begin : begin + HALF] * taps[i * count + q : i * count + q + 1]
                    value = half * jnp.tanh(half) + half
                    xc[j, first : first + HALF, lanes] = value.astype(BF16)
                    column.append(value * inside[first : first + HALF, lanes])
                parts.append(column)
            scaled = jnp.concatenate([column[1] for column in parts], axis=1).astype(BF16)
            first = jnp.concatenate([column[0] for column in parts], axis=1)
            kept[j, k] = first.astype(BF16)
            first = (first * fades[2 * k + 1 : 2 * k + 2]).astype(BF16)
            scaled = jnp.concatenate([first, scaled], axis=0)
            if k % 2 == 0:
                even[j, k // 2] = scaled
                row = jnp.broadcast_to(
                    fades[2 * k + 2 : 2 * k + 3] * fades[2 * k + 3 : 2 * k + 4], (16, CHUNK)
                ).astype(BF16)[None]
                held = (scaled.reshape(SPAN // 16, 16, CHUNK) * row).reshape(SPAN, CHUNK)
                continue
            scaled = jnp.concatenate([held, scaled], axis=0)
            at = slice((k - 1) * SPAN, (k + 1) * SPAN)
            part = dot(bt[:, at], scaled)
            if state is not None:
                local[j, k // 2 - 1] = state.astype(BF16)
                row = fades[2 * k - 2 : 2 * k - 1]
                for i in range(1, 4):
                    row = row * fades[2 * k - 2 + i : 2 * k - 1 + i]
                part = row * state + part
            state = part
        state = state.astype(BF16)
        sent[j] = state

        @pl.when(me == 0)
        def _():
            merged[j] = state
            onward(j).start()

        @pl.when(me == n - 1)
        def _():
            later_out[j] = state[: STATE - share]
            fade_out[j] = jnp.broadcast_to(fades[total : total + 1], (8, CHUNK))
            lax.fori_loop(0, n - 1, lambda q, z: (behind(q, j).start(), z)[1], 0)
            fading(j).start()

    @pl.when(s == 0)
    def _():
        for g in range(1, groups):
            project(0, g, range(spans))
        project(1, 0, range(spans))

    @pl.when(s == 1)
    def _():
        fetch(0).start()
        for g in range(1, groups):
            project(1, g, range(spans))
        causal = lax.broadcasted_iota(jnp.int32, (HALF, SPAN), 0) >= (
            lax.broadcasted_iota(jnp.int32, (HALF, SPAN), 1) % HALF
        )
        for g in range(groups):
            for k in range(spans):
                at = slice(k * SPAN, (k + 1) * SPAN)
                scores = dot(c_ref[g, at], bt_ref[g, :, at])
                if k % 2:
                    prior = bt_ref[g, :, (k - 1) * SPAN : k * SPAN]
                    mid_ref[g, (k // 2) * SPAN : (k // 2 + 1) * SPAN] = dot(
                        c_ref[g, at], prior
                    ).astype(BF16)
                for i in range(2):
                    own = slice(i * HALF, (i + 1) * HALF)
                    near = jnp.concatenate([scores[own, own]] * 2, axis=1)
                    near_ref[g, k * SPAN + i * HALF : k * SPAN + (i + 1) * HALF] = jnp.where(
                        causal, near, 0.0
                    )
                far_ref[g, k * HALF : (k + 1) * HALF] = scores[HALF:, :HALF].astype(BF16)
        for k in range(spans):
            at = slice(k * SPAN, (k + 1) * SPAN)
            cumul_ref[at] = split(exact_ref[at], 3)
            rowed = exact_ref[at] - jnp.log2(step_ref[at])
            wide = jnp.concatenate([rowed] * (128 // heads), axis=1) if heads < 128 else rowed
            turn_ref[...] = wide.T[:heads]
            first = turn_ref[pl.ds(0, heads // 2, stride=2), :]
            second = turn_ref[pl.ds(1, heads // 2, stride=2), :]
            for i in range(2):
                own = slice(i * HALF, (i + 1) * HALF)
                pairs_row = jnp.concatenate([first[:, own], second[:, own]], axis=1)
                for c in range(chunks):
                    row_ref[c, :, (2 * k + i) * SPAN : (2 * k + i + 1) * SPAN] = pairs_row[
                        c * (HEADS_CHUNK // 2) : (c + 1) * (HEADS_CHUNK // 2)
                    ]

        @pl.when(me == 0)
        def _():
            came[...] = jnp.zeros_like(came)

    @pl.when(s >= lead)
    def _():
        j = s - lead
        fetch(j).wait()

        @pl.when(s < last_step)
        def _():
            fetch(j + 1).start()

        slot = lax.rem(j, 2)
        fades = wide_ref[j]
        spread = spread_ref[j]
        g = j // per
        none = jnp.zeros((), BF16)
        low = lax.broadcasted_iota(jnp.int32, (HALF, 2 * HEAD_DIM), 1) < HEAD_DIM

        outside[...] = dot(cumul_ref[...], spread)
        for k in range(spans):
            at = slice(k * SPAN, (k + 1) * SPAN)
            carried = None
            if k > 1:
                if k % 2 == 0:
                    both = slice(k * SPAN, (k + 2) * SPAN)
                    inside[both] = dot(c_ref[g, both], local[j, k // 2 - 1])
                carried = inside[at]
            if k % 2:
                prior = dot(mid_ref[g, (k // 2) * SPAN : (k // 2 + 1) * SPAN], even[j, k // 2])
                if carried is not None:
                    prior = prior + carried * (
                        fades[2 * k - 2 : 2 * k - 1] * fades[2 * k - 1 : 2 * k]
                    )
                carried = prior
            beside = dot(far_ref[g, k * HALF : (k + 1) * HALF], kept[j, k])
            for i in range(2):
                mine = slice(i * HALF, (i + 1) * HALF)
                there = slice(k * SPAN + i * HALF, k * SPAN + (i + 1) * HALF)
                near = near_ref[g, there]
                before = None if carried is None else carried[mine]
                if i == 1:
                    before = beside if before is None else beside + before * fades[2 * k : 2 * k + 1]
                so_far = fades[total + 2 + 2 * k + i : total + 3 + 2 * k + i]
                for pair in range(pairs):
                    lanes = pair_lanes(pair)
                    away = outside[there, lanes]
                    spacing = away - row_ref[
                        j, pair : pair + 1, (2 * k + i) * SPAN : (2 * k + i + 1) * SPAN
                    ]
                    weights = (jnp.exp2(jnp.minimum(spacing, 64.0)) * near).astype(BF16)
                    x_pair = xc[j, there, lanes]
                    stacked = jnp.concatenate(
                        [jnp.where(low, x_pair, none), jnp.where(low, none, x_pair)], axis=0
                    )
                    within = dot(weights, stacked) + x_pair.astype(F32) * fades[
                        total + 1 : total + 2, lanes
                    ]
                    half = (0.5 * z_buf[slot, there, lanes]).astype(F32)
                    gate = half * jnp.tanh(half) + half
                    entry = jnp.exp2(away)
                    if before is not None:
                        within = within + entry * before[:, lanes]
                    inside[there, lanes] = within * gate
                    outside[there, lanes] = entry * gate * so_far[:, lanes]

    @pl.when(me > 0)
    def _():
        each(join_at, join)

    each(close_at, close)

    @pl.when(s >= lead)
    def _():
        j = s - lead
        g = j // per
        own = pl.ds(pl.multiple_of(j * CHUNK, CHUNK), CHUNK)
        readout = dot(c_ref[g], came[j])
        y_ref[:, own] = (inside[...] + outside[...] * readout).astype(BF16)

    @pl.when(s == last_step)
    def _():
        @pl.when(me < n - 1)
        def _():
            for copy in edge_copies():
                copy.wait_send()
            for c in range(chunks):
                onward(c).wait_send()

        @pl.when(me > 0)
        def _():
            for c in range(chunks):
                lax.fori_loop(0, me, lambda q, z: (behind(q, c).wait_send(), z)[1], 0)
                fading(c).wait_send()


def scan(n, x, taps, bias, bc, taps_bc, bias_bc, dt, dt_bias, a_log, skip, z, groups):
    rows, channels = x.shape
    chunks = channels // CHUNK
    heads = dt.shape[0]
    lead = leading(n, chunks)
    lines = bc.shape[0] // rows
    fade_rows = -(-(4 * (rows // SPAN) + 2) // 8) * 8
    share = STATE // n
    spans = rows // SPAN
    return pl.pallas_call(
        functools.partial(scan_kernel, n),
        grid=(lead + chunks,),
        in_specs=[pl.BlockSpec(memory_space=pl.ANY)] * 11,
        out_specs=[
            pl.BlockSpec(memory_space=pltpu.VMEM),
            pl.BlockSpec(memory_space=pltpu.VMEM),
        ],
        out_shape=[
            pltpu.VMEM((rows, channels), BF16),
            pltpu.VMEM((share, channels), BF16),
        ],
        scratch_shapes=[
            pltpu.VMEM((chunks, rows, CHUNK), BF16),
            pltpu.VMEM((chunks, STATE, CHUNK), BF16),
            pltpu.VMEM((chunks, STATE, CHUNK), BF16),
            pltpu.VMEM((chunks, STATE, CHUNK), BF16),
            pltpu.VMEM((chunks, STATE - share, CHUNK), BF16),
            pltpu.VMEM((chunks, STATE - share, CHUNK), BF16),
            pltpu.VMEM((chunks, 8, CHUNK), F32),
            pltpu.VMEM((chunks, 8, CHUNK), F32),
            pltpu.VMEM((chunks, max(spans // 2 - 1, 1), STATE, CHUNK), BF16),
            pltpu.VMEM((rows, heads), F32),
            pltpu.VMEM((rows, heads), F32),
            pltpu.VMEM((rows, 3 * heads), BF16),
            pltpu.VMEM((chunks, HEADS_CHUNK // 2, 2 * rows), F32),
            pltpu.VMEM((heads, SPAN), F32),
            pltpu.VMEM((rows, 2 * heads), BF16),
            pltpu.VMEM((fade_rows, heads), F32),
            pltpu.VMEM((groups, STATE, rows), BF16),
            pltpu.VMEM((groups, rows, STATE), BF16),
            pltpu.VMEM((groups, rows, SPAN), F32),
            pltpu.VMEM((groups, rows // 2, HALF), BF16),
            pltpu.VMEM((chunks, spans, HALF, CHUNK), BF16),
            pltpu.VMEM((chunks, spans // 2, SPAN, CHUNK), BF16),
            pltpu.VMEM((groups, rows // 2, SPAN), BF16),
            pltpu.VMEM((rows, CHUNK), F32),
            pltpu.VMEM((rows, CHUNK), F32),
            pltpu.VMEM(((EDGE_TOKENS + rows) * lines, 128), F32),
            pltpu.VMEM((CHUNK // 128, HALO + rows, 128), F32),
            pltpu.VMEM((chunks, 3 * heads, CHUNK), BF16),
            pltpu.VMEM((chunks, fade_rows, CHUNK), F32),
            pltpu.VMEM((2, rows, CHUNK), BF16),
            pltpu.VMEM((2, rows, CHUNK), BF16),
            pltpu.VMEM(taps.shape, BF16),
            pltpu.VMEM(bias.shape, F32),
            pltpu.VMEM(bc.shape, BF16),
            pltpu.VMEM(taps_bc.shape, BF16),
            pltpu.VMEM(bias_bc.shape, F32),
            pltpu.VMEM(dt.shape, F32),
            pltpu.VMEM(dt_bias.shape, F32),
            pltpu.VMEM(a_log.shape, F32),
            pltpu.VMEM(skip.shape, F32),
            pltpu.VMEM((EDGE, channels), BF16),
            pltpu.VMEM((EDGE_TOKENS * lines, 128), BF16),
            pltpu.SemaphoreType.DMA((2,)),
            pltpu.SemaphoreType.DMA((2,)),
            pltpu.SemaphoreType.DMA((9,)),
            pltpu.SemaphoreType.DMA((chunks,)),
            pltpu.SemaphoreType.DMA((chunks,)),
            pltpu.SemaphoreType.DMA((n - 1, chunks)),
            pltpu.SemaphoreType.DMA((n - 1, chunks)),
            pltpu.SemaphoreType.DMA((chunks,)),
            pltpu.SemaphoreType.DMA((chunks,)),
            pltpu.SemaphoreType.DMA((3,)),
            pltpu.SemaphoreType.DMA((3,)),
        ],
        compiler_params=pltpu.CompilerParams(
            dimension_semantics=("arbitrary",),
            vmem_limit_bytes=56 << 20,
            collective_id=0,
            has_side_effects=True,
        ),
        cost_estimate=pl.CostEstimate(
            flops=20 * rows * channels * STATE, bytes_accessed=4 * rows * channels, transcendentals=4 * rows * channels
        ),
    )(x, taps, bias, bc, taps_bc, bias_bc, dt, dt_bias, a_log, skip, z)


def per_device(
    x_in,
    bc_in,
    z_in,
    dt_raw,
    conv_x,
    conv_bc,
    conv_bias_x,
    conv_bias_bc,
    dt_bias,
    a_log,
    d_skip,
    norm_gain,
):
    rows, channels = x_in.shape
    heads = dt_raw.shape[1]
    n = lax.axis_size("ctx")
    tiles = bc_in.shape[2] // 128
    groups = bc_in.shape[2] // STATE

    def lined(v):
        return v.reshape(-1, 2, tiles, 128).transpose(0, 2, 1, 3).reshape(-1, 128)

    gated, final = scan(
        n,
        x_in,
        conv_x.reshape(-1, channels // 128, 128).transpose(1, 0, 2).reshape(-1, 128),
        conv_bias_x[None],
        lined(bc_in),
        lined(conv_bc),
        lined(conv_bias_bc),
        dt_raw.T,
        dt_bias[None],
        a_log[None],
        d_skip[None],
        z_in,
        groups,
    )
    return tuple(finish(gated, norm_gain[None], final, groups))


def solution(mesh):
    in_specs = (
        P(("group", "ctx"), "tp"),
        P(("group", "ctx"), None, "tp"),
        P(("group", "ctx"), "tp"),
        P(("group", "ctx"), "tp"),
        P(None, "tp"),
        P(None, None, "tp"),
        P("tp"),
        P(None, "tp"),
        P("tp"),
        P("tp"),
        P("tp"),
        P("tp"),
    )
    out_specs = (P(("group", "ctx"), "tp"), P(("group", "tp"), None, "ctx"))
    return jax.shard_map(
        per_device, mesh=mesh, in_specs=in_specs, out_specs=out_specs, check_vma=False
    )
```

```python
import functools
import math

import jax
import jax.numpy as jnp
from jax import lax
from jax.experimental import pallas as pl
from jax.experimental.pallas import tpu as pltpu
from jax.sharding import PartitionSpec as P

HEAD_DIM = 64
STATE = 256
SPAN = 128
HALF = SPAN // 2
CHUNK = 512
HEADS_CHUNK = CHUNK // HEAD_DIM
HALO = 8
LOG2E = math.log2(math.e)

eps = 1e-05
F32 = jnp.float32
BF16 = jnp.bfloat16


def dot(a, b):
    return jnp.dot(a, b, preferred_element_type=F32)


def rescaled(gated, gain):
    gated = gated.astype(F32)
    meansq = jnp.mean(gated * gated, axis=-1, keepdims=True)
    return (gated * lax.rsqrt(meansq + eps) * gain).astype(BF16)


def finish_kernel(groups, gated_ref, gain_ref, final_ref, out_any, state_any, mixed, turned, sems):
    rows, channels = gated_ref.shape
    width = channels // groups
    blocks = rows // SPAN
    part = CHUNK // HEAD_DIM
    for c in range(channels // CHUNK):
        block = final_ref[:, c * CHUNK : (c + 1) * CHUNK].astype(F32).T
        turned[c * part : (c + 1) * part] = block.reshape(part, HEAD_DIM, block.shape[1])
    copies = [pltpu.make_async_copy(turned, state_any, sems.at[blocks])]
    copies[-1].start()
    for b in range(blocks):
        at = slice(b * SPAN, (b + 1) * SPAN)
        for g in range(groups):
            own = slice(g * width, (g + 1) * width)
            mixed[at, own] = rescaled(gated_ref[at, own], gain_ref[:, own])
        there = pl.ds(b * SPAN, SPAN)
        copies.append(pltpu.make_async_copy(mixed.at[there], out_any.at[there], sems.at[b]))
        copies[-1].start()
    for copy in copies:
        copy.wait()


def finish(gated, gain, final, groups):
    rows, channels = gated.shape
    share = final.shape[0]
    heads = channels // HEAD_DIM
    whole = pl.BlockSpec(memory_space=pltpu.VMEM)
    away = pl.BlockSpec(memory_space=pl.ANY)
    return pl.pallas_call(
        functools.partial(finish_kernel, groups),
        in_specs=[whole, whole, whole],
        out_specs=[away, away],
        out_shape=[
            jax.ShapeDtypeStruct((rows, channels), BF16),
            jax.ShapeDtypeStruct((heads, HEAD_DIM, share), F32),
        ],
        scratch_shapes=[
            pltpu.VMEM((rows, channels), BF16),
            pltpu.VMEM((heads, HEAD_DIM, share), F32),
            pltpu.SemaphoreType.DMA((1 + rows // SPAN,)),
        ],
        compiler_params=pltpu.CompilerParams(vmem_limit_bytes=16 << 20),
        cost_estimate=pl.CostEstimate(
            flops=4 * rows * channels, bytes_accessed=4 * rows * channels, transcendentals=rows
        ),
    )(gated, gain, final)


EDGE = 16
EDGE_TOKENS = 4
PARTS = 2
MESH = pl.DeviceIdType.MESH


def leading(n, chunks):
    return chunks + max(0, n - 4)


def pieces(v, parts):
    out = []
    for _ in range(parts):
        out.append(v.astype(BF16))
        v = v - out[-1].astype(F32)
    return out


def split(v, parts):
    return jnp.concatenate([piece.astype(F32) for piece in pieces(v, parts)], axis=1).astype(BF16)


def scan_kernel(
    n,
    x_any,
    taps_any,
    bias_any,
    bc_any,
    taps_bc_any,
    bias_bc_any,
    dt_any,
    dt_bias_any,
    a_log_any,
    skip_any,
    z_any,
    y_ref,
    final_out,
    xc,
    sent,
    merged,
    came,
    later_out,
    later_in,
    fade_out,
    fade_in,
    local,
    exact_ref,
    step_ref,
    cumul_ref,
    row_ref,
    turn_ref,
    tail_ref,
    fade_ref,
    bt_ref,
    c_ref,
    near_ref,
    far_ref,
    kept,
    even,
    mid_ref,
    inside,
    outside,
    raw_ref,
    lift_ref,
    spread_ref,
    wide_ref,
    z_buf,
    x_buf,
    taps_ref,
    bias_ref,
    bc_ref,
    taps_bc_ref,
    bias_bc_ref,
    dt_ref,
    dt_bias_ref,
    a_log_ref,
    skip_ref,
    edge_x,
    edge_bc,
    z_sem,
    x_sem,
    in_sem,
    send_sem,
    recv_sem,
    later_send,
    later_recv,
    fade_send,
    fade_recv,
    edge_send,
    edge_recv,
):
    s = pl.program_id(0)
    chunks = sent.shape[0]
    lead = leading(n, chunks)
    last_step = lead + chunks - 1
    me = lax.axis_index("ctx")
    rows = x_any.shape[0]
    spans = rows // SPAN
    heads = dt_ref.shape[0]
    groups = bt_ref.shape[0]
    per = chunks // groups
    lines = bc_ref.shape[0] // rows
    reach = EDGE_TOKENS * lines
    share = STATE // n
    right = jnp.minimum(me + 1, n - 1)
    left = jnp.maximum(me - 1, 0)
    total = 2 * spans

    def edge_copies():
        ends = [(bc_any, edge_bc, 0, 128), (x_any, edge_x, 0, CHUNK)]
        if chunks > 1:
            ends.append((x_any, edge_x, CHUNK, (chunks - 1) * CHUNK))
        return [
            pltpu.make_async_remote_copy(
                src_ref=whole.at[
                    pl.ds(whole.shape[0] - edge.shape[0], edge.shape[0]), pl.ds(at, size)
                ],
                dst_ref=edge.at[:, pl.ds(at, size)],
                send_sem=edge_send.at[i],
                recv_sem=edge_recv.at[i],
                device_id={"ctx": right},
                device_id_type=MESH,
            )
            for i, (whole, edge, at, size) in enumerate(ends)
        ]

    piece = STATE // PARTS

    def onward(c, p):
        return pltpu.make_async_remote_copy(
            src_ref=merged.at[c, pl.ds(p * piece, piece)],
            dst_ref=came.at[c, pl.ds(p * piece, piece)],
            send_sem=send_sem.at[p, c],
            recv_sem=recv_sem.at[p, c],
            device_id={"ctx": right},
            device_id_type=MESH,
        )

    def load(c):
        return pltpu.make_async_copy(
            x_any.at[:, pl.ds(pl.multiple_of(c * CHUNK, CHUNK), CHUNK)],
            x_buf.at[lax.rem(c, 2)],
            x_sem.at[lax.rem(c, 2)],
        )

    early = [
        pltpu.make_async_copy(src, dst, in_sem.at[i])
        for i, (src, dst) in enumerate(
            (
                (dt_any, dt_ref),
                (dt_bias_any, dt_bias_ref),
                (a_log_any, a_log_ref),
                (skip_any, skip_ref),
                (bc_any, bc_ref),
                (taps_bc_any, taps_bc_ref),
                (bias_bc_any, bias_bc_ref),
                (taps_any, taps_ref),
                (bias_any, bias_ref),
            )
        )
    ]

    def fetch(c):
        return pltpu.make_async_copy(
            z_any.at[:, pl.ds(pl.multiple_of(c * CHUNK, CHUNK), CHUNK)],
            z_buf.at[lax.rem(c, 2)],
            z_sem.at[lax.rem(c, 2)],
        )

    def rows_of(q):
        return pl.ds(pl.multiple_of(q * share, share), share)

    def behind(q, c):
        return pltpu.make_async_remote_copy(
            src_ref=later_out.at[c, rows_of(q)],
            dst_ref=later_in.at[c, rows_of(q)],
            send_sem=later_send.at[q, c],
            recv_sem=later_recv.at[q, c],
            device_id={"ctx": left},
            device_id_type=MESH,
        )

    def fading(c):
        return pltpu.make_async_remote_copy(
            src_ref=fade_out.at[c],
            dst_ref=fade_in.at[c],
            send_sem=fade_send.at[c],
            recv_sem=fade_recv.at[c],
            device_id={"ctx": left},
            device_id_type=MESH,
        )

    def spread_of(c):
        shape = (3 * heads, CHUNK)
        return (
            lax.broadcasted_iota(jnp.int32, shape, 1) // HEAD_DIM + c * HEADS_CHUNK
            == lax.broadcasted_iota(jnp.int32, shape, 0) % heads
        ).astype(BF16)

    def project(side, g, over):
        taps = 0.5 * taps_bc_ref[...].astype(F32)
        bias = 0.5 * bias_bc_ref[...]
        lag = taps.shape[0] // lines - 1
        for k in over:
            at = slice(k * SPAN, (k + 1) * SPAN)
            for i in range(STATE // 128):
                line = 2 * (g * (STATE // 128) + i) + side
                own = slice(i * 128, (i + 1) * 128)
                half = bias[line : line + 1]
                for q in range(lag + 1):
                    begin = (k * SPAN + EDGE_TOKENS - lag + q) * lines + line
                    tap = taps[q * lines + line : q * lines + line + 1]
                    half = half + raw_ref[pl.ds(begin, SPAN, stride=lines), :] * tap
                v = half * jnp.tanh(half) + half
                if side == 0:
                    bt_ref[g, own, at] = v.astype(BF16).astype(F32).T.astype(BF16)
                else:
                    c_ref[g, at, own] = v.astype(BF16)

    @pl.when(s == 0)
    def _():
        barrier = pltpu.get_barrier_semaphore()

        @pl.when(me > 0)
        def _():
            pl.semaphore_signal(barrier, inc=1, device_id={"ctx": left}, device_id_type=MESH)

        @pl.when(me < n - 1)
        def _():
            pl.semaphore_signal(barrier, inc=1, device_id={"ctx": right}, device_id_type=MESH)

        for copy in early:
            copy.start()
        load(0).start()
        for copy in early[:4]:
            copy.wait()
        rate = -LOG2E * jnp.exp(a_log_ref[...])
        above = lax.broadcasted_iota(jnp.int32, (SPAN, SPAN), 0)
        across = lax.broadcasted_iota(jnp.int32, (SPAN, SPAN), 1)
        lower = ((above >= across) & (above // HALF == across // HALF)).astype(BF16)
        lower = jnp.concatenate([lower] * 3, axis=1)
        so_far = jnp.zeros((1, heads), F32)
        fade_ref[...] = jnp.zeros_like(fade_ref)
        ats = [slice(k * SPAN, (k + 1) * SPAN) for k in range(spans)]
        raws = [dt_ref[:, at].T + dt_bias_ref[...] for at in ats]
        steps = [jnp.maximum(v, 0.0) + jnp.log1p(jnp.exp(-jnp.abs(v))) for v in raws]
        cumuls = [dot(lower, jnp.concatenate(pieces(step * rate, 3), axis=0)) for step in steps]
        for k, at in enumerate(ats):
            cumul = cumuls[k]
            step = steps[k]
            ends = cumul[HALF - 1 : HALF], cumul[SPAN - 1 :]
            tail = jnp.concatenate(
                [end - cumul[i * HALF : (i + 1) * HALF] for i, end in enumerate(ends)], axis=0
            )
            exact_ref[at] = cumul
            step_ref[at] = step
            tail_ref[at] = split(jnp.exp2(tail) * step, 2)
            for i in range(2):
                part = 2 * k + i
                fade_ref[part : part + 1] = jnp.exp2(ends[i])
                fade_ref[total + 2 + part : total + 3 + part] = jnp.exp2(so_far)
                so_far = so_far + ends[i]
        fade_ref[2 * spans : 2 * spans + 1] = jnp.exp2(so_far)
        fade_ref[2 * spans + 1 : 2 * spans + 2] = skip_ref[...]
        pl.semaphore_wait(barrier, jnp.where((me == 0) | (me == n - 1), 1, 2))

        @pl.when(me < n - 1)
        def _():
            for copy in edge_copies():
                copy.start()

        for copy in early[4:]:
            copy.wait()
        raw_ref[reach:] = bc_ref[...].astype(F32)
        project(0, 0, range(1, spans))

        @pl.when(me == 0)
        def _():
            edge_x[...] = jnp.zeros_like(edge_x)
            edge_bc[...] = jnp.zeros_like(edge_bc)

        @pl.when(me > 0)
        def _():
            for copy in edge_copies()[:2]:
                copy.wait_recv()

        raw_ref[:reach] = edge_bc[...].astype(F32)
        project(0, 0, range(1))

    def join(c, carry):
        fade = wide_ref[c, total : total + 1]
        for p in range(PARTS):
            own = slice(p * piece, (p + 1) * piece)
            onward(c, p).wait_recv()
            got = came[c, own].astype(F32)
            merged[c, own] = (fade * got + sent[c, own].astype(F32)).astype(BF16)

            @pl.when(me < n - 1)
            def _(p=p):
                onward(c, p).start()

        return carry

    def turn_back(c, carry):
        lax.fori_loop(0, me + 1, lambda q, z: (behind(q, c).wait_recv(), z)[1], 0)
        fading(c).wait_recv()

        def add(q, z):
            mine = sent[c, rows_of(q)].astype(F32)
            after = later_in[c, rows_of(q)].astype(F32)
            later_out[c, rows_of(q)] = (fade_in[c, :1] * mine + after).astype(BF16)
            behind(q, c).start()
            return z

        lax.fori_loop(0, me, add, 0)

        @pl.when(me > 0)
        def _():
            fade_out[c] = fade_in[c] * wide_ref[c, total : total + 1]
            fading(c).start()

        return carry

    def close(c, carry):
        there = pl.ds(pl.multiple_of(c * CHUNK, CHUNK), CHUNK)

        @pl.when(me < n - 1)
        def _():
            mine = merged[c, rows_of(me)].astype(F32)
            after = later_in[c, rows_of(jnp.minimum(me, n - 2))].astype(F32)
            final_out[:, there] = (fade_in[c, :1] * mine + after).astype(BF16)

        @pl.when(me == n - 1)
        def _():
            final_out[:, there] = merged[c, STATE - share :]

        return carry

    def each(first, work):
        start = jnp.clip(s - first, 0, chunks)
        stop = jnp.where(s == last_step, chunks, jnp.clip(s - first + 1, 0, chunks))
        lax.fori_loop(start, stop, work, 0)

    join_at = jnp.where(me == 1, 0, jnp.minimum(lead, chunks + me - 2))
    back_at = 2 + 3 * jnp.maximum(n - 2 - me, 0)
    close_at = jnp.maximum(jnp.where(me == 0, 0, join_at), jnp.where(me < n - 1, back_at, 0))

    @pl.when(me < n - 1)
    def _():
        each(back_at, turn_back)

    pairs = HEADS_CHUNK // 2

    def pair_lanes(pair):
        return slice(pair * 2 * HEAD_DIM, (pair + 1) * 2 * HEAD_DIM)

    if chunks > 1:

        @pl.when((s == 1) & (me > 0))
        def _():
            edge_copies()[2].wait_recv()

    @pl.when(s < chunks)
    def _():
        j = s
        bt = bt_ref.at[j // per]
        load(j).wait()

        @pl.when(s < chunks - 1)
        def _():
            load(j + 1).start()

        count = taps_ref.shape[0] // (chunks * CHUNK // 128)
        block = count * CHUNK // 128
        taps = 0.5 * taps_ref[pl.ds(pl.multiple_of(j * block, block), block)].astype(F32)
        bias = 0.5 * bias_ref[:, pl.ds(pl.multiple_of(j * CHUNK, CHUNK), CHUNK)]
        lag = count - 1
        turn = lax.rem(j, 2)
        before = edge_x[:, pl.ds(pl.multiple_of(j * CHUNK, CHUNK), CHUNK)].astype(F32)[EDGE - HALO :]
        spread = spread_of(j)
        spread_ref[j] = spread
        fades = dot(split(fade_ref[...], 3), spread)
        wide_ref[j] = fades
        tiles = [slice(i * 128, (i + 1) * 128) for i in range(CHUNK // 128)]
        for i, lanes in enumerate(tiles):
            lift_ref[i, :HALO] = before[:, lanes]
            lift_ref[i, HALO:] = x_buf[turn, :, lanes].astype(F32)
        inside[...] = dot(tail_ref[...], spread[: 2 * heads])
        state = None
        for k in range(spans):
            at = slice(k * SPAN, (k + 1) * SPAN)
            parts = []
            for i, lanes in enumerate(tiles):
                column = []
                for r in range(0, SPAN, HALF):
                    first = k * SPAN + r
                    half = bias[:, lanes]
                    for q in range(lag + 1):
                        begin = HALO - lag + q + first
                        half = half + lift_ref[i, begin : begin + HALF] * taps[i * count + q : i * count + q + 1]
                    value = half * jnp.tanh(half) + half
                    xc[j, first : first + HALF, lanes] = value.astype(BF16)
                    column.append(value * inside[first : first + HALF, lanes])
                parts.append(column)
            scaled = jnp.concatenate([column[1] for column in parts], axis=1).astype(BF16)
            first = jnp.concatenate([column[0] for column in parts], axis=1)
            kept[j, k] = first.astype(BF16)
            first = (first * fades[2 * k + 1 : 2 * k + 2]).astype(BF16)
            scaled = jnp.concatenate([first, scaled], axis=0)
            if k % 2 == 0:
                even[j, k // 2] = scaled
                row = jnp.broadcast_to(
                    fades[2 * k + 2 : 2 * k + 3] * fades[2 * k + 3 : 2 * k + 4], (16, CHUNK)
                ).astype(BF16)[None]
                held = (scaled.reshape(SPAN // 16, 16, CHUNK) * row).reshape(SPAN, CHUNK)
                continue
            scaled = jnp.concatenate([held, scaled], axis=0)
            at = slice((k - 1) * SPAN, (k + 1) * SPAN)
            part = dot(bt[:, at], scaled)
            if state is not None:
                local[j, k // 2 - 1] = state.astype(BF16)
                row = fades[2 * k - 2 : 2 * k - 1]
                for i in range(1, 4):
                    row = row * fades[2 * k - 2 + i : 2 * k - 1 + i]
                part = row * state + part
            state = part
        state = state.astype(BF16)
        sent[j] = state

        @pl.when(me == 0)
        def _():
            merged[j] = state
            for p in range(PARTS):
                onward(j, p).start()

        @pl.when(me == n - 1)
        def _():
            later_out[j] = state[: STATE - share]
            fade_out[j] = jnp.broadcast_to(fades[total : total + 1], (8, CHUNK))
            lax.fori_loop(0, n - 1, lambda q, z: (behind(q, j).start(), z)[1], 0)
            fading(j).start()

    @pl.when(s == 2)
    def _():
        for g in range(1, groups):
            project(0, g, range(spans))
        project(1, 0, range(spans))

    @pl.when(s == 3)
    def _():
        fetch(0).start()
        for g in range(1, groups):
            project(1, g, range(spans))
        causal = lax.broadcasted_iota(jnp.int32, (HALF, SPAN), 0) >= (
            lax.broadcasted_iota(jnp.int32, (HALF, SPAN), 1) % HALF
        )
        for g in range(groups):
            for k in range(spans):
                at = slice(k * SPAN, (k + 1) * SPAN)
                scores = dot(c_ref[g, at], bt_ref[g, :, at])
                if k % 2:
                    prior = bt_ref[g, :, (k - 1) * SPAN : k * SPAN]
                    mid_ref[g, (k // 2) * SPAN : (k // 2 + 1) * SPAN] = dot(
                        c_ref[g, at], prior
                    ).astype(BF16)
                for i in range(2):
                    own = slice(i * HALF, (i + 1) * HALF)
                    near = jnp.concatenate([scores[own, own]] * 2, axis=1)
                    near_ref[g, k * SPAN + i * HALF : k * SPAN + (i + 1) * HALF] = jnp.where(
                        causal, near, 0.0
                    )
                far_ref[g, k * HALF : (k + 1) * HALF] = scores[HALF:, :HALF].astype(BF16)
        for k in range(spans):
            at = slice(k * SPAN, (k + 1) * SPAN)
            cumul_ref[at] = split(exact_ref[at], 3)
            rowed = exact_ref[at] - jnp.log2(step_ref[at])
            wide = jnp.concatenate([rowed] * (128 // heads), axis=1) if heads < 128 else rowed
            turn_ref[...] = wide.T[:heads]
            first = turn_ref[pl.ds(0, heads // 2, stride=2), :]
            second = turn_ref[pl.ds(1, heads // 2, stride=2), :]
            for i in range(2):
                own = slice(i * HALF, (i + 1) * HALF)
                pairs_row = jnp.concatenate([first[:, own], second[:, own]], axis=1)
                for c in range(chunks):
                    row_ref[c, :, (2 * k + i) * SPAN : (2 * k + i + 1) * SPAN] = pairs_row[
                        c * (HEADS_CHUNK // 2) : (c + 1) * (HEADS_CHUNK // 2)
                    ]

        @pl.when(me == 0)
        def _():
            came[...] = jnp.zeros_like(came)

    @pl.when(s >= lead)
    def _():
        j = s - lead
        fetch(j).wait()

        @pl.when(s < last_step)
        def _():
            fetch(j + 1).start()

        slot = lax.rem(j, 2)
        fades = wide_ref[j]
        spread = spread_ref[j]
        g = j // per
        none = jnp.zeros((), BF16)
        low = lax.broadcasted_iota(jnp.int32, (HALF, 2 * HEAD_DIM), 1) < HEAD_DIM

        outside[...] = dot(cumul_ref[...], spread)
        for k in range(spans):
            at = slice(k * SPAN, (k + 1) * SPAN)
            carried = None
            if k > 1:
                if k % 2 == 0:
                    both = slice(k * SPAN, (k + 2) * SPAN)
                    inside[both] = dot(c_ref[g, both], local[j, k // 2 - 1])
                carried = inside[at]
            if k % 2:
                prior = dot(mid_ref[g, (k // 2) * SPAN : (k // 2 + 1) * SPAN], even[j, k // 2])
                if carried is not None:
                    prior = prior + carried * (
                        fades[2 * k - 2 : 2 * k - 1] * fades[2 * k - 1 : 2 * k]
                    )
                carried = prior
            beside = dot(far_ref[g, k * HALF : (k + 1) * HALF], kept[j, k])
            for i in range(2):
                mine = slice(i * HALF, (i + 1) * HALF)
                there = slice(k * SPAN + i * HALF, k * SPAN + (i + 1) * HALF)
                near = near_ref[g, there]
                before = None if carried is None else carried[mine]
                if i == 1:
                    before = beside if before is None else beside + before * fades[2 * k : 2 * k + 1]
                so_far = fades[total + 2 + 2 * k + i : total + 3 + 2 * k + i]
                for pair in range(pairs):
                    lanes = pair_lanes(pair)
                    away = outside[there, lanes]
                    spacing = away - row_ref[
                        j, pair : pair + 1, (2 * k + i) * SPAN : (2 * k + i + 1) * SPAN
                    ]
                    weights = (jnp.exp2(jnp.minimum(spacing, 64.0)) * near).astype(BF16)
                    x_pair = xc[j, there, lanes]
                    stacked = jnp.concatenate(
                        [jnp.where(low, x_pair, none), jnp.where(low, none, x_pair)], axis=0
                    )
                    within = dot(weights, stacked) + x_pair.astype(F32) * fades[
                        total + 1 : total + 2, lanes
                    ]
                    half = (0.5 * z_buf[slot, there, lanes]).astype(F32)
                    gate = half * jnp.tanh(half) + half
                    entry = jnp.exp2(away)
                    if before is not None:
                        within = within + entry * before[:, lanes]
                    inside[there, lanes] = within * gate
                    outside[there, lanes] = entry * gate * so_far[:, lanes]

    @pl.when(me > 0)
    def _():
        each(join_at, join)

    each(close_at, close)

    @pl.when(s >= lead)
    def _():
        j = s - lead
        g = j // per
        own = pl.ds(pl.multiple_of(j * CHUNK, CHUNK), CHUNK)
        readout = dot(c_ref[g], came[j])
        y_ref[:, own] = (inside[...] + outside[...] * readout).astype(BF16)

    @pl.when(s == last_step)
    def _():
        @pl.when(me < n - 1)
        def _():
            for copy in edge_copies():
                copy.wait_send()
            for c in range(chunks):
                for p in range(PARTS):
                    onward(c, p).wait_send()

        @pl.when(me > 0)
        def _():
            for c in range(chunks):
                lax.fori_loop(0, me, lambda q, z: (behind(q, c).wait_send(), z)[1], 0)
                fading(c).wait_send()


def scan(n, x, taps, bias, bc, taps_bc, bias_bc, dt, dt_bias, a_log, skip, z, groups):
    rows, channels = x.shape
    chunks = channels // CHUNK
    heads = dt.shape[0]
    lead = leading(n, chunks)
    lines = bc.shape[0] // rows
    fade_rows = -(-(4 * (rows // SPAN) + 2) // 8) * 8
    share = STATE // n
    spans = rows // SPAN
    return pl.pallas_call(
        functools.partial(scan_kernel, n),
        grid=(lead + chunks,),
        in_specs=[pl.BlockSpec(memory_space=pl.ANY)] * 11,
        out_specs=[
            pl.BlockSpec(memory_space=pltpu.VMEM),
            pl.BlockSpec(memory_space=pltpu.VMEM),
        ],
        out_shape=[
            pltpu.VMEM((rows, channels), BF16),
            pltpu.VMEM((share, channels), BF16),
        ],
        scratch_shapes=[
            pltpu.VMEM((chunks, rows, CHUNK), BF16),
            pltpu.VMEM((chunks, STATE, CHUNK), BF16),
            pltpu.VMEM((chunks, STATE, CHUNK), BF16),
            pltpu.VMEM((chunks, STATE, CHUNK), BF16),
            pltpu.VMEM((chunks, STATE - share, CHUNK), BF16),
            pltpu.VMEM((chunks, STATE - share, CHUNK), BF16),
            pltpu.VMEM((chunks, 8, CHUNK), F32),
            pltpu.VMEM((chunks, 8, CHUNK), F32),
            pltpu.VMEM((chunks, max(spans // 2 - 1, 1), STATE, CHUNK), BF16),
            pltpu.VMEM((rows, heads), F32),
            pltpu.VMEM((rows, heads), F32),
            pltpu.VMEM((rows, 3 * heads), BF16),
            pltpu.VMEM((chunks, HEADS_CHUNK // 2, 2 * rows), F32),
            pltpu.VMEM((heads, SPAN), F32),
            pltpu.VMEM((rows, 2 * heads), BF16),
            pltpu.VMEM((fade_rows, heads), F32),
            pltpu.VMEM((groups, STATE, rows), BF16),
            pltpu.VMEM((groups, rows, STATE), BF16),
            pltpu.VMEM((groups, rows, SPAN), F32),
            pltpu.VMEM((groups, rows // 2, HALF), BF16),
            pltpu.VMEM((chunks, spans, HALF, CHUNK), BF16),
            pltpu.VMEM((chunks, spans // 2, SPAN, CHUNK), BF16),
            pltpu.VMEM((groups, rows // 2, SPAN), BF16),
            pltpu.VMEM((rows, CHUNK), F32),
            pltpu.VMEM((rows, CHUNK), F32),
            pltpu.VMEM(((EDGE_TOKENS + rows) * lines, 128), F32),
            pltpu.VMEM((CHUNK // 128, HALO + rows, 128), F32),
            pltpu.VMEM((chunks, 3 * heads, CHUNK), BF16),
            pltpu.VMEM((chunks, fade_rows, CHUNK), F32),
            pltpu.VMEM((2, rows, CHUNK), BF16),
            pltpu.VMEM((2, rows, CHUNK), BF16),
            pltpu.VMEM(taps.shape, BF16),
            pltpu.VMEM(bias.shape, F32),
            pltpu.VMEM(bc.shape, BF16),
            pltpu.VMEM(taps_bc.shape, BF16),
            pltpu.VMEM(bias_bc.shape, F32),
            pltpu.VMEM(dt.shape, F32),
            pltpu.VMEM(dt_bias.shape, F32),
            pltpu.VMEM(a_log.shape, F32),
            pltpu.VMEM(skip.shape, F32),
            pltpu.VMEM((EDGE, channels), BF16),
            pltpu.VMEM((EDGE_TOKENS * lines, 128), BF16),
            pltpu.SemaphoreType.DMA((2,)),
            pltpu.SemaphoreType.DMA((2,)),
            pltpu.SemaphoreType.DMA((9,)),
            pltpu.SemaphoreType.DMA((PARTS, chunks)),
            pltpu.SemaphoreType.DMA((PARTS, chunks)),
            pltpu.SemaphoreType.DMA((n - 1, chunks)),
            pltpu.SemaphoreType.DMA((n - 1, chunks)),
            pltpu.SemaphoreType.DMA((chunks,)),
            pltpu.SemaphoreType.DMA((chunks,)),
            pltpu.SemaphoreType.DMA((3,)),
            pltpu.SemaphoreType.DMA((3,)),
        ],
        compiler_params=pltpu.CompilerParams(
            dimension_semantics=("arbitrary",),
            vmem_limit_bytes=56 << 20,
            collective_id=0,
            has_side_effects=True,
        ),
        cost_estimate=pl.CostEstimate(
            flops=20 * rows * channels * STATE, bytes_accessed=4 * rows * channels, transcendentals=4 * rows * channels
        ),
    )(x, taps, bias, bc, taps_bc, bias_bc, dt, dt_bias, a_log, skip, z)


def per_device(
    x_in,
    bc_in,
    z_in,
    dt_raw,
    conv_x,
    conv_bc,
    conv_bias_x,
    conv_bias_bc,
    dt_bias,
    a_log,
    d_skip,
    norm_gain,
):
    rows, channels = x_in.shape
    heads = dt_raw.shape[1]
    n = lax.axis_size("ctx")
    tiles = bc_in.shape[2] // 128
    groups = bc_in.shape[2] // STATE

    def lined(v):
        return v.reshape(-1, 2, tiles, 128).transpose(0, 2, 1, 3).reshape(-1, 128)

    gated, final = scan(
        n,
        x_in,
        conv_x.reshape(-1, channels // 128, 128).transpose(1, 0, 2).reshape(-1, 128),
        conv_bias_x[None],
        lined(bc_in),
        lined(conv_bc),
        lined(conv_bias_bc),
        dt_raw.T,
        dt_bias[None],
        a_log[None],
        d_skip[None],
        z_in,
        groups,
    )
    return tuple(finish(gated, norm_gain[None], final, groups))


def solution(mesh):
    in_specs = (
        P(("group", "ctx"), "tp"),
        P(("group", "ctx"), None, "tp"),
        P(("group", "ctx"), "tp"),
        P(("group", "ctx"), "tp"),
        P(None, "tp"),
        P(None, None, "tp"),
        P("tp"),
        P(None, "tp"),
        P("tp"),
        P("tp"),
        P("tp"),
        P("tp"),
    )
    out_specs = (P(("group", "ctx"), "tp"), P(("group", "tp"), None, "ctx"))
    return jax.shard_map(
        per_device, mesh=mesh, in_specs=in_specs, out_specs=out_specs, check_vma=False
    )
```

```python
import functools
import math

import jax
import jax.numpy as jnp
from jax import lax
from jax.experimental import pallas as pl
from jax.experimental.pallas import tpu as pltpu
from jax.sharding import PartitionSpec as P

HEAD_DIM = 64
STATE = 256
SPAN = 128
HALF = SPAN // 2
CHUNK = 512
HEADS_CHUNK = CHUNK // HEAD_DIM
HALO = 8
LOG2E = math.log2(math.e)

eps = 1e-05
F32 = jnp.float32
BF16 = jnp.bfloat16


def dot(a, b):
    return jnp.dot(a, b, preferred_element_type=F32)


def rescaled(gated, gain):
    gated = gated.astype(F32)
    meansq = jnp.mean(gated * gated, axis=-1, keepdims=True)
    return (gated * lax.rsqrt(meansq + eps) * gain).astype(BF16)


def finish_kernel(groups, gated_ref, gain_ref, final_ref, out_any, state_any, mixed, turned, sems):
    rows, channels = gated_ref.shape
    width = channels // groups
    blocks = rows // SPAN
    part = CHUNK // HEAD_DIM
    for c in range(channels // CHUNK):
        block = final_ref[:, c * CHUNK : (c + 1) * CHUNK].astype(F32).T
        turned[c * part : (c + 1) * part] = block.reshape(part, HEAD_DIM, block.shape[1])
    copies = [pltpu.make_async_copy(turned, state_any, sems.at[blocks])]
    copies[-1].start()
    for b in range(blocks):
        at = slice(b * SPAN, (b + 1) * SPAN)
        for g in range(groups):
            own = slice(g * width, (g + 1) * width)
            mixed[at, own] = rescaled(gated_ref[at, own], gain_ref[:, own])
        there = pl.ds(b * SPAN, SPAN)
        copies.append(pltpu.make_async_copy(mixed.at[there], out_any.at[there], sems.at[b]))
        copies[-1].start()
    for copy in copies:
        copy.wait()


def finish(gated, gain, final, groups):
    rows, channels = gated.shape
    share = final.shape[0]
    heads = channels // HEAD_DIM
    whole = pl.BlockSpec(memory_space=pltpu.VMEM)
    away = pl.BlockSpec(memory_space=pl.ANY)
    return pl.pallas_call(
        functools.partial(finish_kernel, groups),
        in_specs=[whole, whole, whole],
        out_specs=[away, away],
        out_shape=[
            jax.ShapeDtypeStruct((rows, channels), BF16),
            jax.ShapeDtypeStruct((heads, HEAD_DIM, share), F32),
        ],
        scratch_shapes=[
            pltpu.VMEM((rows, channels), BF16),
            pltpu.VMEM((heads, HEAD_DIM, share), F32),
            pltpu.SemaphoreType.DMA((1 + rows // SPAN,)),
        ],
        compiler_params=pltpu.CompilerParams(vmem_limit_bytes=16 << 20),
        cost_estimate=pl.CostEstimate(
            flops=4 * rows * channels, bytes_accessed=4 * rows * channels, transcendentals=rows
        ),
    )(gated, gain, final)


EDGE = 16
EDGE_TOKENS = 4
PARTS = 2
MESH = pl.DeviceIdType.MESH


def leading(n, chunks):
    return chunks + max(0, n - 4)


def pieces(v, parts):
    out = []
    for _ in range(parts):
        out.append(v.astype(BF16))
        v = v - out[-1].astype(F32)
    return out


def split(v, parts):
    return jnp.concatenate([piece.astype(F32) for piece in pieces(v, parts)], axis=1).astype(BF16)


def scan_kernel(
    n,
    x_any,
    taps_any,
    bias_any,
    bc_any,
    taps_bc_any,
    bias_bc_any,
    dt_any,
    dt_bias_any,
    a_log_any,
    skip_any,
    z_any,
    y_ref,
    final_out,
    xc,
    sent,
    merged,
    came,
    later_out,
    later_in,
    fade_out,
    fade_in,
    local,
    exact_ref,
    step_ref,
    cumul_ref,
    row_ref,
    turn_ref,
    tail_ref,
    fade_ref,
    bt_ref,
    c_ref,
    near_ref,
    far_ref,
    kept,
    even,
    mid_ref,
    inside,
    outside,
    raw_ref,
    lift_ref,
    spread_ref,
    wide_ref,
    z_buf,
    x_buf,
    taps_ref,
    bias_ref,
    bc_ref,
    taps_bc_ref,
    bias_bc_ref,
    dt_ref,
    dt_bias_ref,
    a_log_ref,
    skip_ref,
    edge_x,
    edge_bc,
    z_sem,
    x_sem,
    in_sem,
    send_sem,
    recv_sem,
    later_send,
    later_recv,
    fade_send,
    fade_recv,
    edge_send,
    edge_recv,
):
    s = pl.program_id(0)
    chunks = sent.shape[0]
    lead = leading(n, chunks)
    last_step = lead + chunks - 1
    me = lax.axis_index("ctx")
    rows = x_any.shape[0]
    spans = rows // SPAN
    heads = dt_ref.shape[0]
    groups = bt_ref.shape[0]
    per = chunks // groups
    lines = bc_ref.shape[0] // rows
    reach = EDGE_TOKENS * lines
    share = STATE // n
    right = jnp.minimum(me + 1, n - 1)
    left = jnp.maximum(me - 1, 0)
    total = 2 * spans

    def edge_copies():
        ends = [(bc_any, edge_bc, 0, 128), (x_any, edge_x, 0, CHUNK)]
        if chunks > 1:
            ends.append((x_any, edge_x, CHUNK, (chunks - 1) * CHUNK))
        return [
            pltpu.make_async_remote_copy(
                src_ref=whole.at[
                    pl.ds(whole.shape[0] - edge.shape[0], edge.shape[0]), pl.ds(at, size)
                ],
                dst_ref=edge.at[:, pl.ds(at, size)],
                send_sem=edge_send.at[i],
                recv_sem=edge_recv.at[i],
                device_id={"ctx": right},
                device_id_type=MESH,
            )
            for i, (whole, edge, at, size) in enumerate(ends)
        ]

    piece = STATE // PARTS

    def onward(c, p):
        return pltpu.make_async_remote_copy(
            src_ref=merged.at[c, pl.ds(p * piece, piece)],
            dst_ref=came.at[c, pl.ds(p * piece, piece)],
            send_sem=send_sem.at[p, c],
            recv_sem=recv_sem.at[p, c],
            device_id={"ctx": right},
            device_id_type=MESH,
        )

    def load(c):
        return pltpu.make_async_copy(
            x_any.at[:, pl.ds(pl.multiple_of(c * CHUNK, CHUNK), CHUNK)],
            x_buf.at[lax.rem(c, 2)],
            x_sem.at[lax.rem(c, 2)],
        )

    early = [
        pltpu.make_async_copy(src, dst, in_sem.at[i])
        for i, (src, dst) in enumerate(
            (
                (dt_any, dt_ref),
                (dt_bias_any, dt_bias_ref),
                (a_log_any, a_log_ref),
                (skip_any, skip_ref),
                (bc_any, bc_ref),
                (taps_bc_any, taps_bc_ref),
                (bias_bc_any, bias_bc_ref),
                (taps_any, taps_ref),
                (bias_any, bias_ref),
            )
        )
    ]

    def fetch(c):
        return pltpu.make_async_copy(
            z_any.at[:, pl.ds(pl.multiple_of(c * CHUNK, CHUNK), CHUNK)],
            z_buf.at[lax.rem(c, 2)],
            z_sem.at[lax.rem(c, 2)],
        )

    def rows_of(q):
        return pl.ds(pl.multiple_of(q * share, share), share)

    def behind(q, c):
        return pltpu.make_async_remote_copy(
            src_ref=later_out.at[c, rows_of(q)],
            dst_ref=later_in.at[c, rows_of(q)],
            send_sem=later_send.at[q, c],
            recv_sem=later_recv.at[q, c],
            device_id={"ctx": left},
            device_id_type=MESH,
        )

    def fading(c):
        return pltpu.make_async_remote_copy(
            src_ref=fade_out.at[c],
            dst_ref=fade_in.at[c],
            send_sem=fade_send.at[c],
            recv_sem=fade_recv.at[c],
            device_id={"ctx": left},
            device_id_type=MESH,
        )

    def spread_of(c):
        shape = (3 * heads, CHUNK)
        return (
            lax.broadcasted_iota(jnp.int32, shape, 1) // HEAD_DIM + c * HEADS_CHUNK
            == lax.broadcasted_iota(jnp.int32, shape, 0) % heads
        ).astype(BF16)

    def project(side, g, over):
        taps = 0.5 * taps_bc_ref[...].astype(F32)
        bias = 0.5 * bias_bc_ref[...]
        lag = taps.shape[0] // lines - 1
        for k in over:
            at = slice(k * SPAN, (k + 1) * SPAN)
            for i in range(STATE // 128):
                line = 2 * (g * (STATE // 128) + i) + side
                own = slice(i * 128, (i + 1) * 128)
                half = bias[line : line + 1]
                for q in range(lag + 1):
                    begin = (k * SPAN + EDGE_TOKENS - lag + q) * lines + line
                    tap = taps[q * lines + line : q * lines + line + 1]
                    half = half + raw_ref[pl.ds(begin, SPAN, stride=lines), :] * tap
                v = half * jnp.tanh(half) + half
                if side == 0:
                    bt_ref[g, own, at] = v.astype(BF16).astype(F32).T.astype(BF16)
                else:
                    c_ref[g, at, own] = v.astype(BF16)

    @pl.when(s == 0)
    def _():
        barrier = pltpu.get_barrier_semaphore()

        @pl.when(me > 0)
        def _():
            pl.semaphore_signal(barrier, inc=1, device_id={"ctx": left}, device_id_type=MESH)

        @pl.when(me < n - 1)
        def _():
            pl.semaphore_signal(barrier, inc=1, device_id={"ctx": right}, device_id_type=MESH)

        for copy in early:
            copy.start()
        load(0).start()
        for copy in early[:4]:
            copy.wait()
        rate = -LOG2E * jnp.exp(a_log_ref[...])
        above = lax.broadcasted_iota(jnp.int32, (SPAN, SPAN), 0)
        across = lax.broadcasted_iota(jnp.int32, (SPAN, SPAN), 1)
        lower = ((above >= across) & (above // HALF == across // HALF)).astype(BF16)
        lower = jnp.concatenate([lower] * 3, axis=1)
        so_far = jnp.zeros((1, heads), F32)
        fade_ref[...] = jnp.zeros_like(fade_ref)
        ats = [slice(k * SPAN, (k + 1) * SPAN) for k in range(spans)]
        raws = [dt_ref[:, at].T + dt_bias_ref[...] for at in ats]
        steps = [jnp.maximum(v, 0.0) + jnp.log1p(jnp.exp(-jnp.abs(v))) for v in raws]
        cumuls = [dot(lower, jnp.concatenate(pieces(step * rate, 3), axis=0)) for step in steps]
        for k, at in enumerate(ats):
            cumul = cumuls[k]
            step = steps[k]
            ends = cumul[HALF - 1 : HALF], cumul[SPAN - 1 :]
            tail = jnp.concatenate(
                [end - cumul[i * HALF : (i + 1) * HALF] for i, end in enumerate(ends)], axis=0
            )
            exact_ref[at] = cumul
            step_ref[at] = step
            tail_ref[at] = split(jnp.exp2(tail) * step, 2)
            for i in range(2):
                part = 2 * k + i
                fade_ref[part : part + 1] = jnp.exp2(ends[i])
                fade_ref[total + 2 + part : total + 3 + part] = jnp.exp2(so_far)
                so_far = so_far + ends[i]
        fade_ref[2 * spans : 2 * spans + 1] = jnp.exp2(so_far)
        fade_ref[2 * spans + 1 : 2 * spans + 2] = skip_ref[...]
        pl.semaphore_wait(barrier, jnp.where((me == 0) | (me == n - 1), 1, 2))

        @pl.when(me < n - 1)
        def _():
            for copy in edge_copies():
                copy.start()

        for copy in early[4:]:
            copy.wait()
        raw_ref[reach:] = bc_ref[...].astype(F32)
        project(0, 0, range(1, spans))

        @pl.when(me == 0)
        def _():
            edge_x[...] = jnp.zeros_like(edge_x)
            edge_bc[...] = jnp.zeros_like(edge_bc)

        @pl.when(me > 0)
        def _():
            for copy in edge_copies()[:2]:
                copy.wait_recv()

        raw_ref[:reach] = edge_bc[...].astype(F32)
        project(0, 0, range(1))

    def join(c, carry):
        fade = wide_ref[c, total : total + 1]
        for p in range(PARTS):
            own = slice(p * piece, (p + 1) * piece)
            onward(c, p).wait_recv()
            got = came[c, own].astype(F32)
            merged[c, own] = (fade * got + sent[c, own].astype(F32)).astype(BF16)

            @pl.when(me < n - 1)
            def _(p=p):
                onward(c, p).start()

        return carry

    def turn_back(c, carry):
        lax.fori_loop(0, me + 1, lambda q, z: (behind(q, c).wait_recv(), z)[1], 0)
        fading(c).wait_recv()

        def add(q, z):
            mine = sent[c, rows_of(q)].astype(F32)
            after = later_in[c, rows_of(q)].astype(F32)
            later_out[c, rows_of(q)] = (fade_in[c, :1] * mine + after).astype(BF16)
            behind(q, c).start()
            return z

        lax.fori_loop(0, me, add, 0)

        @pl.when(me > 0)
        def _():
            fade_out[c] = fade_in[c] * wide_ref[c, total : total + 1]
            fading(c).start()

        return carry

    def close(c, carry):
        there = pl.ds(pl.multiple_of(c * CHUNK, CHUNK), CHUNK)

        @pl.when(me < n - 1)
        def _():
            mine = merged[c, rows_of(me)].astype(F32)
            after = later_in[c, rows_of(jnp.minimum(me, n - 2))].astype(F32)
            final_out[:, there] = (fade_in[c, :1] * mine + after).astype(BF16)

        @pl.when(me == n - 1)
        def _():
            final_out[:, there] = merged[c, STATE - share :]

        return carry

    def each(first, work):
        start = jnp.clip(s - first, 0, chunks)
        stop = jnp.where(s == last_step, chunks, jnp.clip(s - first + 1, 0, chunks))
        lax.fori_loop(start, stop, work, 0)

    join_at = jnp.where(me == 1, 0, jnp.minimum(lead, chunks + me - 2))
    back_at = 2 + 6 * jnp.maximum(n - 2 - me, 0)
    close_at = jnp.maximum(jnp.where(me == 0, 0, join_at), jnp.where(me < n - 1, back_at, 0))

    @pl.when(me < n - 1)
    def _():
        each(back_at, turn_back)

    pairs = HEADS_CHUNK // 2

    def pair_lanes(pair):
        return slice(pair * 2 * HEAD_DIM, (pair + 1) * 2 * HEAD_DIM)

    if chunks > 1:

        @pl.when((s == 1) & (me > 0))
        def _():
            edge_copies()[2].wait_recv()

    @pl.when(s < chunks)
    def _():
        j = s
        bt = bt_ref.at[j // per]
        load(j).wait()

        @pl.when(s < chunks - 1)
        def _():
            load(j + 1).start()

        count = taps_ref.shape[0] // (chunks * CHUNK // 128)
        block = count * CHUNK // 128
        taps = 0.5 * taps_ref[pl.ds(pl.multiple_of(j * block, block), block)].astype(F32)
        bias = 0.5 * bias_ref[:, pl.ds(pl.multiple_of(j * CHUNK, CHUNK), CHUNK)]
        lag = count - 1
        turn = lax.rem(j, 2)
        before = edge_x[:, pl.ds(pl.multiple_of(j * CHUNK, CHUNK), CHUNK)].astype(F32)[EDGE - HALO :]
        spread = spread_of(j)
        spread_ref[j] = spread
        fades = dot(split(fade_ref[...], 3), spread)
        wide_ref[j] = fades
        tiles = [slice(i * 128, (i + 1) * 128) for i in range(CHUNK // 128)]
        for i, lanes in enumerate(tiles):
            lift_ref[i, :HALO] = before[:, lanes]
            lift_ref[i, HALO:] = x_buf[turn, :, lanes].astype(F32)
        inside[...] = dot(tail_ref[...], spread[: 2 * heads])
        state = None
        for k in range(spans):
            at = slice(k * SPAN, (k + 1) * SPAN)
            parts = []
            for i, lanes in enumerate(tiles):
                column = []
                for r in range(0, SPAN, HALF):
                    first = k * SPAN + r
                    half = bias[:, lanes]
                    for q in range(lag + 1):
                        begin = HALO - lag + q + first
                        half = half + lift_ref[i, begin : begin + HALF] * taps[i * count + q : i * count + q + 1]
                    value = half * jnp.tanh(half) + half
                    xc[j, first : first + HALF, lanes] = value.astype(BF16)
                    column.append(value * inside[first : first + HALF, lanes])
                parts.append(column)
            scaled = jnp.concatenate([column[1] for column in parts], axis=1).astype(BF16)
            first = jnp.concatenate([column[0] for column in parts], axis=1)
            kept[j, k] = first.astype(BF16)
            first = (first * fades[2 * k + 1 : 2 * k + 2]).astype(BF16)
            scaled = jnp.concatenate([first, scaled], axis=0)
            if k % 2 == 0:
                even[j, k // 2] = scaled
                row = jnp.broadcast_to(
                    fades[2 * k + 2 : 2 * k + 3] * fades[2 * k + 3 : 2 * k + 4], (16, CHUNK)
                ).astype(BF16)[None]
                held = (scaled.reshape(SPAN // 16, 16, CHUNK) * row).reshape(SPAN, CHUNK)
                continue
            scaled = jnp.concatenate([held, scaled], axis=0)
            at = slice((k - 1) * SPAN, (k + 1) * SPAN)
            part = dot(bt[:, at], scaled)
            if state is not None:
                local[j, k // 2 - 1] = state.astype(BF16)
                row = fades[2 * k - 2 : 2 * k - 1]
                for i in range(1, 4):
                    row = row * fades[2 * k - 2 + i : 2 * k - 1 + i]
                part = row * state + part
            state = part
        state = state.astype(BF16)
        sent[j] = state

        @pl.when(me == 0)
        def _():
            merged[j] = state
            for p in range(PARTS):
                onward(j, p).start()

        @pl.when(me == n - 1)
        def _():
            later_out[j] = state[: STATE - share]
            fade_out[j] = jnp.broadcast_to(fades[total : total + 1], (8, CHUNK))
            lax.fori_loop(0, n - 1, lambda q, z: (behind(q, j).start(), z)[1], 0)
            fading(j).start()

    @pl.when(s == 2)
    def _():
        for g in range(1, groups):
            project(0, g, range(spans))
        project(1, 0, range(spans))

    @pl.when(s == 3)
    def _():
        fetch(0).start()
        for g in range(1, groups):
            project(1, g, range(spans))
        causal = lax.broadcasted_iota(jnp.int32, (HALF, SPAN), 0) >= (
            lax.broadcasted_iota(jnp.int32, (HALF, SPAN), 1) % HALF
        )
        for g in range(groups):
            for k in range(spans):
                at = slice(k * SPAN, (k + 1) * SPAN)
                scores = dot(c_ref[g, at], bt_ref[g, :, at])
                if k % 2:
                    prior = bt_ref[g, :, (k - 1) * SPAN : k * SPAN]
                    mid_ref[g, (k // 2) * SPAN : (k // 2 + 1) * SPAN] = dot(
                        c_ref[g, at], prior
                    ).astype(BF16)
                for i in range(2):
                    own = slice(i * HALF, (i + 1) * HALF)
                    near = jnp.concatenate([scores[own, own]] * 2, axis=1)
                    near_ref[g, k * SPAN + i * HALF : k * SPAN + (i + 1) * HALF] = jnp.where(
                        causal, near, 0.0
                    )
                far_ref[g, k * HALF : (k + 1) * HALF] = scores[HALF:, :HALF].astype(BF16)
        for k in range(spans):
            at = slice(k * SPAN, (k + 1) * SPAN)
            cumul_ref[at] = split(exact_ref[at], 3)
            rowed = exact_ref[at] - jnp.log2(step_ref[at])
            wide = jnp.concatenate([rowed] * (128 // heads), axis=1) if heads < 128 else rowed
            turn_ref[...] = wide.T[:heads]
            first = turn_ref[pl.ds(0, heads // 2, stride=2), :]
            second = turn_ref[pl.ds(1, heads // 2, stride=2), :]
            for i in range(2):
                own = slice(i * HALF, (i + 1) * HALF)
                pairs_row = jnp.concatenate([first[:, own], second[:, own]], axis=1)
                for c in range(chunks):
                    row_ref[c, :, (2 * k + i) * SPAN : (2 * k + i + 1) * SPAN] = pairs_row[
                        c * (HEADS_CHUNK // 2) : (c + 1) * (HEADS_CHUNK // 2)
                    ]

        @pl.when(me == 0)
        def _():
            came[...] = jnp.zeros_like(came)

    @pl.when(s >= lead)
    def _():
        j = s - lead
        fetch(j).wait()

        @pl.when(s < last_step)
        def _():
            fetch(j + 1).start()

        slot = lax.rem(j, 2)
        fades = wide_ref[j]
        spread = spread_ref[j]
        g = j // per
        none = jnp.zeros((), BF16)
        low = lax.broadcasted_iota(jnp.int32, (HALF, 2 * HEAD_DIM), 1) < HEAD_DIM

        outside[...] = dot(cumul_ref[...], spread)
        for k in range(spans):
            at = slice(k * SPAN, (k + 1) * SPAN)
            carried = None
            if k > 1:
                if k % 2 == 0:
                    both = slice(k * SPAN, (k + 2) * SPAN)
                    inside[both] = dot(c_ref[g, both], local[j, k // 2 - 1])
                carried = inside[at]
            if k % 2:
                prior = dot(mid_ref[g, (k // 2) * SPAN : (k // 2 + 1) * SPAN], even[j, k // 2])
                if carried is not None:
                    prior = prior + carried * (
                        fades[2 * k - 2 : 2 * k - 1] * fades[2 * k - 1 : 2 * k]
                    )
                carried = prior
            beside = dot(far_ref[g, k * HALF : (k + 1) * HALF], kept[j, k])
            for i in range(2):
                mine = slice(i * HALF, (i + 1) * HALF)
                there = slice(k * SPAN + i * HALF, k * SPAN + (i + 1) * HALF)
                near = near_ref[g, there]
                before = None if carried is None else carried[mine]
                if i == 1:
                    before = beside if before is None else beside + before * fades[2 * k : 2 * k + 1]
                so_far = fades[total + 2 + 2 * k + i : total + 3 + 2 * k + i]
                for pair in range(pairs):
                    lanes = pair_lanes(pair)
                    away = outside[there, lanes]
                    spacing = away - row_ref[
                        j, pair : pair + 1, (2 * k + i) * SPAN : (2 * k + i + 1) * SPAN
                    ]
                    weights = (jnp.exp2(jnp.minimum(spacing, 64.0)) * near).astype(BF16)
                    x_pair = xc[j, there, lanes]
                    stacked = jnp.concatenate(
                        [jnp.where(low, x_pair, none), jnp.where(low, none, x_pair)], axis=0
                    )
                    within = dot(weights, stacked) + x_pair.astype(F32) * fades[
                        total + 1 : total + 2, lanes
                    ]
                    half = (0.5 * z_buf[slot, there, lanes]).astype(F32)
                    gate = half * jnp.tanh(half) + half
                    entry = jnp.exp2(away)
                    if before is not None:
                        within = within + entry * before[:, lanes]
                    inside[there, lanes] = within * gate
                    outside[there, lanes] = entry * gate * so_far[:, lanes]

    @pl.when(me > 0)
    def _():
        each(join_at, join)

    @pl.when(s >= lead)
    def _():
        j = s - lead
        g = j // per
        own = pl.ds(pl.multiple_of(j * CHUNK, CHUNK), CHUNK)
        readout = dot(c_ref[g], came[j])
        y_ref[:, own] = (inside[...] + outside[...] * readout).astype(BF16)

    each(close_at, close)

    @pl.when(s == last_step)
    def _():
        @pl.when(me < n - 1)
        def _():
            for copy in edge_copies():
                copy.wait_send()
            for c in range(chunks):
                for p in range(PARTS):
                    onward(c, p).wait_send()

        @pl.when(me > 0)
        def _():
            for c in range(chunks):
                lax.fori_loop(0, me, lambda q, z: (behind(q, c).wait_send(), z)[1], 0)
                fading(c).wait_send()


def scan(n, x, taps, bias, bc, taps_bc, bias_bc, dt, dt_bias, a_log, skip, z, groups):
    rows, channels = x.shape
    chunks = channels // CHUNK
    heads = dt.shape[0]
    lead = leading(n, chunks)
    lines = bc.shape[0] // rows
    fade_rows = -(-(4 * (rows // SPAN) + 2) // 8) * 8
    share = STATE // n
    spans = rows // SPAN
    return pl.pallas_call(
        functools.partial(scan_kernel, n),
        grid=(lead + chunks,),
        in_specs=[pl.BlockSpec(memory_space=pl.ANY)] * 11,
        out_specs=[
            pl.BlockSpec(memory_space=pltpu.VMEM),
            pl.BlockSpec(memory_space=pltpu.VMEM),
        ],
        out_shape=[
            pltpu.VMEM((rows, channels), BF16),
            pltpu.VMEM((share, channels), BF16),
        ],
        scratch_shapes=[
            pltpu.VMEM((chunks, rows, CHUNK), BF16),
            pltpu.VMEM((chunks, STATE, CHUNK), BF16),
            pltpu.VMEM((chunks, STATE, CHUNK), BF16),
            pltpu.VMEM((chunks, STATE, CHUNK), BF16),
            pltpu.VMEM((chunks, STATE - share, CHUNK), BF16),
            pltpu.VMEM((chunks, STATE - share, CHUNK), BF16),
            pltpu.VMEM((chunks, 8, CHUNK), F32),
            pltpu.VMEM((chunks, 8, CHUNK), F32),
            pltpu.VMEM((chunks, max(spans // 2 - 1, 1), STATE, CHUNK), BF16),
            pltpu.VMEM((rows, heads), F32),
            pltpu.VMEM((rows, heads), F32),
            pltpu.VMEM((rows, 3 * heads), BF16),
            pltpu.VMEM((chunks, HEADS_CHUNK // 2, 2 * rows), F32),
            pltpu.VMEM((heads, SPAN), F32),
            pltpu.VMEM((rows, 2 * heads), BF16),
            pltpu.VMEM((fade_rows, heads), F32),
            pltpu.VMEM((groups, STATE, rows), BF16),
            pltpu.VMEM((groups, rows, STATE), BF16),
            pltpu.VMEM((groups, rows, SPAN), F32),
            pltpu.VMEM((groups, rows // 2, HALF), BF16),
            pltpu.VMEM((chunks, spans, HALF, CHUNK), BF16),
            pltpu.VMEM((chunks, spans // 2, SPAN, CHUNK), BF16),
            pltpu.VMEM((groups, rows // 2, SPAN), BF16),
            pltpu.VMEM((rows, CHUNK), F32),
            pltpu.VMEM((rows, CHUNK), F32),
            pltpu.VMEM(((EDGE_TOKENS + rows) * lines, 128), F32),
            pltpu.VMEM((CHUNK // 128, HALO + rows, 128), F32),
            pltpu.VMEM((chunks, 3 * heads, CHUNK), BF16),
            pltpu.VMEM((chunks, fade_rows, CHUNK), F32),
            pltpu.VMEM((2, rows, CHUNK), BF16),
            pltpu.VMEM((2, rows, CHUNK), BF16),
            pltpu.VMEM(taps.shape, BF16),
            pltpu.VMEM(bias.shape, F32),
            pltpu.VMEM(bc.shape, BF16),
            pltpu.VMEM(taps_bc.shape, BF16),
            pltpu.VMEM(bias_bc.shape, F32),
            pltpu.VMEM(dt.shape, F32),
            pltpu.VMEM(dt_bias.shape, F32),
            pltpu.VMEM(a_log.shape, F32),
            pltpu.VMEM(skip.shape, F32),
            pltpu.VMEM((EDGE, channels), BF16),
            pltpu.VMEM((EDGE_TOKENS * lines, 128), BF16),
            pltpu.SemaphoreType.DMA((2,)),
            pltpu.SemaphoreType.DMA((2,)),
            pltpu.SemaphoreType.DMA((9,)),
            pltpu.SemaphoreType.DMA((PARTS, chunks)),
            pltpu.SemaphoreType.DMA((PARTS, chunks)),
            pltpu.SemaphoreType.DMA((n - 1, chunks)),
            pltpu.SemaphoreType.DMA((n - 1, chunks)),
            pltpu.SemaphoreType.DMA((chunks,)),
            pltpu.SemaphoreType.DMA((chunks,)),
            pltpu.SemaphoreType.DMA((3,)),
            pltpu.SemaphoreType.DMA((3,)),
        ],
        compiler_params=pltpu.CompilerParams(
            dimension_semantics=("arbitrary",),
            vmem_limit_bytes=56 << 20,
            collective_id=0,
            has_side_effects=True,
        ),
        cost_estimate=pl.CostEstimate(
            flops=20 * rows * channels * STATE, bytes_accessed=4 * rows * channels, transcendentals=4 * rows * channels
        ),
    )(x, taps, bias, bc, taps_bc, bias_bc, dt, dt_bias, a_log, skip, z)


def per_device(
    x_in,
    bc_in,
    z_in,
    dt_raw,
    conv_x,
    conv_bc,
    conv_bias_x,
    conv_bias_bc,
    dt_bias,
    a_log,
    d_skip,
    norm_gain,
):
    rows, channels = x_in.shape
    heads = dt_raw.shape[1]
    n = lax.axis_size("ctx")
    tiles = bc_in.shape[2] // 128
    groups = bc_in.shape[2] // STATE

    def lined(v):
        return v.reshape(-1, 2, tiles, 128).transpose(0, 2, 1, 3).reshape(-1, 128)

    gated, final = scan(
        n,
        x_in,
        conv_x.reshape(-1, channels // 128, 128).transpose(1, 0, 2).reshape(-1, 128),
        conv_bias_x[None],
        lined(bc_in),
        lined(conv_bc),
        lined(conv_bias_bc),
        dt_raw.T,
        dt_bias[None],
        a_log[None],
        d_skip[None],
        z_in,
        groups,
    )
    return tuple(finish(gated, norm_gain[None], final, groups))


def solution(mesh):
    in_specs = (
        P(("group", "ctx"), "tp"),
        P(("group", "ctx"), None, "tp"),
        P(("group", "ctx"), "tp"),
        P(("group", "ctx"), "tp"),
        P(None, "tp"),
        P(None, None, "tp"),
        P("tp"),
        P(None, "tp"),
        P("tp"),
        P("tp"),
        P("tp"),
        P("tp"),
    )
    out_specs = (P(("group", "ctx"), "tp"), P(("group", "tp"), None, "ctx"))
    return jax.shard_map(
        per_device, mesh=mesh, in_specs=in_specs, out_specs=out_specs, check_vma=False
    )
```
